32 devices in a mesh: dom: 8 (over z, x), orb: 4 (over y, core).
Axes of the slice: x: 2, y: 2, z: 4, core: 2. Of those that a mesh axis runs over, the one named last changes fastest.
Arguments:
- orbitals: float32 [16, 96, 64, 128], P('orb', 'dom'), may hold values from -400 to 400
- potential: float32 [96, 64, 128], P('dom'), may hold values from -8 to 8
Outputs:
- filtered_basis: float32 [16, 96, 64, 128], P('orb', 'dom')
The draws below stay inside these ranges and needn't reach their ends.
All inputs are finite; a program needn't handle non-finite values.
Results may differ from the reference program's by a relative error of at most 0.0003.
Values sent between devices are 32-bit elements; how exact they have to be, the bound alone decides.
No kernel may reach another device: no remote copies, remote signals or barrier semaphores. Data moves between devices by JAX's collectives and lax.ppermute only.
A program may use at most 64 MiB of HBM per device.

```python
import math
import jax
import jax.numpy as jnp
from jax import lax

ORBITALS = 16
NY = 64
NZ = 128
NX = 96


def draw_orbitals(key, part):
    key_base, key_noise, key_scale = jax.random.split(jax.random.fold_in(key, 7), 3)
    scales = jnp.exp(jax.random.uniform(key_scale, (ORBITALS, 1, 1, 1), jnp.float32, 0.0, math.log(10.0)))
    along_x = jnp.arange(NX, dtype=jnp.float32) / max(NX - 1, 1)
    along_y = jnp.arange(NY, dtype=jnp.float32) / max(NY - 1, 1)
    base = jnp.clip(jax.random.normal(key_base, (NX, NY, NZ), jnp.float32), -5.5, 5.5)
    noise = jnp.clip(jax.random.normal(key_noise, (ORBITALS, NX, NY, NZ), jnp.float32), -5.5, 5.5)
    share = 16.0
    envelope = jnp.sqrt((1.0 + 2.0 * along_x)[:, None, None] * (1.0 + 2.0 * along_y)[None, :, None])
    return (scales * envelope[None] * (base[None] + noise / share)).astype(jnp.float32)


def shard_levels(stream_key, shape, shards, smallest, high):
    gain, own = 1.0, jax.random.fold_in(stream_key, 6)
    for dim, blocks in shards:
        steps = jnp.exp(jax.random.uniform(jax.random.fold_in(own, dim), (blocks,), jnp.float32, smallest / len(shards), high / len(shards)))
        gain = gain * jnp.repeat(steps, shape[dim] // blocks).reshape([-1 if axis == dim else 1 for axis in range(len(shape))])
    return gain


def setup_inputs(seed: int = 0) -> dict:
    key_list = jax.random.split(jax.random.key(seed), 3)
    orbitals = draw_orbitals(jax.random.fold_in(key_list[2], 71), 0)
    potential = jnp.clip(jax.random.uniform(key_list[1], (NX, NY, NZ), jnp.float32, -8.0, 8.0) * shard_levels(key_list[1], (NX, NY, NZ), ((0, 8),), -0.4, 0.0), -8.0, 8.0)
    return dict(orbitals=orbitals, potential=potential)


coefficients = (-49.0 / 18.0, 1.5, -0.15, 1.0 / 90.0)
spacing = 0.5
filter_centre = 23.0
filter_half = 23.0

def hamiltonian(field, potential):
    laplace = 3.0 * coefficients[0] * field
    for offset in range(1, 4):
        for axis_number in range(3):
            laplace = laplace + coefficients[offset] * (jnp.roll(field, offset, axis_number) + jnp.roll(field, -offset, axis_number))
    return -0.5 / (spacing * spacing) * laplace + potential * field

def filtered(field, potential):
    first = (hamiltonian(field, potential) - filter_centre * field) / filter_half
    second = 2.0 * (hamiltonian(first, potential) - filter_centre * first) / filter_half - field
    third = 2.0 * (hamiltonian(second, potential) - filter_centre * second) / filter_half - first
    return third

def orthonormal(block, cell_total):
    gram = jnp.dot(block.astype(jnp.float32), block.T.astype(jnp.float32), precision=lax.Precision.HIGHEST, preferred_element_type=jnp.float32) / cell_total
    lower = jnp.linalg.cholesky(gram)
    return lax.linalg.triangular_solve(lower, block, left_side=True, lower=True)

def reference(orbitals, potential):

    def one_orbital(field):
        return filtered(field, potential)
    result = lax.map(one_orbital, orbitals)
    flat = result.reshape(ORBITALS, -1)
    cell_total = NX * NY * NZ
    basis = orthonormal(orthonormal(flat, cell_total), cell_total)
    return basis.reshape(result.shape)
```

```python
import functools

import jax
import jax.numpy as jnp
from jax import lax
from jax.experimental import pallas as pl
from jax.experimental.pallas import tpu as pltpu
from jax.sharding import Mesh
from jax.sharding import PartitionSpec as P

coefficients = (-49.0 / 18.0, 1.5, -0.15, 1.0 / 90.0)
spacing = 0.5
filter_centre = 23.0
filter_half = 23.0

REACH = 3
STEPS = 3
DEEP = REACH * STEPS
WIDE = REACH * (STEPS - 1)
EIGHT = 8
GROUP = 6
ALL = ("pair", "side", "orb")

VMEM = pl.BlockSpec(memory_space=pltpu.VMEM)
SMEM = pl.BlockSpec(memory_space=pltpu.SMEM)

kinetic = -0.5 / (spacing * spacing)
taps = tuple(kinetic * c / filter_half for c in coefficients)
shift = (kinetic * 3.0 * coefficients[0] - filter_centre) / filter_half


def filter_kernel(side_ref, own, swapped, slanted, straight, own_pot, pot_far, out, field, first, second, weight):
    side = side_ref[0]
    kept, rows, cols, _ = swapped.shape
    both = 2 * rows
    strips = cols // EIGHT

    def keep(ref, orbital, row, strip, value):
        ref[orbital, row, pl.ds(EIGHT * (strip + 1), EIGHT), :] = value
        if strip == 0:
            ref[orbital, row, pl.ds(cols + EIGHT, EIGHT), :] = value
        if strip == strips - 1:
            ref[orbital, row, pl.ds(0, EIGHT), :] = value

    def gather(source, orbital_from, count, row_to):
        for orbital in range(kept):

            def body(row, carry, orbital=orbital):
                for strip in range(strips):
                    value = source[orbital_from + orbital, row, pl.ds(EIGHT * strip, EIGHT), :]
                    keep(field, orbital, row_to + row, strip, value)
                return carry

            lax.fori_loop(0, count, body, 0)

    gather(own, side * kept, rows, DEEP + side * rows)
    gather(swapped, 0, rows, DEEP + (1 - side) * rows)
    gather(slanted, 0, DEEP, side * (both + DEEP))
    gather(straight, 0, DEEP, (1 - side) * (both + DEEP))

    def weigh(values):
        return values * (1.0 / filter_half) + shift

    weight[pl.ds(WIDE + side * rows, rows)] = weigh(own_pot[...])
    weight[pl.ds(WIDE + (1 - side) * rows, rows)] = weigh(pot_far[pl.ds(0, rows)])
    weight[pl.ds(side * (both + WIDE), WIDE)] = weigh(pot_far[pl.ds(rows, WIDE)])
    weight[pl.ds((1 - side) * (both + WIDE), WIDE)] = weigh(pot_far[pl.ds(rows + WIDE, WIDE)])

    def step(source, before, before_at, weight_at, total, store):
        width = source.shape[3]
        blocks = total // GROUP

        def body(index, carry):
            orbital = index // blocks
            base = (index % blocks) * GROUP
            for strip in range(strips):
                start = EIGHT * (strip + 1)
                window = [source[orbital, base + i, pl.ds(start, EIGHT), :] for i in range(GROUP + 2 * REACH)]
                for i in range(GROUP):
                    row = base + i
                    centre = window[i + REACH]
                    value = centre * weight[weight_at + row, pl.ds(EIGHT * strip, EIGHT), :]
                    for k in range(1, REACH + 1):
                        near = window[i + REACH - k] + window[i + REACH + k]
                        near = near + (
                            source[orbital, row + REACH, pl.ds(start - k, EIGHT), :]
                            + source[orbital, row + REACH, pl.ds(start + k, EIGHT), :]
                        )
                        near = near + (pltpu.roll(centre, k, 1) + pltpu.roll(centre, width - k, 1))
                        value = value + taps[k] * near
                    if before is not None:
                        value = 2.0 * value - before[orbital, before_at + row, pl.ds(start, EIGHT), :]
                    store(orbital, row, strip, value)
            return carry

        lax.fori_loop(0, kept * blocks, body, 0)

    step(field, None, 0, 0, both + 2 * WIDE, functools.partial(keep, first))
    step(first, field, 2 * REACH, REACH, both + 2 * REACH, functools.partial(keep, second))
    piece = out.shape[3]

    def store_out(orbital, row, strip, value):
        to = (EIGHT * strip) // piece
        half = row // rows
        out[2 * to + half, orbital, row - half * rows, pl.ds(EIGHT * strip - to * piece, EIGHT), :] = value

    step(second, first, 2 * REACH, 2 * REACH, both, store_out)


def filtered_pieces(side, own, swapped, slanted, straight, own_pot, pot_far, orb_count):
    kept, rows, cols, width = swapped.shape
    both = 2 * rows

    def scratch(margin):
        return pltpu.VMEM((kept, both + 2 * margin, cols + 2 * EIGHT, width), jnp.float32)

    return pl.pallas_call(
        filter_kernel,
        out_shape=jax.ShapeDtypeStruct((2 * orb_count, kept, rows, cols // orb_count, width), jnp.float32),
        in_specs=[SMEM] + [VMEM] * 6,
        out_specs=VMEM,
        scratch_shapes=[
            scratch(DEEP),
            scratch(WIDE),
            scratch(REACH),
            pltpu.VMEM((both + 2 * WIDE, cols, width), jnp.float32),
        ],
    )(side[None], own, swapped, slanted, straight, own_pot, pot_far)


def summed_everywhere(part, devices):
    copies = lax.all_to_all(jnp.broadcast_to(part[None], (devices,) + part.shape), ALL, 0, 0)
    return jnp.sum(copies, axis=0)


def orthonormal(flat, cell_total, devices):
    local_gram = jnp.dot(flat, flat.T, precision=lax.Precision.HIGHEST, preferred_element_type=jnp.float32)
    gram = summed_everywhere(local_gram, devices) / cell_total
    lower = jnp.linalg.cholesky(gram)
    return lax.linalg.triangular_solve(lower, flat, left_side=True, lower=True)


def on_device(orbitals, potential):
    pair_count, orb_count = lax.axis_size("pair"), lax.axis_size("orb")
    slabs = 2 * pair_count
    side, orb = lax.axis_index("side"), lax.axis_index("orb")
    held, rows, cols, width = orbitals.shape
    kept = held // 2
    part = cols // orb_count

    slant = [(i, (i + (1 if i % 2 else -1)) % slabs) for i in range(slabs)]
    ahead = [(i, (i + (2 if i % 2 else -2)) % slabs) for i in range(slabs)]
    swap = [(0, 1), (1, 0)]
    slab_axes = ("pair", "side")

    mine = lax.dynamic_slice_in_dim(potential, orb * part, part, axis=1)
    edge = lax.dynamic_slice_in_dim(mine, side * (rows - WIDE), WIDE, axis=0)
    pot_far = jnp.concatenate(
        [
            lax.ppermute(mine, "side", swap),
            lax.ppermute(edge, slab_axes, slant),
            lax.ppermute(edge, slab_axes, ahead),
        ],
        axis=0,
    )
    reach = 1
    while reach < orb_count:
        other = lax.ppermute(pot_far, "orb", [(i, i ^ reach) for i in range(orb_count)])
        low = (orb // reach) % 2 == 0
        pot_far = jnp.concatenate([jnp.where(low, pot_far, other), jnp.where(low, other, pot_far)], axis=1)
        reach *= 2

    given = lax.dynamic_slice_in_dim(orbitals, (1 - side) * kept, kept, axis=0)
    edges = lax.dynamic_slice_in_dim(orbitals, side * (rows - DEEP), DEEP, axis=1)
    given_edge = lax.dynamic_slice_in_dim(edges, (1 - side) * kept, kept, axis=0)
    kept_edge = lax.dynamic_slice_in_dim(edges, side * kept, kept, axis=0)
    swapped = lax.ppermute(given, "side", swap)
    slanted = lax.ppermute(given_edge, slab_axes, slant)
    straight = lax.ppermute(kept_edge, slab_axes, ahead)

    pieces = filtered_pieces(side, orbitals, swapped, slanted, straight, potential, pot_far, orb_count)
    grouped = lax.all_to_all(pieces, ("orb", "side"), 0, 0)
    total = held * orb_count
    devices = slabs * orb_count
    flat = grouped.reshape(total, -1)
    cell_total = flat.shape[1] * devices
    basis = orthonormal(orthonormal(flat, cell_total, devices), cell_total, devices)
    basis = basis.reshape(total, rows, part, width)
    return lax.all_to_all(basis, "orb", split_axis=0, concat_axis=2, tiled=True)


def solution(mesh):
    slabs, orb_count = mesh.shape["dom"], mesh.shape["orb"]
    fine = Mesh(mesh.devices.reshape(slabs // 2, 2, orb_count), ALL)
    spec = P("orb", ("pair", "side"), None, None)
    return jax.shard_map(
        on_device,
        mesh=fine,
        in_specs=(spec, P(("pair", "side"), None, None)),
        out_specs=spec,
        check_vma=False,
    )
```

```python
import functools

import jax
import jax.numpy as jnp
from jax import lax
from jax.experimental import pallas as pl
from jax.experimental.pallas import tpu as pltpu
from jax.sharding import Mesh
from jax.sharding import PartitionSpec as P

coefficients = (-49.0 / 18.0, 1.5, -0.15, 1.0 / 90.0)
spacing = 0.5
filter_centre = 23.0
filter_half = 23.0

REACH = 3
STEPS = 3
DEEP = REACH * STEPS
WIDE = REACH * (STEPS - 1)
EIGHT = 8
GROUP = 6
ALL = ("pair", "side", "orb")

VMEM = pl.BlockSpec(memory_space=pltpu.VMEM)
SMEM = pl.BlockSpec(memory_space=pltpu.SMEM)

kinetic = -0.5 / (spacing * spacing)
taps = tuple(kinetic * c / filter_half for c in coefficients)
shift = (kinetic * 3.0 * coefficients[0] - filter_centre) / filter_half


def filter_kernel(side_ref, own, swapped, slanted, straight, own_pot, pot_far, out, field, first, second, weight):
    side = side_ref[0]
    kept, rows, cols, _ = swapped.shape
    both = 2 * rows
    strips = cols // EIGHT

    def keep(ref, orbital, row, strip, value):
        ref[orbital, row, pl.ds(EIGHT * (strip + 1), EIGHT), :] = value
        if strip == 0:
            ref[orbital, row, pl.ds(cols + EIGHT, EIGHT), :] = value
        if strip == strips - 1:
            ref[orbital, row, pl.ds(0, EIGHT), :] = value

    def gather(source, orbital_from, count, row_to):
        for orbital in range(kept):

            def body(row, carry, orbital=orbital):
                for strip in range(strips):
                    value = source[orbital_from + orbital, row, pl.ds(EIGHT * strip, EIGHT), :]
                    keep(field, orbital, row_to + row, strip, value)
                return carry

            lax.fori_loop(0, count, body, 0)

    gather(own, side * kept, rows, DEEP + side * rows)
    gather(swapped, 0, rows, DEEP + (1 - side) * rows)
    gather(slanted, 0, DEEP, side * (both + DEEP))
    gather(straight, 0, DEEP, (1 - side) * (both + DEEP))

    def weigh(values):
        return values * (1.0 / filter_half) + shift

    weight[pl.ds(WIDE + side * rows, rows)] = weigh(own_pot[...])
    weight[pl.ds(WIDE + (1 - side) * rows, rows)] = weigh(pot_far[pl.ds(0, rows)])
    weight[pl.ds(side * (both + WIDE), WIDE)] = weigh(pot_far[pl.ds(rows, WIDE)])
    weight[pl.ds((1 - side) * (both + WIDE), WIDE)] = weigh(pot_far[pl.ds(rows + WIDE, WIDE)])

    def step(source, before, before_at, weight_at, total, store):
        width = source.shape[3]
        blocks = total // GROUP

        def body(index, carry):
            orbital = index // blocks
            base = (index % blocks) * GROUP
            for strip in range(strips):
                start = EIGHT * (strip + 1)
                window = [source[orbital, base + i, pl.ds(start, EIGHT), :] for i in range(GROUP + 2 * REACH)]
                for i in range(GROUP):
                    row = base + i
                    centre = window[i + REACH]
                    value = centre * weight[weight_at + row, pl.ds(EIGHT * strip, EIGHT), :]
                    left, right = pltpu.roll(centre, 1, 1), pltpu.roll(centre, width - 1, 1)
                    far = taps[3] * centre
                    value = value + pltpu.roll(taps[2] * right + far, 3, 1)
                    value = value + pltpu.roll(taps[2] * left + far, width - 3, 1)
                    for k in range(1, REACH + 1):
                        near = window[i + REACH - k] + window[i + REACH + k]
                        near = near + (
                            source[orbital, row + REACH, pl.ds(start - k, EIGHT), :]
                            + source[orbital, row + REACH, pl.ds(start + k, EIGHT), :]
                        )
                        if k == 1:
                            near = near + (left + right)
                        value = value + taps[k] * near
                    if before is not None:
                        value = 2.0 * value - before[orbital, before_at + row, pl.ds(start, EIGHT), :]
                    store(orbital, row, strip, value)
            return carry

        lax.fori_loop(0, kept * blocks, body, 0)

    step(field, None, 0, 0, both + 2 * WIDE, functools.partial(keep, first))
    step(first, field, 2 * REACH, REACH, both + 2 * REACH, functools.partial(keep, second))
    piece = out.shape[3]

    def store_out(orbital, row, strip, value):
        to = (EIGHT * strip) // piece
        half = row // rows
        out[2 * to + half, orbital, row - half * rows, pl.ds(EIGHT * strip - to * piece, EIGHT), :] = value

    step(second, first, 2 * REACH, 2 * REACH, both, store_out)


def filtered_pieces(side, own, swapped, slanted, straight, own_pot, pot_far, orb_count):
    kept, rows, cols, width = swapped.shape
    both = 2 * rows

    def scratch(margin):
        return pltpu.VMEM((kept, both + 2 * margin, cols + 2 * EIGHT, width), jnp.float32)

    return pl.pallas_call(
        filter_kernel,
        out_shape=jax.ShapeDtypeStruct((2 * orb_count, kept, rows, cols // orb_count, width), jnp.float32),
        in_specs=[SMEM] + [VMEM] * 6,
        out_specs=VMEM,
        scratch_shapes=[
            scratch(DEEP),
            scratch(WIDE),
            scratch(REACH),
            pltpu.VMEM((both + 2 * WIDE, cols, width), jnp.float32),
        ],
    )(side[None], own, swapped, slanted, straight, own_pot, pot_far)


def factor_kernel(cell_total, copies, inverse):
    total = inverse.shape[0]
    gram = jnp.sum(copies[...], axis=0) * (1.0 / cell_total)
    lanes = 128
    row = lax.broadcasted_iota(jnp.int32, (total, total), 0)
    column = lax.broadcasted_iota(jnp.int32, (total, total), 1)
    unit = jnp.where(row == column, 1.0, 0.0).astype(jnp.float32)
    table = jnp.concatenate([gram, unit, jnp.zeros((total, lanes - 2 * total), jnp.float32)], axis=1)
    index = lax.broadcasted_iota(jnp.int32, (total, lanes), 0)
    for j in range(total):
        pivot = table[j : j + 1, :]
        scale = lax.rsqrt(table[j : j + 1, j : j + 1])
        scale = scale * (1.5 - 0.5 * table[j : j + 1, j : j + 1] * scale * scale)
        scaled = pivot * scale
        factor = table[:, j : j + 1] * scale
        table = jnp.where(index == j, scaled, jnp.where(index > j, table - factor * scaled, table))
    inverse[...] = table[:, total : 2 * total]


def orthonormal(flat, cell_total, devices):
    total = flat.shape[0]
    local_gram = jnp.dot(flat, flat.T, precision=lax.Precision.HIGHEST, preferred_element_type=jnp.float32)
    copies = lax.all_to_all(jnp.broadcast_to(local_gram[None], (devices, total, total)), ALL, 0, 0)
    inverse = pl.pallas_call(
        functools.partial(factor_kernel, cell_total),
        out_shape=jax.ShapeDtypeStruct((total, total), jnp.float32),
        in_specs=[VMEM],
        out_specs=VMEM,
    )(copies)
    return jnp.dot(inverse, flat, precision=lax.Precision.HIGHEST, preferred_element_type=jnp.float32)


def whole(orbitals, potential):
    pair_count, orb_count = lax.axis_size("pair"), lax.axis_size("orb")
    slabs = 2 * pair_count
    side, orb = lax.axis_index("side"), lax.axis_index("orb")
    held, rows, cols, width = orbitals.shape
    kept = held // 2
    part = cols // orb_count

    slant = [(i, (i + (1 if i % 2 else -1)) % slabs) for i in range(slabs)]
    ahead = [(i, (i + (2 if i % 2 else -2)) % slabs) for i in range(slabs)]
    swap = [(0, 1), (1, 0)]
    slab_axes = ("pair", "side")

    mine = lax.dynamic_slice_in_dim(potential, orb * part, part, axis=1)
    edge = lax.dynamic_slice_in_dim(mine, side * (rows - WIDE), WIDE, axis=0)
    pot_far = jnp.concatenate(
        [lax.ppermute(mine, "side", swap), lax.ppermute(edge, slab_axes, slant), lax.ppermute(edge, slab_axes, ahead)],
        axis=0,
    )
    reach = 1
    while reach < orb_count:
        other = lax.ppermute(pot_far, "orb", [(i, i ^ reach) for i in range(orb_count)])
        low = (orb // reach) % 2 == 0
        pot_far = jnp.concatenate([jnp.where(low, pot_far, other), jnp.where(low, other, pot_far)], axis=1)
        reach *= 2

    given = lax.dynamic_slice_in_dim(orbitals, (1 - side) * kept, kept, axis=0)
    edges = lax.dynamic_slice_in_dim(orbitals, side * (rows - DEEP), DEEP, axis=1)
    given_edge = lax.dynamic_slice_in_dim(edges, (1 - side) * kept, kept, axis=0)
    kept_edge = lax.dynamic_slice_in_dim(edges, side * kept, kept, axis=0)
    slanted = lax.ppermute(given_edge, slab_axes, slant)
    swapped = lax.ppermute(given, "side", swap)
    straight = lax.ppermute(kept_edge, slab_axes, ahead)

    pieces = filtered_pieces(side, orbitals, swapped, slanted, straight, potential, pot_far, orb_count)
    grouped = lax.all_to_all(pieces, ("orb", "side"), 0, 0)
    total = held * orb_count
    devices = slabs * orb_count
    flat = grouped.reshape(total, -1)
    cell_total = flat.shape[1] * devices
    basis = orthonormal(orthonormal(flat, cell_total, devices), cell_total, devices)
    basis = basis.reshape(total, rows, part, width)
    return lax.all_to_all(basis, "orb", split_axis=0, concat_axis=2, tiled=True)


def solution(mesh):
    slabs, orb_count = mesh.shape["dom"], mesh.shape["orb"]
    fine = Mesh(mesh.devices.reshape(slabs // 2, 2, orb_count), ALL)
    spec = P("orb", ("pair", "side"), None, None)
    return jax.shard_map(
        whole,
        mesh=fine,
        in_specs=(spec, P(("pair", "side"), None, None)),
        out_specs=spec,
        check_vma=False,
    )
```

```python
import functools

import jax
import jax.numpy as jnp
from jax import lax
from jax.experimental import pallas as pl
from jax.experimental.pallas import tpu as pltpu
from jax.sharding import Mesh
from jax.sharding import PartitionSpec as P

coefficients = (-49.0 / 18.0, 1.5, -0.15, 1.0 / 90.0)
spacing = 0.5
filter_centre = 23.0
filter_half = 23.0

REACH = 3
STEPS = 3
DEEP = REACH * STEPS
WIDE = REACH * (STEPS - 1)
EIGHT = 8
BLOCKS = 3
ALL = ("pair", "side", "orb")

VMEM = pl.BlockSpec(memory_space=pltpu.VMEM)
SMEM = pl.BlockSpec(memory_space=pltpu.SMEM)

kinetic = -0.5 / (spacing * spacing)
taps = tuple(kinetic * c / filter_half for c in coefficients)
denominator = 180.0
whole_taps = tuple(round(denominator * c) for c in coefficients)
lane_scale = kinetic / filter_half / denominator
shift = (kinetic * 2.0 * coefficients[0] - filter_centre) / filter_half


def split_dot(values, table):
    high = values.astype(jnp.bfloat16)
    rest = values - high.astype(jnp.float32)
    middle = rest.astype(jnp.bfloat16)
    low = (rest - middle.astype(jnp.float32)).astype(jnp.bfloat16)
    wide = jnp.concatenate([high, middle], axis=1)
    twice = jnp.concatenate([table, table], axis=0)
    return jnp.dot(wide, twice, preferred_element_type=jnp.float32) + jnp.dot(
        low, table, preferred_element_type=jnp.float32
    )


def filter_kernel(at, place, own, swapped, slanted, straight, own_pot, pot_far, lane_table, *rest):
    outs, (field, first, second, weight, sorted_pieces) = rest[:-5], rest[-5:]
    side, me = place[0], place[1]
    rows, cols, _ = swapped.shape
    both = 2 * rows
    strips = cols // EIGHT

    def keep(ref, row, strip, value):
        ref[row, pl.ds(EIGHT * (strip + 1), EIGHT), :] = value
        if strip == 0:
            ref[row, pl.ds(cols + EIGHT, EIGHT), :] = value
        if strip == strips - 1:
            ref[row, pl.ds(0, EIGHT), :] = value

    def gather(load, count, row_to):
        def body(row, carry):
            for strip in range(strips):
                keep(field, row_to + row, strip, load(row, pl.ds(EIGHT * strip, EIGHT)))
            return carry

        lax.fori_loop(0, count, body, 0, unroll=3)

    kept = own.shape[0] // 2
    gather(lambda row, span: own[side * kept + at, row, span, :], rows, DEEP + side * rows)
    gather(lambda row, span: swapped[row, span, :], rows, DEEP + (1 - side) * rows)
    gather(lambda row, span: slanted[row, span, :], DEEP, side * (both + DEEP))
    gather(lambda row, span: straight[row, span, :], DEEP, (1 - side) * (both + DEEP))

    def weigh(values):
        return values * (1.0 / filter_half) + shift

    weight[pl.ds(WIDE + side * rows, rows)] = weigh(own_pot[...])
    weight[pl.ds(WIDE + (1 - side) * rows, rows)] = weigh(pot_far[pl.ds(0, rows)])
    weight[pl.ds(side * (both + WIDE), WIDE)] = weigh(pot_far[pl.ds(rows, WIDE)])
    weight[pl.ds((1 - side) * (both + WIDE), WIDE)] = weigh(pot_far[pl.ds(rows + WIDE, WIDE)])

    def step(source, before, before_at, weight_at, total, store):
        width = source.shape[2]
        count = total // BLOCKS

        def body(index, carry):
            base = index * count
            centres = source[pl.ds(base + REACH, count), pl.ds(EIGHT, cols), :]
            along = split_dot(centres.reshape(count * cols, width), lane_table[...])
            for strip in range(strips):
                start = EIGHT * (strip + 1)
                window = [source[base + i, pl.ds(start, EIGHT), :] for i in range(count + 2 * REACH)]
                for i in range(count):
                    row = base + i
                    value = window[i + REACH] * weight[weight_at + row, pl.ds(EIGHT * strip, EIGHT), :]
                    from_lanes = i * cols + EIGHT * strip
                    value = value + along[from_lanes : from_lanes + EIGHT] * lane_scale
                    for k in range(1, REACH + 1):
                        near = window[i + REACH - k] + window[i + REACH + k]
                        near = near + (
                            source[row + REACH, pl.ds(start - k, EIGHT), :]
                            + source[row + REACH, pl.ds(start + k, EIGHT), :]
                        )
                        value = value + taps[k] * near
                    if before is not None:
                        value = 2.0 * value - before[before_at + row, pl.ds(start, EIGHT), :]
                    store(row, strip, value)
            return carry

        lax.fori_loop(0, BLOCKS, body, 0)

    step(field, None, 0, 0, both + 2 * WIDE, functools.partial(keep, first))
    step(first, field, 2 * REACH, REACH, both + 2 * REACH, functools.partial(keep, second))
    piece = sorted_pieces.shape[2]

    def store_out(row, strip, value):
        to = (EIGHT * strip) // piece
        half = row // rows
        sorted_pieces[2 * to + half, row - half * rows, pl.ds(EIGHT * strip - to * piece, EIGHT), :] = value

    step(second, first, 2 * REACH, 2 * REACH, both, store_out)
    for apart, out in enumerate(outs):
        out[...] = sorted_pieces[me ^ apart]


def filtered_pieces(at, place, own, swapped, slanted, straight, own_pot, pot_far, group):
    rows, cols, width = swapped.shape
    both = 2 * rows
    apart = jnp.arange(width)[:, None] - jnp.arange(width)[None, :]
    lane_table = jnp.zeros((width, width), jnp.float32)
    for k, tap in enumerate(whole_taps):
        hit = (apart % width == k) | (-apart % width == k)
        lane_table = jnp.where(hit, float(tap), lane_table)

    def scratch(margin):
        return pltpu.VMEM((both + 2 * margin, cols + 2 * EIGHT, width), jnp.float32)

    piece = (rows, 2 * cols // group, width)
    return pl.pallas_call(
        functools.partial(filter_kernel, at),
        out_shape=[jax.ShapeDtypeStruct(piece, jnp.float32)] * group,
        in_specs=[SMEM] + [VMEM] * 7,
        out_specs=[VMEM] * group,
        scratch_shapes=[
            scratch(DEEP),
            scratch(WIDE),
            scratch(REACH),
            pltpu.VMEM((both + 2 * WIDE, cols, width), jnp.float32),
            pltpu.VMEM((group,) + piece, jnp.float32),
        ],
        compiler_params=pltpu.CompilerParams(vmem_limit_bytes=24 * 1024 * 1024),
    )(place, own, swapped, slanted, straight, own_pot, pot_far, lane_table.astype(jnp.bfloat16))


def sort_kernel(place, *refs):
    given, out = refs[:-1], refs[-1]
    kept = out.shape[1]
    for index, ref in enumerate(given):
        out[place[1] ^ (index // kept), index % kept] = ref[...]


def factor_kernel(cell_total, copies, inverse):
    total = inverse.shape[0]
    gram = jnp.sum(copies[...], axis=0) * (1.0 / cell_total)
    lanes = 128
    row = lax.broadcasted_iota(jnp.int32, (total, total), 0)
    column = lax.broadcasted_iota(jnp.int32, (total, total), 1)
    unit = jnp.where(row == column, 1.0, 0.0).astype(jnp.float32)
    table = jnp.concatenate([gram, unit, jnp.zeros((total, lanes - 2 * total), jnp.float32)], axis=1)
    index = lax.broadcasted_iota(jnp.int32, (total, lanes), 0)
    for j in range(total):
        pivot = table[j : j + 1, :]
        scale = lax.rsqrt(table[j : j + 1, j : j + 1])
        scale = scale * (1.5 - 0.5 * table[j : j + 1, j : j + 1] * scale * scale)
        scaled = pivot * scale
        factor = table[:, j : j + 1] * scale
        table = jnp.where(index == j, scaled, jnp.where(index > j, table - factor * scaled, table))
    inverse[...] = table[:, total : 2 * total]


def orthonormal(flat, cell_total, devices):
    total = flat.shape[0]
    local_gram = jnp.dot(flat, flat.T, precision=lax.Precision.HIGHEST, preferred_element_type=jnp.float32)
    copies = lax.all_to_all(jnp.broadcast_to(local_gram[None], (devices, total, total)), ALL, 0, 0)
    inverse = pl.pallas_call(
        functools.partial(factor_kernel, cell_total),
        out_shape=jax.ShapeDtypeStruct((total, total), jnp.float32),
        in_specs=[VMEM],
        out_specs=VMEM,
    )(copies)
    return jnp.dot(inverse, flat, precision=lax.Precision.HIGHEST, preferred_element_type=jnp.float32)


def whole(orbitals, potential):
    pair_count, orb_count = lax.axis_size("pair"), lax.axis_size("orb")
    slabs = 2 * pair_count
    side, orb = lax.axis_index("side"), lax.axis_index("orb")
    held, rows, cols, width = orbitals.shape
    kept = held // 2
    part = cols // orb_count

    slant = [(i, (i + (1 if i % 2 else -1)) % slabs) for i in range(slabs)]
    ahead = [(i, (i + (2 if i % 2 else -2)) % slabs) for i in range(slabs)]
    swap = [(0, 1), (1, 0)]
    slab_axes = ("pair", "side")

    mine = lax.dynamic_slice_in_dim(potential, orb * part, part, axis=1)
    edge = lax.dynamic_slice_in_dim(mine, side * (rows - WIDE), WIDE, axis=0)
    pot_far = [
        lax.ppermute(mine, "side", swap),
        lax.ppermute(edge, slab_axes, slant),
        lax.ppermute(edge, slab_axes, ahead),
    ]
    pot_far = jnp.concatenate(pot_far, axis=0)
    reach = 1
    while reach < orb_count:
        other = lax.ppermute(pot_far, "orb", [(i, i ^ reach) for i in range(orb_count)])
        low = (orb // reach) % 2 == 0
        pot_far = jnp.concatenate([jnp.where(low, pot_far, other), jnp.where(low, other, pot_far)], axis=1)
        reach *= 2

    fetched = []
    for at in range(kept):
        given = lax.dynamic_index_in_dim(orbitals, (1 - side) * kept + at, 0, keepdims=False)
        given_edge = lax.dynamic_slice_in_dim(given, side * (rows - DEEP), DEEP, axis=0)
        stays = lax.dynamic_index_in_dim(orbitals, side * kept + at, 0, keepdims=False)
        stays_edge = lax.dynamic_slice_in_dim(stays, side * (rows - DEEP), DEEP, axis=0)
        fetched.append(
            (
                lax.ppermute(given, "side", swap),
                lax.ppermute(given_edge, slab_axes, slant),
                lax.ppermute(stays_edge, slab_axes, ahead),
            )
        )

    group = 2 * orb_count
    me = 2 * orb + side

    def flat_of(index):
        return (index % 2) * orb_count + index // 2

    place = jnp.stack([side, me]).astype(jnp.int32)
    returned = []
    for at in range(kept):
        pieces = filtered_pieces(at, place, orbitals, *fetched[at], potential, pot_far, group)
        returned.append(
            [pieces[0]]
            + [
                lax.ppermute(pieces[m], ("side", "orb"), [(flat_of(i), flat_of(i ^ m)) for i in range(group)])
                for m in range(1, group)
            ]
        )
    grouped = pl.pallas_call(
        sort_kernel,
        out_shape=jax.ShapeDtypeStruct((group, kept, rows, part, width), jnp.float32),
        in_specs=[SMEM] + [VMEM] * (group * kept),
        out_specs=VMEM,
        compiler_params=pltpu.CompilerParams(vmem_limit_bytes=16 * 1024 * 1024),
    )(place, *[returned[at][m] for m in range(group) for at in range(kept)])
    total = held * orb_count
    devices = slabs * orb_count
    flat = grouped.reshape(total, -1)
    cell_total = flat.shape[1] * devices
    basis = orthonormal(orthonormal(flat, cell_total, devices), cell_total, devices)
    basis = basis.reshape(total, rows, part, width)
    return lax.all_to_all(basis, "orb", split_axis=0, concat_axis=2, tiled=True)


def solution(mesh):
    slabs, orb_count = mesh.shape["dom"], mesh.shape["orb"]
    fine = Mesh(mesh.devices.reshape(slabs // 2, 2, orb_count), ALL)
    spec = P("orb", ("pair", "side"), None, None)
    return jax.shard_map(
        whole,
        mesh=fine,
        in_specs=(spec, P(("pair", "side"), None, None)),
        out_specs=spec,
        check_vma=False,
    )
```

```python
import functools

import jax
import jax.numpy as jnp
from jax import lax
from jax.experimental import pallas as pl
from jax.experimental.pallas import tpu as pltpu
from jax.sharding import Mesh
from jax.sharding import PartitionSpec as P

coefficients = (-49.0 / 18.0, 1.5, -0.15, 1.0 / 90.0)
spacing = 0.5
filter_centre = 23.0
filter_half = 23.0

REACH = 3
STEPS = 3
DEEP = REACH * STEPS
WIDE = REACH * (STEPS - 1)
EIGHT = 8
BLOCKS = 3
ALL = ("pair", "side", "orb")

VMEM = pl.BlockSpec(memory_space=pltpu.VMEM)
SMEM = pl.BlockSpec(memory_space=pltpu.SMEM)
HBM = pl.BlockSpec(memory_space=pltpu.HBM)

kinetic = -0.5 / (spacing * spacing)
taps = tuple(kinetic * c / filter_half for c in coefficients)
denominator = 180.0
whole_taps = tuple(round(denominator * c) for c in coefficients)
lane_scale = kinetic / filter_half / denominator
shift = (kinetic * 2.0 * coefficients[0] - filter_centre) / filter_half


def pack_kernel(place, orbitals, potential, *rest):
    outs, sems = rest[:-1], rest[-1]
    side, orb = place[0], place[2]
    kept, rows = orbitals.shape[0] // 2, orbitals.shape[1]
    part = outs[0].shape[1]
    columns = pl.ds(pl.multiple_of(orb * part, part), part)
    edge, shallow = pl.ds(side * (rows - DEEP), DEEP), pl.ds(side * (rows - WIDE), WIDE)
    sources = [potential.at[:, columns], potential.at[shallow, columns]]
    for at in range(kept):
        given, stays = orbitals.at[(1 - side) * kept + at], orbitals.at[side * kept + at]
        sources += [given.at[edge], given, stays.at[edge]]
    copies = [pltpu.make_async_copy(a, b, sems.at[i]) for i, (a, b) in enumerate(zip(sources, outs))]
    for copy in copies:
        copy.start()
    for copy in copies:
        copy.wait()


def packed(place, orbitals, potential, orb_count):
    held, rows, cols, width = orbitals.shape
    part = cols // orb_count
    shapes = [(rows, part, width), (WIDE, part, width)]
    shapes += [(DEEP, cols, width), (rows, cols, width), (DEEP, cols, width)] * (held // 2)
    return pl.pallas_call(
        pack_kernel,
        out_shape=[jax.ShapeDtypeStruct(shape, jnp.float32) for shape in shapes],
        in_specs=[SMEM, HBM, HBM],
        out_specs=[VMEM] * len(shapes),
        scratch_shapes=[pltpu.SemaphoreType.DMA((len(shapes),))],
        compiler_params=pltpu.CompilerParams(vmem_limit_bytes=16 * 1024 * 1024),
    )(place, orbitals, potential)


def join_kernel(swapped, slanted, straight, out):
    rows = swapped.shape[0]
    out[pl.ds(0, rows)] = swapped[...]
    out[pl.ds(rows, WIDE)] = slanted[...]
    out[pl.ds(rows + WIDE, WIDE)] = straight[...]


def split_dot(values, table):
    high = values.astype(jnp.bfloat16)
    rest = values - high.astype(jnp.float32)
    middle = rest.astype(jnp.bfloat16)
    low = (rest - middle.astype(jnp.float32)).astype(jnp.bfloat16)
    wide = jnp.concatenate([high, middle], axis=1)
    twice = jnp.concatenate([table, table], axis=0)
    return jnp.dot(wide, twice, preferred_element_type=jnp.float32) + jnp.dot(
        low, table, preferred_element_type=jnp.float32
    )


def filter_kernel(at, shares, place, own, swapped, slanted, straight, own_pot, lane_table, *rest):
    pot_far, outs = rest[:shares], rest[shares:-5]
    field, first, second, weight, sorted_pieces = rest[-5:]
    side, me, orb = place[0], place[1], place[2]
    rows, cols, _ = swapped.shape
    both = 2 * rows
    strips = cols // EIGHT

    def keep(ref, row, strip, value):
        ref[row, pl.ds(EIGHT * (strip + 1), EIGHT), :] = value
        if strip == 0:
            ref[row, pl.ds(cols + EIGHT, EIGHT), :] = value
        if strip == strips - 1:
            ref[row, pl.ds(0, EIGHT), :] = value

    def gather(load, count, row_to):
        def body(row, carry):
            for strip in range(strips):
                keep(field, row_to + row, strip, load(row, pl.ds(EIGHT * strip, EIGHT)))
            return carry

        lax.fori_loop(0, count, body, 0, unroll=3)

    kept = own.shape[0] // 2
    gather(lambda row, span: own[side * kept + at, row, span, :], rows, DEEP + side * rows)
    gather(lambda row, span: swapped[row, span, :], rows, DEEP + (1 - side) * rows)
    gather(lambda row, span: slanted[row, span, :], DEEP, side * (both + DEEP))
    gather(lambda row, span: straight[row, span, :], DEEP, (1 - side) * (both + DEEP))

    def weigh(values):
        return values * (1.0 / filter_half) + shift

    weight[pl.ds(WIDE + side * rows, rows)] = weigh(own_pot[...])
    part = cols // shares
    for apart, far in enumerate(pot_far):
        columns = pl.ds(pl.multiple_of((orb ^ apart) * part, part), part)
        weight[pl.ds(WIDE + (1 - side) * rows, rows), columns] = weigh(far[pl.ds(0, rows)])
        weight[pl.ds(side * (both + WIDE), WIDE), columns] = weigh(far[pl.ds(rows, WIDE)])
        weight[pl.ds((1 - side) * (both + WIDE), WIDE), columns] = weigh(far[pl.ds(rows + WIDE, WIDE)])

    def step(source, before, before_at, weight_at, total, store):
        width = source.shape[2]
        count = total // BLOCKS

        def body(index, carry):
            base = index * count
            centres = source[pl.ds(base + REACH, count), pl.ds(EIGHT, cols), :]
            along = split_dot(centres.reshape(count * cols, width), lane_table[...])
            for strip in range(strips):
                start = EIGHT * (strip + 1)
                window = [source[base + i, pl.ds(start, EIGHT), :] for i in range(count + 2 * REACH)]
                for i in range(count):
                    row = base + i
                    value = window[i + REACH] * weight[weight_at + row, pl.ds(EIGHT * strip, EIGHT), :]
                    from_lanes = i * cols + EIGHT * strip
                    value = value + along[from_lanes : from_lanes + EIGHT] * lane_scale
                    for k in range(1, REACH + 1):
                        near = window[i + REACH - k] + window[i + REACH + k]
                        near = near + (
                            source[row + REACH, pl.ds(start - k, EIGHT), :]
                            + source[row + REACH, pl.ds(start + k, EIGHT), :]
                        )
                        value = value + taps[k] * near
                    if before is not None:
                        value = 2.0 * value - before[before_at + row, pl.ds(start, EIGHT), :]
                    store(row, strip, value)
            return carry

        lax.fori_loop(0, BLOCKS, body, 0)

    step(field, None, 0, 0, both + 2 * WIDE, functools.partial(keep, first))
    step(first, field, 2 * REACH, REACH, both + 2 * REACH, functools.partial(keep, second))
    piece = sorted_pieces.shape[2]

    def store_out(row, strip, value):
        to = (EIGHT * strip) // piece
        half = row // rows
        sorted_pieces[2 * to + half, row - half * rows, pl.ds(EIGHT * strip - to * piece, EIGHT), :] = value

    step(second, first, 2 * REACH, 2 * REACH, both, store_out)
    for apart, out in enumerate(outs):
        out[...] = sorted_pieces[me ^ apart]


def filtered_pieces(at, place, own, slanted_order, own_pot, pot_far, group):
    rows, cols, width = own.shape[1:]
    both = 2 * rows
    apart = jnp.arange(width)[:, None] - jnp.arange(width)[None, :]
    lane_table = jnp.zeros((width, width), jnp.float32)
    for k, tap in enumerate(whole_taps):
        hit = (apart % width == k) | (-apart % width == k)
        lane_table = jnp.where(hit, float(tap), lane_table)

    def scratch(margin):
        return pltpu.VMEM((both + 2 * margin, cols + 2 * EIGHT, width), jnp.float32)

    piece = (rows, 2 * cols // group, width)
    return pl.pallas_call(
        functools.partial(filter_kernel, at, len(pot_far)),
        out_shape=[jax.ShapeDtypeStruct(piece, jnp.float32)] * group,
        in_specs=[SMEM] + [VMEM] * (6 + len(pot_far)),
        out_specs=[VMEM] * group,
        scratch_shapes=[
            scratch(DEEP),
            scratch(WIDE),
            scratch(REACH),
            pltpu.VMEM((both + 2 * WIDE, cols, width), jnp.float32),
            pltpu.VMEM((group,) + piece, jnp.float32),
        ],
        compiler_params=pltpu.CompilerParams(vmem_limit_bytes=24 * 1024 * 1024),
    )(place, own, slanted_order[1], slanted_order[0], slanted_order[2], own_pot, lane_table.astype(jnp.bfloat16), *pot_far)


def sort_kernel(place, *refs):
    given, out = refs[:-1], refs[-1]
    kept = out.shape[1]
    for index, ref in enumerate(given):
        out[place[1] ^ (index // kept), index % kept] = ref[...]


def factor_kernel(cell_total, copies, inverse):
    total = inverse.shape[0]
    gram = jnp.sum(copies[...], axis=0) * (1.0 / cell_total)
    lanes = 128
    row = lax.broadcasted_iota(jnp.int32, (total, total), 0)
    column = lax.broadcasted_iota(jnp.int32, (total, total), 1)
    unit = jnp.where(row == column, 1.0, 0.0).astype(jnp.float32)
    table = jnp.concatenate([gram, unit, jnp.zeros((total, lanes - 2 * total), jnp.float32)], axis=1)
    index = lax.broadcasted_iota(jnp.int32, (total, lanes), 0)
    for j in range(total):
        pivot = table[j : j + 1, :]
        scale = lax.rsqrt(table[j : j + 1, j : j + 1])
        scale = scale * (1.5 - 0.5 * table[j : j + 1, j : j + 1] * scale * scale)
        scaled = pivot * scale
        factor = table[:, j : j + 1] * scale
        table = jnp.where(index == j, scaled, jnp.where(index > j, table - factor * scaled, table))
    inverse[...] = table[:, total : 2 * total]


def orthonormal(flat, cell_total, devices):
    total = flat.shape[0]
    local_gram = jnp.dot(flat, flat.T, precision=lax.Precision.HIGHEST, preferred_element_type=jnp.float32)
    copies = lax.all_to_all(jnp.broadcast_to(local_gram[None], (devices, total, total)), ALL, 0, 0)
    inverse = pl.pallas_call(
        functools.partial(factor_kernel, cell_total),
        out_shape=jax.ShapeDtypeStruct((total, total), jnp.float32),
        in_specs=[VMEM],
        out_specs=VMEM,
    )(copies)
    return jnp.dot(inverse, flat, precision=lax.Precision.HIGHEST, preferred_element_type=jnp.float32)


def whole(orbitals, potential):
    pair_count, orb_count = lax.axis_size("pair"), lax.axis_size("orb")
    slabs = 2 * pair_count
    side, orb = lax.axis_index("side"), lax.axis_index("orb")
    held, rows, cols, width = orbitals.shape
    kept = held // 2
    part = cols // orb_count

    slant = [(i, (i + (1 if i % 2 else -1)) % slabs) for i in range(slabs)]
    ahead = [(i, (i + (2 if i % 2 else -2)) % slabs) for i in range(slabs)]
    swap = [(0, 1), (1, 0)]
    slab_axes = ("pair", "side")

    group = 2 * orb_count
    me = 2 * orb + side

    def flat_of(index):
        return (index % 2) * orb_count + index // 2

    place = jnp.stack([side, me, orb]).astype(jnp.int32)
    mine, edge, *sent = packed(place, orbitals, potential, orb_count)

    pieces = [
        lax.ppermute(mine, "side", swap),
        lax.ppermute(edge, slab_axes, slant),
        lax.ppermute(edge, slab_axes, ahead),
    ]
    joined = pl.pallas_call(
        join_kernel,
        out_shape=jax.ShapeDtypeStruct((rows + 2 * WIDE, part, width), jnp.float32),
        in_specs=[VMEM] * 3,
        out_specs=VMEM,
        compiler_params=pltpu.CompilerParams(vmem_limit_bytes=16 * 1024 * 1024),
    )(*pieces)
    pot_far = [joined] + [
        lax.ppermute(joined, "orb", [(i, i ^ m) for i in range(orb_count)]) for m in range(1, orb_count)
    ]

    fetched = []
    for at in range(kept):
        fetched.append(
            (
                lax.ppermute(sent[3 * at], slab_axes, slant),
                lax.ppermute(sent[3 * at + 1], "side", swap),
                lax.ppermute(sent[3 * at + 2], slab_axes, ahead),
            )
        )

    returned = []
    order = sorted(range(1, group), key=lambda m: (-(m // 4 > 0) - m % 2, m))
    spot = {m: 1 + index for index, m in enumerate(order)} | {0: 0}
    for at in range(kept):
        pieces = filtered_pieces(at, place, orbitals, fetched[at], potential, pot_far, group)
        returned.append(
            [pieces[0]]
            + [
                lax.ppermute(pieces[m], ("side", "orb"), [(flat_of(i), flat_of(i ^ m)) for i in range(group)])
                for m in order
            ]
        )
    grouped = pl.pallas_call(
        sort_kernel,
        out_shape=jax.ShapeDtypeStruct((group, kept, rows, part, width), jnp.float32),
        in_specs=[SMEM] + [VMEM] * (group * kept),
        out_specs=VMEM,
        compiler_params=pltpu.CompilerParams(vmem_limit_bytes=16 * 1024 * 1024),
    )(place, *[returned[at][spot[m]] for m in range(group) for at in range(kept)])
    total = held * orb_count
    devices = slabs * orb_count
    flat = grouped.reshape(total, -1)
    cell_total = flat.shape[1] * devices
    basis = orthonormal(orthonormal(flat, cell_total, devices), cell_total, devices)
    basis = basis.reshape(total, rows, part, width)
    return lax.all_to_all(basis, "orb", split_axis=0, concat_axis=2, tiled=True)


def solution(mesh):
    slabs, orb_count = mesh.shape["dom"], mesh.shape["orb"]
    fine = Mesh(mesh.devices.reshape(slabs // 2, 2, orb_count), ALL)
    spec = P("orb", ("pair", "side"), None, None)
    return jax.shard_map(
        whole,
        mesh=fine,
        in_specs=(spec, P(("pair", "side"), None, None)),
        out_specs=spec,
        check_vma=False,
    )
```

```python
import functools

import jax
import jax.numpy as jnp
from jax import lax
from jax.experimental import pallas as pl
from jax.experimental.pallas import tpu as pltpu
from jax.sharding import Mesh
from jax.sharding import PartitionSpec as P

coefficients = (-49.0 / 18.0, 1.5, -0.15, 1.0 / 90.0)
spacing = 0.5
filter_centre = 23.0
filter_half = 23.0

REACH = 3
STEPS = 3
DEEP = REACH * STEPS
WIDE = REACH * (STEPS - 1)
EIGHT = 8
BLOCKS = 3
ALL = ("pair", "side", "orb")

VMEM = pl.BlockSpec(memory_space=pltpu.VMEM)
SMEM = pl.BlockSpec(memory_space=pltpu.SMEM)
HBM = pl.BlockSpec(memory_space=pltpu.HBM)

kinetic = -0.5 / (spacing * spacing)
taps = tuple(kinetic * c / filter_half for c in coefficients)
denominator = 180.0
whole_taps = tuple(round(denominator * c) for c in coefficients)
lane_scale = kinetic / filter_half / denominator
shift = (kinetic * 2.0 * coefficients[0] - filter_centre) / filter_half


def pack_kernel(place, orbitals, potential, *rest):
    outs, sems = rest[:-1], rest[-1]
    side, orb = place[0], place[2]
    kept, rows = orbitals.shape[0] // 2, orbitals.shape[1]
    part = outs[0].shape[1]
    columns = pl.ds(pl.multiple_of(orb * part, part), part)
    edge, shallow = pl.ds(side * (rows - DEEP), DEEP), pl.ds(side * (rows - WIDE), WIDE)
    sources = [potential.at[:, columns], potential.at[shallow, columns]]
    for at in range(kept):
        given, stays = orbitals.at[(1 - side) * kept + at], orbitals.at[side * kept + at]
        sources += [given.at[edge], given, stays.at[edge]]
    copies = [pltpu.make_async_copy(a, b, sems.at[i]) for i, (a, b) in enumerate(zip(sources, outs))]
    for copy in copies:
        copy.start()
    for copy in copies:
        copy.wait()


def packed(place, orbitals, potential, orb_count):
    held, rows, cols, width = orbitals.shape
    part = cols // orb_count
    shapes = [(rows, part, width), (WIDE, part, width)]
    shapes += [(DEEP, cols, width), (rows, cols, width), (DEEP, cols, width)] * (held // 2)
    return pl.pallas_call(
        pack_kernel,
        out_shape=[jax.ShapeDtypeStruct(shape, jnp.float32) for shape in shapes],
        in_specs=[SMEM, HBM, HBM],
        out_specs=[VMEM] * len(shapes),
        scratch_shapes=[pltpu.SemaphoreType.DMA((len(shapes),))],
        compiler_params=pltpu.CompilerParams(vmem_limit_bytes=16 * 1024 * 1024),
    )(place, orbitals, potential)


def join_kernel(swapped, slanted, straight, out):
    rows = swapped.shape[0]
    out[pl.ds(0, rows)] = swapped[...]
    out[pl.ds(rows, WIDE)] = slanted[...]
    out[pl.ds(rows + WIDE, WIDE)] = straight[...]


def split_dot(values, table):
    high = values.astype(jnp.bfloat16)
    rest = values - high.astype(jnp.float32)
    middle = rest.astype(jnp.bfloat16)
    low = (rest - middle.astype(jnp.float32)).astype(jnp.bfloat16)
    wide = jnp.concatenate([high, middle], axis=1)
    twice = jnp.concatenate([table, table], axis=0)
    return jnp.dot(wide, twice, preferred_element_type=jnp.float32) + jnp.dot(
        low, table, preferred_element_type=jnp.float32
    )


def filter_kernel(at, shares, place, own, swapped, slanted, straight, own_pot, lane_table, *rest):
    pot_far, outs = rest[:shares], rest[shares:-5]
    field, first, second, weight, sorted_pieces = rest[-5:]
    side, me, orb = place[0], place[1], place[2]
    rows, cols, _ = swapped.shape
    both = 2 * rows
    strips = cols // EIGHT

    def keep(ref, row, strip, value):
        ref[row, pl.ds(EIGHT * (strip + 1), EIGHT), :] = value
        if strip == 0:
            ref[row, pl.ds(cols + EIGHT, EIGHT), :] = value
        if strip == strips - 1:
            ref[row, pl.ds(0, EIGHT), :] = value

    def gather(load, count, row_to):
        def body(row, carry):
            for strip in range(strips):
                keep(field, row_to + row, strip, load(row, pl.ds(EIGHT * strip, EIGHT)))
            return carry

        lax.fori_loop(0, count, body, 0, unroll=3)

    kept = own.shape[0] // 2
    gather(lambda row, span: own[side * kept + at, row, span, :], rows, DEEP + side * rows)
    gather(lambda row, span: swapped[row, span, :], rows, DEEP + (1 - side) * rows)
    gather(lambda row, span: slanted[row, span, :], DEEP, side * (both + DEEP))
    gather(lambda row, span: straight[row, span, :], DEEP, (1 - side) * (both + DEEP))

    def weigh(values):
        return values * (1.0 / filter_half) + shift

    weight[pl.ds(WIDE + side * rows, rows)] = weigh(own_pot[...])
    part = cols // shares
    for apart, far in enumerate(pot_far):
        columns = pl.ds(pl.multiple_of((orb ^ apart) * part, part), part)
        weight[pl.ds(WIDE + (1 - side) * rows, rows), columns] = weigh(far[pl.ds(0, rows)])
        weight[pl.ds(side * (both + WIDE), WIDE), columns] = weigh(far[pl.ds(rows, WIDE)])
        weight[pl.ds((1 - side) * (both + WIDE), WIDE), columns] = weigh(far[pl.ds(rows + WIDE, WIDE)])

    def step(source, before, before_at, weight_at, total, store):
        width = source.shape[2]
        count = total // BLOCKS

        def body(index, carry):
            base = index * count
            centres = source[pl.ds(base + REACH, count), pl.ds(EIGHT, cols), :]
            along = split_dot(centres.reshape(count * cols, width), lane_table[...])
            for strip in range(strips):
                start = EIGHT * (strip + 1)
                window = [source[base + i, pl.ds(start, EIGHT), :] for i in range(count + 2 * REACH)]
                for i in range(count):
                    row = base + i
                    value = window[i + REACH] * weight[weight_at + row, pl.ds(EIGHT * strip, EIGHT), :]
                    from_lanes = i * cols + EIGHT * strip
                    value = value + along[from_lanes : from_lanes + EIGHT] * lane_scale
                    for k in range(1, REACH + 1):
                        near = window[i + REACH - k] + window[i + REACH + k]
                        near = near + (
                            source[row + REACH, pl.ds(start - k, EIGHT), :]
                            + source[row + REACH, pl.ds(start + k, EIGHT), :]
                        )
                        value = value + taps[k] * near
                    if before is not None:
                        value = 2.0 * value - before[before_at + row, pl.ds(start, EIGHT), :]
                    store(row, strip, value)
            return carry

        lax.fori_loop(0, BLOCKS, body, 0)

    step(field, None, 0, 0, both + 2 * WIDE, functools.partial(keep, first))
    step(first, field, 2 * REACH, REACH, both + 2 * REACH, functools.partial(keep, second))
    piece = sorted_pieces.shape[2]

    def store_out(row, strip, value):
        to = (EIGHT * strip) // piece
        half = row // rows
        sorted_pieces[2 * to + half, row - half * rows, pl.ds(EIGHT * strip - to * piece, EIGHT), :] = value

    step(second, first, 2 * REACH, 2 * REACH, both, store_out)
    for apart, out in enumerate(outs):
        out[...] = sorted_pieces[me ^ apart]


def filtered_pieces(at, place, own, slanted_order, own_pot, pot_far, group):
    rows, cols, width = own.shape[1:]
    both = 2 * rows
    apart = jnp.arange(width)[:, None] - jnp.arange(width)[None, :]
    lane_table = jnp.zeros((width, width), jnp.float32)
    for k, tap in enumerate(whole_taps):
        hit = (apart % width == k) | (-apart % width == k)
        lane_table = jnp.where(hit, float(tap), lane_table)

    def scratch(margin):
        return pltpu.VMEM((both + 2 * margin, cols + 2 * EIGHT, width), jnp.float32)

    piece = (rows, 2 * cols // group, width)
    return pl.pallas_call(
        functools.partial(filter_kernel, at, len(pot_far)),
        out_shape=[jax.ShapeDtypeStruct(piece, jnp.float32)] * group,
        in_specs=[SMEM] + [VMEM] * (6 + len(pot_far)),
        out_specs=[VMEM] * group,
        scratch_shapes=[
            scratch(DEEP),
            scratch(WIDE),
            scratch(REACH),
            pltpu.VMEM((both + 2 * WIDE, cols, width), jnp.float32),
            pltpu.VMEM((group,) + piece, jnp.float32),
        ],
        compiler_params=pltpu.CompilerParams(vmem_limit_bytes=24 * 1024 * 1024),
    )(place, own, slanted_order[1], slanted_order[0], slanted_order[2], own_pot, lane_table.astype(jnp.bfloat16), *pot_far)


LANES = 128


def exact_dot(a, b, contract=((1,), (0,))):
    return lax.dot_general(
        a, b, (contract, ((), ())), precision=lax.Precision.HIGHEST, preferred_element_type=jnp.float32
    )


def table_of(shape, test):
    rows = lax.broadcasted_iota(jnp.int32, shape, 0)
    columns = lax.broadcasted_iota(jnp.int32, shape, 1)
    return jnp.where(test(rows, columns), 1.0, 0.0).astype(jnp.float32)


def gram_message(read, total, tiles, chunk):
    tall = total * EIGHT

    def body(index, sums):
        wide = jnp.concatenate([read(index * chunk + t) for t in range(chunk)], axis=1)
        return sums + exact_dot(wide, wide, ((1,), (1,)))

    sums = lax.fori_loop(0, tiles // chunk, body, jnp.zeros((tall, tall), jnp.float32))
    sums = sums * table_of((tall, tall), lambda r, c: r % EIGHT == c % EIGHT)
    partial = exact_dot(table_of((total, tall), lambda r, c: c // EIGHT == r), sums)
    spread = exact_dot(partial, table_of((tall, LANES), lambda r, c: r // EIGHT == c % total))
    per = LANES // total
    spread = spread * table_of((total, LANES), lambda r, c: c // total == r % per)
    return jnp.concatenate(
        [jnp.sum(spread[i * per : (i + 1) * per], axis=0, keepdims=True) for i in range(total // per)], axis=1
    )


def inverse_factor(copies, total, cell_total):
    row = jnp.sum(copies[...], axis=0) * (1.0 / cell_total)
    per = LANES // total
    wide = jnp.concatenate(
        [jnp.broadcast_to(row[:, i * LANES : (i + 1) * LANES], (per, LANES)) for i in range(total // per)], axis=0
    )
    wide = wide * table_of((total, LANES), lambda r, c: c // total == r % per)
    table = exact_dot(wide, table_of((LANES, LANES), lambda r, c: r % total == c))
    table = table + table_of((total, LANES), lambda r, c: c - total == r)
    index = lax.broadcasted_iota(jnp.int32, (total, LANES), 0)
    for j in range(total):
        value = table[j : j + 1, j : j + 1]
        scale = lax.rsqrt(value)
        scale = scale * (1.5 - 0.5 * value * scale * scale)
        scaled = table[j : j + 1, :] * scale
        factor = table[:, j : j + 1] * scale
        table = jnp.where(index == j, scaled, jnp.where(index > j, table - factor * scaled, table))
    return table


def by_tiles(table, total):
    tall = total * EIGHT
    wide = exact_dot(table, table_of((LANES, tall), lambda r, c: r - total == c // EIGHT))
    both = exact_dot(table_of((tall, total), lambda r, c: r // EIGHT == c), wide)
    return both * table_of((tall, tall), lambda r, c: r % EIGHT == c % EIGHT)


def tile_reader(ref):
    total, width = ref.shape[0], ref.shape[2]
    return lambda t: ref[:, pl.ds(pl.multiple_of(EIGHT * t, EIGHT), EIGHT), :].reshape(total * EIGHT, width)


def chunk_of(tiles):
    return next(c for c in (6, 4, 3, 2, 1) if tiles % c == 0)


def first_kernel(kept, place, *refs):
    given, (block, message) = refs[:-2], refs[-2:]
    for index, ref in enumerate(given):
        block[(place[1] ^ (index // kept)) * kept + index % kept] = ref[...].reshape(block.shape[1:])
    total, tiles = block.shape[0], block.shape[1] // EIGHT
    row = gram_message(tile_reader(block), total, tiles, chunk_of(tiles))
    message[...] = jnp.broadcast_to(row[None], message.shape)


def second_kernel(cell_total, copies, block, basis, message):
    total, tiles = block.shape[0], block.shape[1] // EIGHT
    apply_all(inverse_factor(copies, total, cell_total), block, basis)
    row = gram_message(tile_reader(basis), total, tiles, chunk_of(tiles))
    message[...] = jnp.broadcast_to(row[None], message.shape)


def third_kernel(cell_total, copies, block, basis):
    apply_all(inverse_factor(copies, block.shape[0], cell_total), block, basis)


def apply_all(table, block, basis):
    total, tiles, width = block.shape[0], block.shape[1] // EIGHT, block.shape[2]
    matrix = by_tiles(table, total)
    read, chunk = tile_reader(block), chunk_of(tiles)

    def body(index, carry):
        wide = jnp.concatenate([read(index * chunk + t) for t in range(chunk)], axis=1)
        result = exact_dot(matrix, wide)
        for t in range(chunk):
            piece = result[:, t * width : (t + 1) * width].reshape(total, EIGHT, width)
            basis[:, pl.ds(pl.multiple_of(EIGHT * (index * chunk + t), EIGHT), EIGHT), :] = piece
        return carry

    lax.fori_loop(0, tiles // chunk, body, 0)


def small_call(kernel, out_shape, specs, *args):
    return pl.pallas_call(
        kernel,
        out_shape=out_shape,
        in_specs=specs,
        out_specs=jax.tree.map(lambda _: VMEM, out_shape),
        compiler_params=pltpu.CompilerParams(vmem_limit_bytes=24 * 1024 * 1024),
    )(*args)


def whole(orbitals, potential):
    pair_count, orb_count = lax.axis_size("pair"), lax.axis_size("orb")
    slabs = 2 * pair_count
    side, orb = lax.axis_index("side"), lax.axis_index("orb")
    held, rows, cols, width = orbitals.shape
    kept = held // 2
    part = cols // orb_count

    slant = [(i, (i + (1 if i % 2 else -1)) % slabs) for i in range(slabs)]
    ahead = [(i, (i + (2 if i % 2 else -2)) % slabs) for i in range(slabs)]
    swap = [(0, 1), (1, 0)]
    slab_axes = ("pair", "side")

    group = 2 * orb_count
    me = 2 * orb + side

    def flat_of(index):
        return (index % 2) * orb_count + index // 2

    place = jnp.stack([side, me, orb]).astype(jnp.int32)
    mine, edge, *sent = packed(place, orbitals, potential, orb_count)

    pieces = [
        lax.ppermute(mine, "side", swap),
        lax.ppermute(edge, slab_axes, slant),
        lax.ppermute(edge, slab_axes, ahead),
    ]
    joined = pl.pallas_call(
        join_kernel,
        out_shape=jax.ShapeDtypeStruct((rows + 2 * WIDE, part, width), jnp.float32),
        in_specs=[VMEM] * 3,
        out_specs=VMEM,
        compiler_params=pltpu.CompilerParams(vmem_limit_bytes=16 * 1024 * 1024),
    )(*pieces)
    pot_far = [joined] + [
        lax.ppermute(joined, "orb", [(i, i ^ m) for i in range(orb_count)]) for m in range(1, orb_count)
    ]

    fetched = []
    for at in range(kept):
        fetched.append(
            (
                lax.ppermute(sent[3 * at], slab_axes, slant),
                lax.ppermute(sent[3 * at + 1], "side", swap),
                lax.ppermute(sent[3 * at + 2], slab_axes, ahead),
            )
        )

    returned = []
    order = sorted(range(1, group), key=lambda m: (-(m // 4 > 0) - m % 2, m))
    spot = {m: 1 + index for index, m in enumerate(order)} | {0: 0}
    for at in range(kept):
        pieces = filtered_pieces(at, place, orbitals, fetched[at], potential, pot_far, group)
        returned.append(
            [pieces[0]]
            + [
                lax.ppermute(pieces[m], ("side", "orb"), [(flat_of(i), flat_of(i ^ m)) for i in range(group)])
                for m in order
            ]
        )
    total, devices = held * orb_count, slabs * orb_count
    cell_total = rows * part * width * devices
    block_shape = jax.ShapeDtypeStruct((total, rows * part, width), jnp.float32)
    message_shape = jax.ShapeDtypeStruct((devices, 1, total * total), jnp.float32)

    def exchanged(message):
        return lax.all_to_all(message, ALL, 0, 0)

    parts = [returned[at][spot[m]] for m in range(group) for at in range(kept)]
    block, message = small_call(
        functools.partial(first_kernel, kept), [block_shape, message_shape], [SMEM] + [VMEM] * len(parts), place, *parts
    )
    basis, message = small_call(
        functools.partial(second_kernel, cell_total), [block_shape, message_shape], [VMEM] * 2, exchanged(message), block
    )
    basis = small_call(
        functools.partial(third_kernel, cell_total), block_shape, [VMEM] * 2, exchanged(message), basis
    )
    basis = basis.reshape(total, rows, part, width)
    return lax.all_to_all(basis, "orb", split_axis=0, concat_axis=2, tiled=True)


def solution(mesh):
    slabs, orb_count = mesh.shape["dom"], mesh.shape["orb"]
    fine = Mesh(mesh.devices.reshape(slabs // 2, 2, orb_count), ALL)
    spec = P("orb", ("pair", "side"), None, None)
    return jax.shard_map(
        whole,
        mesh=fine,
        in_specs=(spec, P(("pair", "side"), None, None)),
        out_specs=spec,
        check_vma=False,
    )
```

```python
import functools

import jax
import jax.numpy as jnp
from jax import lax
from jax.experimental import pallas as pl
from jax.experimental.pallas import tpu as pltpu
from jax.sharding import Mesh
from jax.sharding import PartitionSpec as P

coefficients = (-49.0 / 18.0, 1.5, -0.15, 1.0 / 90.0)
spacing = 0.5
filter_centre = 23.0
filter_half = 23.0

REACH = 3
STEPS = 3
DEEP = REACH * STEPS
WIDE = REACH * (STEPS - 1)
EIGHT = 8
CORES = 2
BLOCKS = 3
ALL = ("pair", "side", "orb")

VMEM = pl.BlockSpec(memory_space=pltpu.VMEM)
SMEM = pl.BlockSpec(memory_space=pltpu.SMEM)
HBM = pl.BlockSpec(memory_space=pltpu.HBM)

kinetic = -0.5 / (spacing * spacing)
taps = tuple(kinetic * c / filter_half for c in coefficients)
denominator = 180.0
whole_taps = tuple(round(denominator * c) for c in coefficients)
lane_scale = kinetic / filter_half / denominator
shift = (kinetic * 2.0 * coefficients[0] - filter_centre) / filter_half


def pack_kernel(place, orbitals, potential, *rest):
    outs, sems = rest[:-1], rest[-1]
    side, orb = place[0], place[2]
    kept, rows = orbitals.shape[0] // 2, orbitals.shape[1]
    part = outs[0].shape[1]
    columns = pl.ds(pl.multiple_of(orb * part, part), part)
    edge, shallow = pl.ds(side * (rows - DEEP), DEEP), pl.ds(side * (rows - WIDE), WIDE)
    sources = [potential.at[:, columns], potential.at[shallow, columns]]
    for at in range(kept):
        given, stays = orbitals.at[(1 - side) * kept + at], orbitals.at[side * kept + at]
        sources += [given.at[edge], given, stays.at[edge]]
    copies = [pltpu.make_async_copy(a, b, sems.at[i]) for i, (a, b) in enumerate(zip(sources, outs))]
    for copy in copies:
        copy.start()
    for copy in copies:
        copy.wait()


def packed(place, orbitals, potential, orb_count):
    held, rows, cols, width = orbitals.shape
    part = cols // orb_count
    shapes = [(rows, part, width), (WIDE, part, width)]
    shapes += [(DEEP, cols, width), (rows, cols, width), (DEEP, cols, width)] * (held // 2)
    return pl.pallas_call(
        pack_kernel,
        out_shape=[jax.ShapeDtypeStruct(shape, jnp.float32) for shape in shapes],
        in_specs=[SMEM, HBM, HBM],
        out_specs=[VMEM] * len(shapes),
        scratch_shapes=[pltpu.SemaphoreType.DMA((len(shapes),))],
        compiler_params=pltpu.CompilerParams(vmem_limit_bytes=16 * 1024 * 1024),
    )(place, orbitals, potential)


def join_kernel(swapped, slanted, straight, out):
    rows = swapped.shape[0]
    out[pl.ds(0, rows)] = swapped[...]
    out[pl.ds(rows, WIDE)] = slanted[...]
    out[pl.ds(rows + WIDE, WIDE)] = straight[...]


def split_dot(values, table):
    high = values.astype(jnp.bfloat16)
    rest = values - high.astype(jnp.float32)
    middle = rest.astype(jnp.bfloat16)
    low = (rest - middle.astype(jnp.float32)).astype(jnp.bfloat16)
    wide = jnp.concatenate([high, middle], axis=1)
    twice = jnp.concatenate([table, table], axis=0)
    return jnp.dot(wide, twice, preferred_element_type=jnp.float32) + jnp.dot(
        low, table, preferred_element_type=jnp.float32
    )


def filter_kernel(at, shares, place, own, swapped, slanted, straight, own_pot, lane_table, *rest):
    pot_far, outs = rest[:shares], rest[shares:-5]
    field, first, second, weight, sorted_pieces = rest[-5:]
    side, me, orb = place[0], place[1], place[2]
    rows, cols, _ = swapped.shape
    both = 2 * rows
    strips = cols // EIGHT

    def keep(ref, row, strip, value):
        ref[row, pl.ds(EIGHT * (strip + 1), EIGHT), :] = value
        if strip == 0:
            ref[row, pl.ds(cols + EIGHT, EIGHT), :] = value
        if strip == strips - 1:
            ref[row, pl.ds(0, EIGHT), :] = value

    def gather(load, count, row_to):
        def body(row, carry):
            for strip in range(strips):
                keep(field, row_to + row, strip, load(row, pl.ds(EIGHT * strip, EIGHT)))
            return carry

        lax.fori_loop(0, count, body, 0, unroll=3)

    kept = own.shape[0] // 2
    gather(lambda row, span: own[side * kept + at, row, span, :], rows, DEEP + side * rows)
    gather(lambda row, span: swapped[row, span, :], rows, DEEP + (1 - side) * rows)
    gather(lambda row, span: slanted[row, span, :], DEEP, side * (both + DEEP))
    gather(lambda row, span: straight[row, span, :], DEEP, (1 - side) * (both + DEEP))

    def weigh(values):
        return values * (1.0 / filter_half) + shift

    weight[pl.ds(WIDE + side * rows, rows)] = weigh(own_pot[...])
    part = cols // shares
    for apart, far in enumerate(pot_far):
        columns = pl.ds(pl.multiple_of((orb ^ apart) * part, part), part)
        weight[pl.ds(WIDE + (1 - side) * rows, rows), columns] = weigh(far[pl.ds(0, rows)])
        weight[pl.ds(side * (both + WIDE), WIDE), columns] = weigh(far[pl.ds(rows, WIDE)])
        weight[pl.ds((1 - side) * (both + WIDE), WIDE), columns] = weigh(far[pl.ds(rows + WIDE, WIDE)])

    def step(source, before, before_at, weight_at, total, store):
        width = source.shape[2]
        count = total // BLOCKS

        def body(index, carry):
            base = index * count
            centres = source[pl.ds(base + REACH, count), pl.ds(EIGHT, cols), :]
            along = split_dot(centres.reshape(count * cols, width), lane_table[...])
            for strip in range(strips):
                start = EIGHT * (strip + 1)
                window = [source[base + i, pl.ds(start, EIGHT), :] for i in range(count + 2 * REACH)]
                for i in range(count):
                    row = base + i
                    value = window[i + REACH] * weight[weight_at + row, pl.ds(EIGHT * strip, EIGHT), :]
                    from_lanes = i * cols + EIGHT * strip
                    value = value + along[from_lanes : from_lanes + EIGHT] * lane_scale
                    for k in range(1, REACH + 1):
                        near = window[i + REACH - k] + window[i + REACH + k]
                        near = near + (
                            source[row + REACH, pl.ds(start - k, EIGHT), :]
                            + source[row + REACH, pl.ds(start + k, EIGHT), :]
                        )
                        value = value + taps[k] * near
                    if before is not None:
                        value = 2.0 * value - before[before_at + row, pl.ds(start, EIGHT), :]
                    store(row, strip, value)
            return carry

        lax.fori_loop(0, BLOCKS, body, 0)

    step(field, None, 0, 0, both + 2 * WIDE, functools.partial(keep, first))
    step(first, field, 2 * REACH, REACH, both + 2 * REACH, functools.partial(keep, second))
    piece = sorted_pieces.shape[2]

    def store_out(row, strip, value):
        to = (EIGHT * strip) // piece
        half = row // rows
        sorted_pieces[2 * to + half, row - half * rows, pl.ds(EIGHT * strip - to * piece, EIGHT), :] = value

    step(second, first, 2 * REACH, 2 * REACH, both, store_out)
    group = sorted_pieces.shape[0]
    for apart, out in enumerate(outs[:group]):
        out[...] = sorted_pieces[me ^ apart]
    for index, out in enumerate(outs[group:]):
        chip = orb // CORES ^ (1 if index < 2 else 0)
        slab = side ^ (index % 2)
        for core in range(CORES):
            out[core] = sorted_pieces[2 * (CORES * chip + core) + slab]


def filtered_pieces(at, place, own, slanted_order, own_pot, pot_far, group, spares):
    rows, cols, width = own.shape[1:]
    both = 2 * rows
    apart = jnp.arange(width)[:, None] - jnp.arange(width)[None, :]
    lane_table = jnp.zeros((width, width), jnp.float32)
    for k, tap in enumerate(whole_taps):
        hit = (apart % width == k) | (-apart % width == k)
        lane_table = jnp.where(hit, float(tap), lane_table)

    def scratch(margin):
        return pltpu.VMEM((both + 2 * margin, cols + 2 * EIGHT, width), jnp.float32)

    piece = (rows, 2 * cols // group, width)
    return pl.pallas_call(
        functools.partial(filter_kernel, at, len(pot_far)),
        out_shape=[jax.ShapeDtypeStruct(piece, jnp.float32)] * group
        + [jax.ShapeDtypeStruct((CORES,) + piece, jnp.float32)] * spares,
        in_specs=[SMEM] + [VMEM] * (6 + len(pot_far)),
        out_specs=[VMEM] * (group + spares),
        scratch_shapes=[
            scratch(DEEP),
            scratch(WIDE),
            scratch(REACH),
            pltpu.VMEM((both + 2 * WIDE, cols, width), jnp.float32),
            pltpu.VMEM((group,) + piece, jnp.float32),
        ],
        compiler_params=pltpu.CompilerParams(vmem_limit_bytes=24 * 1024 * 1024),
    )(place, own, slanted_order[1], slanted_order[0], slanted_order[2], own_pot, lane_table.astype(jnp.bfloat16), *pot_far)


LANES = 128


def exact_dot(a, b, contract=((1,), (0,))):
    return lax.dot_general(
        a, b, (contract, ((), ())), precision=lax.Precision.HIGHEST, preferred_element_type=jnp.float32
    )


def table_of(shape, test):
    rows = lax.broadcasted_iota(jnp.int32, shape, 0)
    columns = lax.broadcasted_iota(jnp.int32, shape, 1)
    return jnp.where(test(rows, columns), 1.0, 0.0).astype(jnp.float32)


def gram_message(read, total, tiles, chunk):
    tall = total * EIGHT

    def body(index, sums):
        wide = jnp.concatenate([read(index * chunk + t) for t in range(chunk)], axis=1)
        return sums + exact_dot(wide, wide, ((1,), (1,)))

    sums = lax.fori_loop(0, tiles // chunk, body, jnp.zeros((tall, tall), jnp.float32))
    sums = sums * table_of((tall, tall), lambda r, c: r % EIGHT == c % EIGHT)
    partial = exact_dot(table_of((total, tall), lambda r, c: c // EIGHT == r), sums)
    spread = exact_dot(partial, table_of((tall, LANES), lambda r, c: r // EIGHT == c % total))
    per = LANES // total
    spread = spread * table_of((total, LANES), lambda r, c: c // total == r % per)
    return jnp.concatenate(
        [jnp.sum(spread[i * per : (i + 1) * per], axis=0, keepdims=True) for i in range(total // per)], axis=1
    )


def inverse_factor(copies, total, cell_total):
    row = jnp.sum(copies[...], axis=0) * (1.0 / cell_total)
    per = LANES // total
    wide = jnp.concatenate(
        [jnp.broadcast_to(row[:, i * LANES : (i + 1) * LANES], (per, LANES)) for i in range(total // per)], axis=0
    )
    wide = wide * table_of((total, LANES), lambda r, c: c // total == r % per)
    table = exact_dot(wide, table_of((LANES, LANES), lambda r, c: r % total == c))
    table = table + table_of((total, LANES), lambda r, c: c - total == r)
    index = lax.broadcasted_iota(jnp.int32, (total, LANES), 0)
    for j in range(total):
        value = table[j : j + 1, j : j + 1]
        scale = lax.rsqrt(value)
        scale = scale * (1.5 - 0.5 * value * scale * scale)
        scaled = table[j : j + 1, :] * scale
        factor = table[:, j : j + 1] * scale
        table = jnp.where(index == j, scaled, jnp.where(index > j, table - factor * scaled, table))
    return table


def by_tiles(table, total):
    tall = total * EIGHT
    wide = exact_dot(table, table_of((LANES, tall), lambda r, c: r - total == c // EIGHT))
    both = exact_dot(table_of((tall, total), lambda r, c: r // EIGHT == c), wide)
    return both * table_of((tall, tall), lambda r, c: r % EIGHT == c % EIGHT)


def tile_reader(ref):
    total, width = ref.shape[0], ref.shape[2]
    return lambda t: ref[:, pl.ds(pl.multiple_of(EIGHT * t, EIGHT), EIGHT), :].reshape(total * EIGHT, width)


def chunk_of(tiles):
    return next(c for c in (6, 4, 3, 2, 1) if tiles % c == 0)


def first_kernel(kept, place, *refs):
    given, (block, message) = refs[:-2], refs[-2:]
    for index, ref in enumerate(given):
        block[(place[1] ^ (index // kept)) * kept + index % kept] = ref[...].reshape(block.shape[1:])
    total, tiles = block.shape[0], block.shape[1] // EIGHT
    row = gram_message(tile_reader(block), total, tiles, chunk_of(tiles))
    message[...] = jnp.broadcast_to(row[None], message.shape)


def second_kernel(cell_total, copies, block, basis, message):
    total, tiles = block.shape[0], block.shape[1] // EIGHT
    apply_all(inverse_factor(copies, total, cell_total), block, basis)
    row = gram_message(tile_reader(basis), total, tiles, chunk_of(tiles))
    message[...] = jnp.broadcast_to(row[None], message.shape)


def third_kernel(cell_total, copies, block, basis):
    apply_all(inverse_factor(copies, block.shape[0], cell_total), block, basis)


def second_and_bundle_kernel(cell_total, place, copies, block, *refs):
    given, (table_out, message, bundle, basis) = refs[:-4], refs[-4:]
    total, tiles = block.shape[0], block.shape[1] // EIGHT
    table = inverse_factor(copies, total, cell_total)
    table_out[...] = table
    apply_all(table, block, basis)
    row = gram_message(tile_reader(basis), total, tiles, chunk_of(tiles))
    message[...] = jnp.broadcast_to(row[None], message.shape)
    kept = len(given) // 4
    side = place[0]
    for index, ref in enumerate(given):
        kind, at = index // kept, index % kept
        slot = (kind // 2) * 2 * kept + (side ^ (kind % 2)) * kept + at
        bundle[slot] = ref[...].reshape(bundle.shape[1:])


def last_kernel(cell_total, place, copies, table, block, block_near, bundle, bundle_near, out):
    total, width = block.shape[0], block.shape[2]
    held, rows, _ = out.shape[:3]
    orb = place[2]
    core, chip = orb % CORES, orb // CORES
    tall, short = total * EIGHT, held * EIGHT
    second = inverse_factor(copies, total, cell_total)
    pick = table_of((LANES, total), lambda r, c: r - total == c)
    product = exact_dot(exact_dot(second, pick), exact_dot(table[...], pick))

    def matrix_for(orbital_of):
        wide = exact_dot(product, table_of((total, tall), lambda r, c: orbital_of(c // EIGHT) == r))
        own = exact_dot(table_of((short, total), lambda r, c: orb * held + r // EIGHT == c), wide)
        return own * table_of((short, tall), lambda r, c: r % EIGHT == c % EIGHT)

    def write(matrix, read, tiles, first_column):
        chunk, strips = chunk_of(tiles), tiles // rows

        def body(index, carry):
            wide = jnp.concatenate([read(index * chunk + t) for t in range(chunk)], axis=1)
            result = exact_dot(matrix, wide)
            for t in range(chunk):
                tile = index * chunk + t
                piece = result[:, t * width : (t + 1) * width].reshape(held, EIGHT, width)
                column = pl.multiple_of(first_column + (tile % strips) * EIGHT, EIGHT)
                out[:, tile // strips, pl.ds(column, EIGHT), :] = piece
            return carry

        lax.fori_loop(0, tiles // chunk, body, 0)

    tiles = block.shape[1] // EIGHT
    part = block.shape[1] // rows
    natural = matrix_for(lambda index: index)
    write(natural, tile_reader(block), tiles, orb * part)
    write(natural, tile_reader(block_near), tiles, (orb ^ 1) * part)

    def orbital_of(index):
        kind, local = index // held, index % held
        flip = kind // 2
        quad = jnp.where(kind % 2 == 0, orb ^ flip, core ^ flip)
        return quad * held + local

    mixed = matrix_for(orbital_of)
    for share in range(CORES):

        def read(t, share=share):
            span = pl.ds(pl.multiple_of(share * block.shape[1] + EIGHT * t, EIGHT), EIGHT)
            both = jnp.concatenate([bundle[:, span, :], bundle_near[:, span, :]], axis=0)
            return both.reshape(tall, width)

        write(mixed, read, tiles, ((1 - chip) * CORES + share) * part)


def apply_all(table, block, basis):
    total, tiles, width = block.shape[0], block.shape[1] // EIGHT, block.shape[2]
    matrix = by_tiles(table, total)
    read, chunk = tile_reader(block), chunk_of(tiles)

    def body(index, carry):
        wide = jnp.concatenate([read(index * chunk + t) for t in range(chunk)], axis=1)
        result = exact_dot(matrix, wide)
        for t in range(chunk):
            piece = result[:, t * width : (t + 1) * width].reshape(total, EIGHT, width)
            basis[:, pl.ds(pl.multiple_of(EIGHT * (index * chunk + t), EIGHT), EIGHT), :] = piece
        return carry

    lax.fori_loop(0, tiles // chunk, body, 0)


def small_call(kernel, out_shape, specs, *args):
    return pl.pallas_call(
        kernel,
        out_shape=out_shape,
        in_specs=specs,
        out_specs=jax.tree.map(lambda _: VMEM, out_shape),
        compiler_params=pltpu.CompilerParams(vmem_limit_bytes=24 * 1024 * 1024),
    )(*args)


def whole(orbitals, potential):
    pair_count, orb_count = lax.axis_size("pair"), lax.axis_size("orb")
    slabs = 2 * pair_count
    side, orb = lax.axis_index("side"), lax.axis_index("orb")
    held, rows, cols, width = orbitals.shape
    kept = held // 2
    part = cols // orb_count

    slant = [(i, (i + (1 if i % 2 else -1)) % slabs) for i in range(slabs)]
    ahead = [(i, (i + (2 if i % 2 else -2)) % slabs) for i in range(slabs)]
    swap = [(0, 1), (1, 0)]
    slab_axes = ("pair", "side")

    group = 2 * orb_count
    me = 2 * orb + side

    def flat_of(index):
        return (index % 2) * orb_count + index // 2

    place = jnp.stack([side, me, orb]).astype(jnp.int32)
    mine, edge, *sent = packed(place, orbitals, potential, orb_count)

    pieces = [
        lax.ppermute(mine, "side", swap),
        lax.ppermute(edge, slab_axes, slant),
        lax.ppermute(edge, slab_axes, ahead),
    ]
    joined = pl.pallas_call(
        join_kernel,
        out_shape=jax.ShapeDtypeStruct((rows + 2 * WIDE, part, width), jnp.float32),
        in_specs=[VMEM] * 3,
        out_specs=VMEM,
        compiler_params=pltpu.CompilerParams(vmem_limit_bytes=16 * 1024 * 1024),
    )(*pieces)
    pot_far = [joined] + [
        lax.ppermute(joined, "orb", [(i, i ^ m) for i in range(orb_count)]) for m in range(1, orb_count)
    ]

    fetched = []
    for at in range(kept):
        fetched.append(
            (
                lax.ppermute(sent[3 * at], slab_axes, slant),
                lax.ppermute(sent[3 * at + 1], "side", swap),
                lax.ppermute(sent[3 * at + 2], slab_axes, ahead),
            )
        )

    spares = 4 if orb_count == 2 * CORES and kept == 2 else 0
    returned, spare = [], []
    order = sorted(range(1, group), key=lambda m: (-(m // 4 > 0) - m % 2, m))
    spot = {m: 1 + index for index, m in enumerate(order)} | {0: 0}
    for at in range(kept):
        pieces = filtered_pieces(at, place, orbitals, fetched[at], potential, pot_far, group, spares)
        spare.append(pieces[group:])
        returned.append(
            [pieces[0]]
            + [
                lax.ppermute(pieces[m], ("side", "orb"), [(flat_of(i), flat_of(i ^ m)) for i in range(group)])
                for m in order
            ]
        )
    total, devices = held * orb_count, slabs * orb_count
    cell_total = rows * part * width * devices
    block_shape = jax.ShapeDtypeStruct((total, rows * part, width), jnp.float32)
    message_shape = jax.ShapeDtypeStruct((devices, 1, total * total), jnp.float32)

    def exchanged(message):
        return lax.all_to_all(message, ALL, 0, 0)

    parts = [returned[at][spot[m]] for m in range(group) for at in range(kept)]
    block, message = small_call(
        functools.partial(first_kernel, kept), [block_shape, message_shape], [SMEM] + [VMEM] * len(parts), place, *parts
    )
    if spares:
        up = [(i, i + CORES) for i in range(CORES)]
        slanted_up = [(s * orb_count + i, (1 - s) * orb_count + i + CORES) for s in range(2) for i in range(CORES)]
        cores = [(i, i ^ 1) for i in range(orb_count)]
        given = [spare[at][0] for at in range(kept)]
        given += [lax.ppermute(spare[at][1], "side", swap) for at in range(kept)]
        given += [lax.ppermute(spare[at][2], "orb", up) for at in range(kept)]
        given += [lax.ppermute(spare[at][3], ("side", "orb"), slanted_up) for at in range(kept)]
        block_near = lax.ppermute(block, "orb", cores)
        bundle_shape = jax.ShapeDtypeStruct((2 * held, CORES * rows * part, width), jnp.float32)
        table_shape = jax.ShapeDtypeStruct((total, LANES), jnp.float32)
        table, message, bundle = pl.pallas_call(
            functools.partial(second_and_bundle_kernel, cell_total),
            out_shape=[table_shape, message_shape, bundle_shape],
            in_specs=[SMEM] + [VMEM] * (2 + len(given)),
            out_specs=[VMEM] * 3,
            scratch_shapes=[pltpu.VMEM(block_shape.shape, jnp.float32)],
            compiler_params=pltpu.CompilerParams(vmem_limit_bytes=24 * 1024 * 1024),
        )(place, exchanged(message), block, *given)
        bundle_near = lax.ppermute(bundle, "orb", cores)
        return small_call(
            functools.partial(last_kernel, cell_total),
            jax.ShapeDtypeStruct((held, rows, cols, width), jnp.float32),
            [SMEM] + [VMEM] * 6,
            *(place, exchanged(message), table, block, block_near, bundle, bundle_near),
        )
    basis, message = small_call(
        functools.partial(second_kernel, cell_total), [block_shape, message_shape], [VMEM] * 2, exchanged(message), block
    )
    basis = small_call(
        functools.partial(third_kernel, cell_total), block_shape, [VMEM] * 2, exchanged(message), basis
    )
    basis = basis.reshape(total, rows, part, width)
    return lax.all_to_all(basis, "orb", split_axis=0, concat_axis=2, tiled=True)


def solution(mesh):
    slabs, orb_count = mesh.shape["dom"], mesh.shape["orb"]
    fine = Mesh(mesh.devices.reshape(slabs // 2, 2, orb_count), ALL)
    spec = P("orb", ("pair", "side"), None, None)
    return jax.shard_map(
        whole,
        mesh=fine,
        in_specs=(spec, P(("pair", "side"), None, None)),
        out_specs=spec,
        check_vma=False,
    )
```

```python
import functools

import jax
import jax.numpy as jnp
from jax import lax
from jax.experimental import pallas as pl
from jax.experimental.pallas import tpu as pltpu
from jax.sharding import Mesh
from jax.sharding import PartitionSpec as P

coefficients = (-49.0 / 18.0, 1.5, -0.15, 1.0 / 90.0)
spacing = 0.5
filter_centre = 23.0
filter_half = 23.0

REACH = 3
STEPS = 3
DEEP = REACH * STEPS
WIDE = REACH * (STEPS - 1)
EIGHT = 8
CORES = 2
BLOCKS = 3
ALL = ("pair", "side", "orb")

VMEM = pl.BlockSpec(memory_space=pltpu.VMEM)
SMEM = pl.BlockSpec(memory_space=pltpu.SMEM)
HBM = pl.BlockSpec(memory_space=pltpu.HBM)

kinetic = -0.5 / (spacing * spacing)
taps = tuple(kinetic * c / filter_half for c in coefficients)
denominator = 180.0
whole_taps = tuple(round(denominator * c) for c in coefficients)
lane_scale = kinetic / filter_half / denominator
shift = (kinetic * 2.0 * coefficients[0] - filter_centre) / filter_half


def pack_kernel(place, orbitals, potential, *rest):
    outs, sems = rest[:-1], rest[-1]
    side, orb = place[0], place[2]
    kept, rows = orbitals.shape[0] // 2, orbitals.shape[1]
    part = outs[0].shape[1]
    columns = pl.ds(pl.multiple_of(orb * part, part), part)
    edge, shallow = pl.ds(side * (rows - DEEP), DEEP), pl.ds(side * (rows - WIDE), WIDE)
    sources = [potential.at[:, columns], potential.at[shallow, columns]]
    for at in range(kept):
        given, stays = orbitals.at[(1 - side) * kept + at], orbitals.at[side * kept + at]
        sources += [given.at[edge], given, stays.at[edge]]
    copies = [pltpu.make_async_copy(a, b, sems.at[i]) for i, (a, b) in enumerate(zip(sources, outs))]
    for copy in copies:
        copy.start()
    for copy in copies:
        copy.wait()


def packed(place, orbitals, potential, orb_count):
    held, rows, cols, width = orbitals.shape
    part = cols // orb_count
    shapes = [(rows, part, width), (WIDE, part, width)]
    shapes += [(DEEP, cols, width), (rows, cols, width), (DEEP, cols, width)] * (held // 2)
    return pl.pallas_call(
        pack_kernel,
        out_shape=[jax.ShapeDtypeStruct(shape, jnp.float32) for shape in shapes],
        in_specs=[SMEM, HBM, HBM],
        out_specs=[VMEM] * len(shapes),
        scratch_shapes=[pltpu.SemaphoreType.DMA((len(shapes),))],
        compiler_params=pltpu.CompilerParams(vmem_limit_bytes=16 * 1024 * 1024),
    )(place, orbitals, potential)


def join_kernel(swapped, slanted, straight, out):
    rows = swapped.shape[0]
    out[pl.ds(0, rows)] = swapped[...]
    out[pl.ds(rows, WIDE)] = slanted[...]
    out[pl.ds(rows + WIDE, WIDE)] = straight[...]


def split_dot(values, table):
    high = values.astype(jnp.bfloat16)
    rest = values - high.astype(jnp.float32)
    middle = rest.astype(jnp.bfloat16)
    low = (rest - middle.astype(jnp.float32)).astype(jnp.bfloat16)
    wide = jnp.concatenate([high, middle], axis=1)
    twice = jnp.concatenate([table, table], axis=0)
    return jnp.dot(wide, twice, preferred_element_type=jnp.float32) + jnp.dot(
        low, table, preferred_element_type=jnp.float32
    )


def filter_kernel(at, shares, early, late, place, own, swapped, slanted, straight, own_pot, lane_table, *rest):
    pot_far, before, outs = rest[:shares], rest[shares : shares + at], rest[shares + at : -4]
    field, first, second, weight = rest[-4:]
    outs, sorted_pieces = outs[:-1], outs[-1]
    side, me, orb = place[0], place[1], place[2]
    rows, cols, _ = swapped.shape
    both = 2 * rows
    strips = cols // EIGHT

    def keep(ref, row, strip, value):
        ref[row, pl.ds(EIGHT * (strip + 1), EIGHT), :] = value
        if strip == 0:
            ref[row, pl.ds(cols + EIGHT, EIGHT), :] = value
        if strip == strips - 1:
            ref[row, pl.ds(0, EIGHT), :] = value

    def gather(load, count, row_to):
        def body(row, carry):
            for strip in range(strips):
                keep(field, row_to + row, strip, load(row, pl.ds(EIGHT * strip, EIGHT)))
            return carry

        lax.fori_loop(0, count, body, 0, unroll=3)

    kept = own.shape[0] // 2
    gather(lambda row, span: own[side * kept + at, row, span, :], rows, DEEP + side * rows)
    gather(lambda row, span: swapped[row, span, :], rows, DEEP + (1 - side) * rows)
    gather(lambda row, span: slanted[row, span, :], DEEP, side * (both + DEEP))
    gather(lambda row, span: straight[row, span, :], DEEP, (1 - side) * (both + DEEP))

    def weigh(values):
        return values * (1.0 / filter_half) + shift

    weight[pl.ds(WIDE + side * rows, rows)] = weigh(own_pot[...])
    part = cols // shares
    for apart, far in enumerate(pot_far):
        columns = pl.ds(pl.multiple_of((orb ^ apart) * part, part), part)
        weight[pl.ds(WIDE + (1 - side) * rows, rows), columns] = weigh(far[pl.ds(0, rows)])
        weight[pl.ds(side * (both + WIDE), WIDE), columns] = weigh(far[pl.ds(rows, WIDE)])
        weight[pl.ds((1 - side) * (both + WIDE), WIDE), columns] = weigh(far[pl.ds(rows + WIDE, WIDE)])

    def step(source, before, before_at, weight_at, total, store):
        width = source.shape[2]
        count = total // BLOCKS

        def body(index, carry):
            base = index * count
            centres = source[pl.ds(base + REACH, count), pl.ds(EIGHT, cols), :]
            along = split_dot(centres.reshape(count * cols, width), lane_table[...])
            for strip in range(strips):
                start = EIGHT * (strip + 1)
                window = [source[base + i, pl.ds(start, EIGHT), :] for i in range(count + 2 * REACH)]
                for i in range(count):
                    row = base + i
                    value = window[i + REACH] * weight[weight_at + row, pl.ds(EIGHT * strip, EIGHT), :]
                    from_lanes = i * cols + EIGHT * strip
                    value = value + along[from_lanes : from_lanes + EIGHT] * lane_scale
                    for k in range(1, REACH + 1):
                        near = window[i + REACH - k] + window[i + REACH + k]
                        near = near + (
                            source[row + REACH, pl.ds(start - k, EIGHT), :]
                            + source[row + REACH, pl.ds(start + k, EIGHT), :]
                        )
                        value = value + taps[k] * near
                    if before is not None:
                        value = 2.0 * value - before[before_at + row, pl.ds(start, EIGHT), :]
                    store(row, strip, value)
            return carry

        lax.fori_loop(0, BLOCKS, body, 0)

    step(field, None, 0, 0, both + 2 * WIDE, functools.partial(keep, first))
    step(first, field, 2 * REACH, REACH, both + 2 * REACH, functools.partial(keep, second))
    piece = sorted_pieces.shape[2]

    def store_out(row, strip, value):
        to = (EIGHT * strip) // piece
        half = row // rows
        sorted_pieces[2 * to + half, row - half * rows, pl.ds(EIGHT * strip - to * piece, EIGHT), :] = value

    step(second, first, 2 * REACH, 2 * REACH, both, store_out)
    for apart, out in zip(early, outs):
        out[...] = sorted_pieces[me ^ apart]
    stages = (*before, sorted_pieces)
    for apart, out in zip(late, outs[len(early) :]):
        for stage, pieces in enumerate(stages):
            out[stage] = pieces[me ^ apart]
    for index, out in enumerate(outs[len(early) + len(late) :]):
        chip = orb // CORES ^ (1 if index < 2 else 0)
        slab = side ^ (index % 2)
        for stage, pieces in enumerate(stages):
            for core in range(CORES):
                out[stage, core] = pieces[2 * (CORES * chip + core) + slab]


def filtered_pieces(at, place, own, fetched, own_pot, pot_far, group, before, early, late, spares):
    slanted, swapped, straight = fetched
    rows, cols, width = own.shape[1:]
    both = 2 * rows
    apart = jnp.arange(width)[:, None] - jnp.arange(width)[None, :]
    lane_table = jnp.zeros((width, width), jnp.float32)
    for k, tap in enumerate(whole_taps):
        hit = (apart % width == k) | (-apart % width == k)
        lane_table = jnp.where(hit, float(tap), lane_table)

    def scratch(margin):
        return pltpu.VMEM((both + 2 * margin, cols + 2 * EIGHT, width), jnp.float32)

    piece = (rows, 2 * cols // group, width)
    shapes = [piece] * len(early) + [(at + 1, *piece)] * len(late) + [(at + 1, CORES, *piece)] * spares + [(group, *piece)]
    return pl.pallas_call(
        functools.partial(filter_kernel, at, len(pot_far), early, late),
        out_shape=[jax.ShapeDtypeStruct(shape, jnp.float32) for shape in shapes],
        in_specs=[SMEM] + [VMEM] * (6 + len(pot_far) + at),
        out_specs=[VMEM] * len(shapes),
        scratch_shapes=[
            scratch(DEEP),
            scratch(WIDE),
            scratch(REACH),
            pltpu.VMEM((both + 2 * WIDE, cols, width), jnp.float32),
        ],
        compiler_params=pltpu.CompilerParams(vmem_limit_bytes=24 * 1024 * 1024),
    )(place, own, swapped, slanted, straight, own_pot, lane_table.astype(jnp.bfloat16), *pot_far, *before)


LANES = 128


def exact_dot(a, b, contract=((1,), (0,))):
    return lax.dot_general(
        a, b, (contract, ((), ())), precision=lax.Precision.HIGHEST, preferred_element_type=jnp.float32
    )


def table_of(shape, test):
    rows = lax.broadcasted_iota(jnp.int32, shape, 0)
    columns = lax.broadcasted_iota(jnp.int32, shape, 1)
    return jnp.where(test(rows, columns), 1.0, 0.0).astype(jnp.float32)


def gram_message(read, total, tiles, chunk):
    tall = total * EIGHT

    def body(index, sums):
        wide = jnp.concatenate([read(index * chunk + t) for t in range(chunk)], axis=1)
        return sums + exact_dot(wide, wide, ((1,), (1,)))

    sums = lax.fori_loop(0, tiles // chunk, body, jnp.zeros((tall, tall), jnp.float32))
    sums = sums * table_of((tall, tall), lambda r, c: r % EIGHT == c % EIGHT)
    partial = exact_dot(table_of((total, tall), lambda r, c: c // EIGHT == r), sums)
    spread = exact_dot(partial, table_of((tall, LANES), lambda r, c: r // EIGHT == c % total))
    per = LANES // total
    spread = spread * table_of((total, LANES), lambda r, c: c // total == r % per)
    return jnp.concatenate(
        [jnp.sum(spread[i * per : (i + 1) * per], axis=0, keepdims=True) for i in range(total // per)], axis=1
    )


def inverse_factor(copies, total, cell_total):
    row = jnp.sum(copies[...], axis=0) * (1.0 / cell_total)
    per = LANES // total
    wide = jnp.concatenate(
        [jnp.broadcast_to(row[:, i * LANES : (i + 1) * LANES], (per, LANES)) for i in range(total // per)], axis=0
    )
    wide = wide * table_of((total, LANES), lambda r, c: c // total == r % per)
    table = exact_dot(wide, table_of((LANES, LANES), lambda r, c: r % total == c))
    table = table + table_of((total, LANES), lambda r, c: c - total == r)
    index = lax.broadcasted_iota(jnp.int32, (total, LANES), 0)
    for j in range(total):
        value = table[j : j + 1, j : j + 1]
        scale = lax.rsqrt(value)
        scale = scale * (1.5 - 0.5 * value * scale * scale)
        scaled = table[j : j + 1, :] * scale
        factor = table[:, j : j + 1] * scale
        table = jnp.where(index == j, scaled, jnp.where(index > j, table - factor * scaled, table))
    return table


def by_tiles(table, total):
    tall = total * EIGHT
    wide = exact_dot(table, table_of((LANES, tall), lambda r, c: r - total == c // EIGHT))
    both = exact_dot(table_of((tall, total), lambda r, c: r // EIGHT == c), wide)
    return both * table_of((tall, tall), lambda r, c: r % EIGHT == c % EIGHT)


def tile_reader(ref):
    total, width = ref.shape[0], ref.shape[2]
    return lambda t: ref[:, pl.ds(pl.multiple_of(EIGHT * t, EIGHT), EIGHT), :].reshape(total * EIGHT, width)


def chunk_of(tiles):
    return next(c for c in (6, 4, 3, 2, 1) if tiles % c == 0)


def first_kernel(early, late, kept, place, *refs):
    given, (block, message) = refs[:-2], refs[-2:]
    me, shape = place[1], block.shape[1:]
    for at in range(kept):
        for index, apart in enumerate(early):
            block[(me ^ apart) * kept + at] = given[at * len(early) + index][...].reshape(shape)
        for index, apart in enumerate(late):
            block[(me ^ apart) * kept + at] = given[kept * len(early) + index][at].reshape(shape)
    total, tiles = block.shape[0], block.shape[1] // EIGHT
    row = gram_message(tile_reader(block), total, tiles, chunk_of(tiles))
    message[...] = jnp.broadcast_to(row[None], message.shape)


def second_kernel(cell_total, copies, block, basis, message):
    total, tiles = block.shape[0], block.shape[1] // EIGHT
    apply_all(inverse_factor(copies, total, cell_total), block, basis)
    row = gram_message(tile_reader(basis), total, tiles, chunk_of(tiles))
    message[...] = jnp.broadcast_to(row[None], message.shape)


def third_kernel(cell_total, copies, block, basis):
    apply_all(inverse_factor(copies, block.shape[0], cell_total), block, basis)


def second_and_bundle_kernel(cell_total, place, copies, block, *refs):
    given, (table_out, message, bundle, basis) = refs[:-4], refs[-4:]
    total, tiles = block.shape[0], block.shape[1] // EIGHT
    table = inverse_factor(copies, total, cell_total)
    table_out[...] = table
    apply_all(table, block, basis)
    row = gram_message(tile_reader(basis), total, tiles, chunk_of(tiles))
    message[...] = jnp.broadcast_to(row[None], message.shape)
    side, kept = place[0], given[0].shape[0]
    for kind, ref in enumerate(given):
        for at in range(kept):
            slot = (kind // 2) * 2 * kept + (side ^ (kind % 2)) * kept + at
            bundle[slot] = ref[at].reshape(bundle.shape[1:])


def last_kernel(cell_total, place, copies, table, block, block_near, bundle, bundle_near, out, splats):
    total, length, width = block.shape
    held, rows = out.shape[:2]
    part = length // rows
    orb = place[2]
    core, chip = orb % CORES, orb // CORES
    second = inverse_factor(copies, total, cell_total)
    pick = table_of((LANES, total), lambda r, c: r - total == c)
    product = exact_dot(exact_dot(second, pick), exact_dot(table[...], pick))
    own = exact_dot(table_of((held * EIGHT, total), lambda r, c: orb * held + r // EIGHT == c), product)
    wide = exact_dot(own, table_of((total, total * width), lambda r, c: c // width == r))
    for orbital in range(total):
        splats[orbital] = wide[:, orbital * width : (orbital + 1) * width].reshape(held, EIGHT, width)

    def write(sources, first_column):
        def body(row, carry):
            for strip in range(part // EIGHT):
                sums = None
                for orbital, load in sources:
                    values = load(row, strip)
                    terms = [splats[orbital, i] * values for i in range(held)]
                    sums = terms if sums is None else [a + b for a, b in zip(sums, terms)]
                column = pl.multiple_of(first_column + strip * EIGHT, EIGHT)
                for i in range(held):
                    out[i, row, pl.ds(column, EIGHT), :] = sums[i]
            return carry

        lax.fori_loop(0, rows, body, 0, unroll=2)

    def at(ref, index, offset=0):
        def load(row, strip):
            start = pl.multiple_of(offset + row * part + strip * EIGHT, EIGHT)
            return ref[index, pl.ds(start, EIGHT), :]

        return load

    write([(j, at(block, j)) for j in range(total)], orb * part)
    write([(j, at(block_near, j)) for j in range(total)], (orb ^ 1) * part)
    for share in range(CORES):
        sources = []
        for flip, ref in enumerate((bundle, bundle_near)):
            for j in range(2 * held):
                quad = (core if j // held else orb) ^ flip
                sources.append((quad * held + j % held, at(ref, j, share * length)))
        write(sources, ((1 - chip) * CORES + share) * part)


def apply_all(table, block, basis):
    total, tiles, width = block.shape[0], block.shape[1] // EIGHT, block.shape[2]
    matrix = by_tiles(table, total)
    read, chunk = tile_reader(block), chunk_of(tiles)

    def body(index, carry):
        wide = jnp.concatenate([read(index * chunk + t) for t in range(chunk)], axis=1)
        result = exact_dot(matrix, wide)
        for t in range(chunk):
            piece = result[:, t * width : (t + 1) * width].reshape(total, EIGHT, width)
            basis[:, pl.ds(pl.multiple_of(EIGHT * (index * chunk + t), EIGHT), EIGHT), :] = piece
        return carry

    lax.fori_loop(0, tiles // chunk, body, 0)


def small_call(kernel, out_shape, specs, *args):
    return pl.pallas_call(
        kernel,
        out_shape=out_shape,
        in_specs=specs,
        out_specs=jax.tree.map(lambda _: VMEM, out_shape),
        compiler_params=pltpu.CompilerParams(vmem_limit_bytes=24 * 1024 * 1024),
    )(*args)


def whole(orbitals, potential):
    pair_count, orb_count = lax.axis_size("pair"), lax.axis_size("orb")
    slabs = 2 * pair_count
    side, orb = lax.axis_index("side"), lax.axis_index("orb")
    held, rows, cols, width = orbitals.shape
    kept = held // 2
    part = cols // orb_count

    slant = [(i, (i + (1 if i % 2 else -1)) % slabs) for i in range(slabs)]
    ahead = [(i, (i + (2 if i % 2 else -2)) % slabs) for i in range(slabs)]
    swap = [(0, 1), (1, 0)]
    slab_axes = ("pair", "side")

    group = 2 * orb_count
    me = 2 * orb + side

    def flat_of(index):
        return (index % 2) * orb_count + index // 2

    place = jnp.stack([side, me, orb]).astype(jnp.int32)
    mine, edge, *sent = packed(place, orbitals, potential, orb_count)

    pieces = [
        lax.ppermute(mine, "side", swap),
        lax.ppermute(edge, slab_axes, slant),
        lax.ppermute(edge, slab_axes, ahead),
    ]
    joined = pl.pallas_call(
        join_kernel,
        out_shape=jax.ShapeDtypeStruct((rows + 2 * WIDE, part, width), jnp.float32),
        in_specs=[VMEM] * 3,
        out_specs=VMEM,
        compiler_params=pltpu.CompilerParams(vmem_limit_bytes=16 * 1024 * 1024),
    )(*pieces)
    pot_far = [joined] + [
        lax.ppermute(joined, "orb", [(i, i ^ m) for i in range(orb_count)]) for m in range(1, orb_count)
    ]

    fetched = []
    for at in range(kept):
        fetched.append(
            (
                lax.ppermute(sent[3 * at], slab_axes, slant),
                lax.ppermute(sent[3 * at + 1], "side", swap),
                lax.ppermute(sent[3 * at + 2], slab_axes, ahead),
            )
        )

    early = tuple(sorted((m for m in range(1, group) if m >= 2 * CORES), key=lambda m: (-(m % 2), m)))
    late = tuple(m for m in range(group) if m < 2 * CORES)
    spares = 4 if orb_count == 2 * CORES and kept == 2 else 0

    def to_partner(piece, m):
        if m == 0:
            return piece
        return lax.ppermute(piece, ("side", "orb"), [(flat_of(i), flat_of(i ^ m)) for i in range(group)])

    parts, before = [], []
    for at in range(kept):
        final = at == kept - 1
        outs = filtered_pieces(
            at,
            place,
            orbitals,
            fetched[at],
            potential,
            pot_far,
            group,
            before,
            early,
            late if final else (),
            spares if final else 0,
        )
        parts += [to_partner(piece, m) for piece, m in zip(outs, early)]
        before.append(outs[-1])
    parts += [to_partner(piece, m) for piece, m in zip(outs[len(early) :], late)]
    spare = outs[len(early) + len(late) : -1]
    total, devices = held * orb_count, slabs * orb_count
    cell_total = rows * part * width * devices
    block_shape = jax.ShapeDtypeStruct((total, rows * part, width), jnp.float32)
    message_shape = jax.ShapeDtypeStruct((devices, 1, total * total), jnp.float32)

    def exchanged(message):
        return lax.all_to_all(message, ALL, 0, 0)

    block, message = small_call(
        functools.partial(first_kernel, early, late, kept), [block_shape, message_shape], [SMEM] + [VMEM] * len(parts), place, *parts
    )
    if spares:
        up = [(i, i + CORES) for i in range(CORES)]
        slanted_up = [(s * orb_count + i, (1 - s) * orb_count + i + CORES) for s in range(2) for i in range(CORES)]
        cores = [(i, i ^ 1) for i in range(orb_count)]
        given = [
            spare[0],
            lax.ppermute(spare[1], "side", swap),
            lax.ppermute(spare[2], "orb", up),
            lax.ppermute(spare[3], ("side", "orb"), slanted_up),
        ]
        block_near = lax.ppermute(block, "orb", cores)
        bundle_shape = jax.ShapeDtypeStruct((2 * held, CORES * rows * part, width), jnp.float32)
        table_shape = jax.ShapeDtypeStruct((total, LANES), jnp.float32)
        table, message, bundle = pl.pallas_call(
            functools.partial(second_and_bundle_kernel, cell_total),
            out_shape=[table_shape, message_shape, bundle_shape],
            in_specs=[SMEM] + [VMEM] * (2 + len(given)),
            out_specs=[VMEM] * 3,
            scratch_shapes=[pltpu.VMEM(block_shape.shape, jnp.float32)],
            compiler_params=pltpu.CompilerParams(vmem_limit_bytes=24 * 1024 * 1024),
        )(place, exchanged(message), block, *given)
        bundle_near = lax.ppermute(bundle, "orb", cores)
        return pl.pallas_call(
            functools.partial(last_kernel, cell_total),
            out_shape=jax.ShapeDtypeStruct((held, rows, cols, width), jnp.float32),
            in_specs=[SMEM] + [VMEM] * 6,
            out_specs=VMEM,
            scratch_shapes=[pltpu.VMEM((total, held, EIGHT, width), jnp.float32)],
            compiler_params=pltpu.CompilerParams(vmem_limit_bytes=24 * 1024 * 1024),
        )(place, exchanged(message), table, block, block_near, bundle, bundle_near)
    basis, message = small_call(
        functools.partial(second_kernel, cell_total), [block_shape, message_shape], [VMEM] * 2, exchanged(message), block
    )
    basis = small_call(
        functools.partial(third_kernel, cell_total), block_shape, [VMEM] * 2, exchanged(message), basis
    )
    basis = basis.reshape(total, rows, part, width)
    return lax.all_to_all(basis, "orb", split_axis=0, concat_axis=2, tiled=True)


def solution(mesh):
    slabs, orb_count = mesh.shape["dom"], mesh.shape["orb"]
    fine = Mesh(mesh.devices.reshape(slabs // 2, 2, orb_count), ALL)
    spec = P("orb", ("pair", "side"), None, None)
    return jax.shard_map(
        whole,
        mesh=fine,
        in_specs=(spec, P(("pair", "side"), None, None)),
        out_specs=spec,
        check_vma=False,
    )
```

```python
import functools

import jax
import jax.numpy as jnp
from jax import lax
from jax.experimental import pallas as pl
from jax.experimental.pallas import tpu as pltpu
from jax.sharding import Mesh
from jax.sharding import PartitionSpec as P

coefficients = (-49.0 / 18.0, 1.5, -0.15, 1.0 / 90.0)
spacing = 0.5
filter_centre = 23.0
filter_half = 23.0

REACH = 3
STEPS = 3
DEEP = REACH * STEPS
WIDE = REACH * (STEPS - 1)
EIGHT = 8
CORES = 2
WIDTH = 4
BLOCKS = 3
ALL = ("pair", "side", "orb")

VMEM = pl.BlockSpec(memory_space=pltpu.VMEM)
SMEM = pl.BlockSpec(memory_space=pltpu.SMEM)
HBM = pl.BlockSpec(memory_space=pltpu.HBM)

kinetic = -0.5 / (spacing * spacing)
taps = tuple(kinetic * c / filter_half for c in coefficients)
denominator = 180.0
whole_taps = tuple(round(denominator * c) for c in coefficients)
lane_scale = kinetic / filter_half / denominator
shift = (kinetic * 2.0 * coefficients[0] - filter_centre) / filter_half


def pack_kernel(place, orbitals, potential, *rest):
    outs, sems = rest[:-1], rest[-1]
    side, orb = place[0], place[2]
    kept, rows = orbitals.shape[0] // 2, orbitals.shape[1]
    part = outs[0].shape[1]
    columns = pl.ds(pl.multiple_of(orb * part, part), part)
    edge, shallow = pl.ds(side * (rows - DEEP), DEEP), pl.ds(side * (rows - WIDE), WIDE)
    sources = [potential.at[:, columns], potential.at[shallow, columns]]
    for at in range(kept):
        given, stays = orbitals.at[(1 - side) * kept + at], orbitals.at[side * kept + at]
        sources += [given.at[edge], given, stays.at[edge]]
    copies = [pltpu.make_async_copy(a, b, sems.at[i]) for i, (a, b) in enumerate(zip(sources, outs))]
    for copy in copies:
        copy.start()
    for copy in copies:
        copy.wait()


def packed(place, orbitals, potential, orb_count):
    held, rows, cols, width = orbitals.shape
    part = cols // orb_count
    shapes = [(rows, part, width), (WIDE, part, width)]
    shapes += [(DEEP, cols, width), (rows, cols, width), (DEEP, cols, width)] * (held // 2)
    return pl.pallas_call(
        pack_kernel,
        out_shape=[jax.ShapeDtypeStruct(shape, jnp.float32) for shape in shapes],
        in_specs=[SMEM, HBM, HBM],
        out_specs=[VMEM] * len(shapes),
        scratch_shapes=[pltpu.SemaphoreType.DMA((len(shapes),))],
        compiler_params=pltpu.CompilerParams(vmem_limit_bytes=16 * 1024 * 1024),
    )(place, *(pltpu.with_memory_space_constraint(array, pltpu.HBM) for array in (orbitals, potential)))


def join_kernel(swapped, slanted, straight, out):
    rows = swapped.shape[0]
    out[pl.ds(0, rows)] = swapped[...]
    out[pl.ds(rows, WIDE)] = slanted[...]
    out[pl.ds(rows + WIDE, WIDE)] = straight[...]


def split_dot(values, table):
    high = values.astype(jnp.bfloat16)
    rest = values - high.astype(jnp.float32)
    middle = rest.astype(jnp.bfloat16)
    low = (rest - middle.astype(jnp.float32)).astype(jnp.bfloat16)
    wide = jnp.concatenate([high, middle], axis=1)
    twice = jnp.concatenate([table, table], axis=0)
    return jnp.dot(wide, twice, preferred_element_type=jnp.float32) + jnp.dot(
        low, table, preferred_element_type=jnp.float32
    )


def filter_kernel(at, shares, early, late, place, own, swapped, slanted, straight, own_pot, lane_table, *rest):
    pot_far, before, outs = rest[:shares], rest[shares : shares + at], rest[shares + at : -4]
    field, first, second, weight = rest[-4:]
    outs, sorted_pieces = outs[:-1], outs[-1]
    side, me, orb = place[0], place[1], place[2]
    rows, cols, _ = swapped.shape
    both = 2 * rows
    strips = cols // EIGHT

    def keep(ref, row, strip, value):
        ref[row, pl.ds(EIGHT * (strip + 1), EIGHT), :] = value
        if strip == 0:
            ref[row, pl.ds(cols + EIGHT, EIGHT), :] = value
        if strip == strips - 1:
            ref[row, pl.ds(0, EIGHT), :] = value

    def gather(load, count, row_to):
        def body(row, carry):
            for strip in range(strips):
                keep(field, row_to + row, strip, load(row, pl.ds(EIGHT * strip, EIGHT)))
            return carry

        lax.fori_loop(0, count, body, 0, unroll=3)

    kept = own.shape[0] // 2
    gather(lambda row, span: own[side * kept + at, row, span, :], rows, DEEP + side * rows)
    gather(lambda row, span: swapped[row, span, :], rows, DEEP + (1 - side) * rows)
    gather(lambda row, span: slanted[row, span, :], DEEP, side * (both + DEEP))
    gather(lambda row, span: straight[row, span, :], DEEP, (1 - side) * (both + DEEP))

    def weigh(values):
        return values * (1.0 / filter_half) + shift

    weight[pl.ds(WIDE + side * rows, rows)] = weigh(own_pot[...])
    part = cols // shares
    for apart, far in enumerate(pot_far):
        columns = pl.ds(pl.multiple_of((orb ^ apart) * part, part), part)
        weight[pl.ds(WIDE + (1 - side) * rows, rows), columns] = weigh(far[pl.ds(0, rows)])
        weight[pl.ds(side * (both + WIDE), WIDE), columns] = weigh(far[pl.ds(rows, WIDE)])
        weight[pl.ds((1 - side) * (both + WIDE), WIDE), columns] = weigh(far[pl.ds(rows + WIDE, WIDE)])

    def step(source, before, before_at, weight_at, total, store):
        width = source.shape[2]
        count = total // BLOCKS

        def body(index, carry):
            base = index * count
            centres = source[pl.ds(base + REACH, count), pl.ds(EIGHT, cols), :]
            along = split_dot(centres.reshape(count * cols, width), lane_table[...])
            for strip in range(strips):
                start = EIGHT * (strip + 1)
                window = [source[base + i, pl.ds(start, EIGHT), :] for i in range(count + 2 * REACH)]
                for i in range(count):
                    row = base + i
                    value = window[i + REACH] * weight[weight_at + row, pl.ds(EIGHT * strip, EIGHT), :]
                    from_lanes = i * cols + EIGHT * strip
                    value = value + along[from_lanes : from_lanes + EIGHT] * lane_scale
                    for k in range(1, REACH + 1):
                        near = window[i + REACH - k] + window[i + REACH + k]
                        near = near + (
                            source[row + REACH, pl.ds(start - k, EIGHT), :]
                            + source[row + REACH, pl.ds(start + k, EIGHT), :]
                        )
                        value = value + taps[k] * near
                    if before is not None:
                        value = 2.0 * value - before[before_at + row, pl.ds(start, EIGHT), :]
                    store(row, strip, value)
            return carry

        lax.fori_loop(0, BLOCKS, body, 0)

    step(field, None, 0, 0, both + 2 * WIDE, functools.partial(keep, first))
    step(first, field, 2 * REACH, REACH, both + 2 * REACH, functools.partial(keep, second))
    piece = sorted_pieces.shape[2]

    def store_out(row, strip, value):
        to = (EIGHT * strip) // piece
        half = row // rows
        sorted_pieces[2 * to + half, row - half * rows, pl.ds(EIGHT * strip - to * piece, EIGHT), :] = value

    step(second, first, 2 * REACH, 2 * REACH, both, store_out)
    for apart, out in zip(early, outs):
        out[...] = sorted_pieces[me ^ apart]
    stages = (*before, sorted_pieces)
    for apart, out in zip(late, outs[len(early) :]):
        for stage, pieces in enumerate(stages):
            out[stage] = pieces[me ^ apart]
    for index, out in enumerate(outs[len(early) + len(late) :]):
        chip = orb // CORES ^ (1 if index < 2 else 0)
        slab = side ^ (index % 2)
        for stage, pieces in enumerate(stages):
            for core in range(CORES):
                out[stage, core] = pieces[2 * (CORES * chip + core) + slab]


def filtered_pieces(at, place, own, fetched, own_pot, pot_far, group, before, early, late, spares):
    slanted, swapped, straight = fetched
    rows, cols, width = own.shape[1:]
    both = 2 * rows
    apart = jnp.arange(width)[:, None] - jnp.arange(width)[None, :]
    lane_table = jnp.zeros((width, width), jnp.float32)
    for k, tap in enumerate(whole_taps):
        hit = (apart % width == k) | (-apart % width == k)
        lane_table = jnp.where(hit, float(tap), lane_table)

    def scratch(margin):
        return pltpu.VMEM((both + 2 * margin, cols + 2 * EIGHT, width), jnp.float32)

    piece = (rows, 2 * cols // group, width)
    shapes = [piece] * len(early) + [(at + 1, *piece)] * len(late) + [(at + 1, CORES, *piece)] * spares + [(group, *piece)]
    return pl.pallas_call(
        functools.partial(filter_kernel, at, len(pot_far), early, late),
        out_shape=[jax.ShapeDtypeStruct(shape, jnp.float32) for shape in shapes],
        in_specs=[SMEM] + [VMEM] * (6 + len(pot_far) + at),
        out_specs=[VMEM] * len(shapes),
        scratch_shapes=[
            scratch(DEEP),
            scratch(WIDE),
            scratch(REACH),
            pltpu.VMEM((both + 2 * WIDE, cols, width), jnp.float32),
        ],
        compiler_params=pltpu.CompilerParams(vmem_limit_bytes=24 * 1024 * 1024),
    )(place, own, swapped, slanted, straight, own_pot, lane_table.astype(jnp.bfloat16), *pot_far, *before)


LANES = 128


def exact_dot(a, b, contract=((1,), (0,))):
    return lax.dot_general(
        a, b, (contract, ((), ())), precision=lax.Precision.HIGHEST, preferred_element_type=jnp.float32
    )


def table_of(shape, test):
    rows = lax.broadcasted_iota(jnp.int32, shape, 0)
    columns = lax.broadcasted_iota(jnp.int32, shape, 1)
    return jnp.where(test(rows, columns), 1.0, 0.0).astype(jnp.float32)


def gram_message(read, total, tiles, chunk):
    tall = total * EIGHT

    def body(index, sums):
        wide = jnp.concatenate([read(index * chunk + t) for t in range(chunk)], axis=1)
        return sums + exact_dot(wide, wide, ((1,), (1,)))

    sums = lax.fori_loop(0, tiles // chunk, body, jnp.zeros((tall, tall), jnp.float32))
    sums = sums * table_of((tall, tall), lambda r, c: r % EIGHT == c % EIGHT)
    partial = exact_dot(table_of((total, tall), lambda r, c: c // EIGHT == r), sums)
    spread = exact_dot(partial, table_of((tall, LANES), lambda r, c: r // EIGHT == c % total))
    per = LANES // total
    spread = spread * table_of((total, LANES), lambda r, c: c // total == r % per)
    return jnp.concatenate(
        [jnp.sum(spread[i * per : (i + 1) * per], axis=0, keepdims=True) for i in range(total // per)], axis=1
    )


def inverse_factor(copies, total, cell_total):
    row = jnp.sum(copies[...], axis=0) * (1.0 / cell_total)
    per = LANES // total
    wide = jnp.concatenate(
        [jnp.broadcast_to(row[:, i * LANES : (i + 1) * LANES], (per, LANES)) for i in range(total // per)], axis=0
    )
    wide = wide * table_of((total, LANES), lambda r, c: c // total == r % per)
    table = exact_dot(wide, table_of((LANES, LANES), lambda r, c: r % total == c))
    table = table + table_of((total, LANES), lambda r, c: c - total == r)
    index = lax.broadcasted_iota(jnp.int32, (total, LANES), 0)
    for start in range(0, total, WIDTH):
        block = range(start, min(start + WIDTH, total))
        columns = {j: jnp.broadcast_to(table[:, j : j + 1], (total, LANES)) for j in block}
        rows = {j: table[j : j + 1, :] for j in block}
        reduced = table
        for j in block:
            value = columns[j][j : j + 1, :]
            scale = lax.rsqrt(value)
            scale = scale * (1.5 - 0.5 * value * scale * scale)
            factor, rows[j] = columns[j] * scale, rows[j] * scale
            for later in block:
                if later > j:
                    share = factor[later : later + 1, :]
                    columns[later] = columns[later] - factor * share
                    rows[later] = rows[later] - share * rows[j]
            reduced = reduced - factor * rows[j]
        for j in block:
            table = jnp.where(index == j, rows[j], table)
        table = jnp.where(index > block[-1], reduced, table)
    return table


def by_tiles(table, total):
    tall = total * EIGHT
    wide = exact_dot(table, table_of((LANES, tall), lambda r, c: r - total == c // EIGHT))
    both = exact_dot(table_of((tall, total), lambda r, c: r // EIGHT == c), wide)
    return both * table_of((tall, tall), lambda r, c: r % EIGHT == c % EIGHT)


def tile_reader(ref):
    total, width = ref.shape[0], ref.shape[2]
    return lambda t: ref[:, pl.ds(pl.multiple_of(EIGHT * t, EIGHT), EIGHT), :].reshape(total * EIGHT, width)


def chunk_of(tiles):
    return next(c for c in (6, 4, 3, 2, 1) if tiles % c == 0)


def first_kernel(early, late, kept, place, *refs):
    given, (block, message) = refs[:-2], refs[-2:]
    me, shape = place[1], block.shape[1:]
    for at in range(kept):
        for index, apart in enumerate(early):
            block[(me ^ apart) * kept + at] = given[at * len(early) + index][...].reshape(shape)
        for index, apart in enumerate(late):
            block[(me ^ apart) * kept + at] = given[kept * len(early) + index][at].reshape(shape)
    total, tiles = block.shape[0], block.shape[1] // EIGHT
    row = gram_message(tile_reader(block), total, tiles, chunk_of(tiles))
    message[...] = jnp.broadcast_to(row[None], message.shape)


def second_kernel(cell_total, copies, block, basis, message):
    total, tiles = block.shape[0], block.shape[1] // EIGHT
    apply_all(inverse_factor(copies, total, cell_total), block, basis)
    row = gram_message(tile_reader(basis), total, tiles, chunk_of(tiles))
    message[...] = jnp.broadcast_to(row[None], message.shape)


def third_kernel(cell_total, copies, block, basis):
    apply_all(inverse_factor(copies, block.shape[0], cell_total), block, basis)


def table_kernel(cell_total, copies, block, table_out, message, basis):
    total, tiles = block.shape[0], block.shape[1] // EIGHT
    table = inverse_factor(copies, total, cell_total)
    table_out[...] = table
    apply_all(table, block, basis)
    row = gram_message(tile_reader(basis), total, tiles, chunk_of(tiles))
    message[...] = jnp.broadcast_to(row[None], message.shape)


def bundle_kernel(place, *refs):
    given, bundle = refs[:-1], refs[-1]
    side, kept = place[0], given[0].shape[0]
    for kind, ref in enumerate(given):
        for at in range(kept):
            slot = (kind // 2) * 2 * kept + (side ^ (kind % 2)) * kept + at
            bundle[slot] = ref[at].reshape(bundle.shape[1:])


def last_kernel(cell_total, place, copies, table, block, block_near, bundle, bundle_near, out, splats):
    total, length, width = block.shape
    held, rows = out.shape[:2]
    part = length // rows
    orb = place[2]
    core, chip = orb % CORES, orb // CORES
    second = inverse_factor(copies, total, cell_total)
    pick = table_of((LANES, total), lambda r, c: r - total == c)
    product = exact_dot(exact_dot(second, pick), exact_dot(table[...], pick))
    own = exact_dot(table_of((held * EIGHT, total), lambda r, c: orb * held + r // EIGHT == c), product)
    wide = exact_dot(own, table_of((total, total * width), lambda r, c: c // width == r))
    for orbital in range(total):
        splats[orbital] = wide[:, orbital * width : (orbital + 1) * width].reshape(held, EIGHT, width)

    def write(sources, first_column):
        def body(row, carry):
            for strip in range(part // EIGHT):
                sums = None
                for orbital, load in sources:
                    values = load(row, strip)
                    terms = [splats[orbital, i] * values for i in range(held)]
                    sums = terms if sums is None else [a + b for a, b in zip(sums, terms)]
                column = pl.multiple_of(first_column + strip * EIGHT, EIGHT)
                for i in range(held):
                    out[i, row, pl.ds(column, EIGHT), :] = sums[i]
            return carry

        lax.fori_loop(0, rows, body, 0, unroll=2)

    def at(ref, index, offset=0):
        def load(row, strip):
            start = pl.multiple_of(offset + row * part + strip * EIGHT, EIGHT)
            return ref[index, pl.ds(start, EIGHT), :]

        return load

    write([(j, at(block, j)) for j in range(total)], orb * part)
    write([(j, at(block_near, j)) for j in range(total)], (orb ^ 1) * part)
    for share in range(CORES):
        sources = []
        for flip, ref in enumerate((bundle, bundle_near)):
            for j in range(2 * held):
                quad = (core if j // held else orb) ^ flip
                sources.append((quad * held + j % held, at(ref, j, share * length)))
        write(sources, ((1 - chip) * CORES + share) * part)


def apply_all(table, block, basis):
    total, tiles, width = block.shape[0], block.shape[1] // EIGHT, block.shape[2]
    matrix = by_tiles(table, total)
    read, chunk = tile_reader(block), chunk_of(tiles)

    def body(index, carry):
        wide = jnp.concatenate([read(index * chunk + t) for t in range(chunk)], axis=1)
        result = exact_dot(matrix, wide)
        for t in range(chunk):
            piece = result[:, t * width : (t + 1) * width].reshape(total, EIGHT, width)
            basis[:, pl.ds(pl.multiple_of(EIGHT * (index * chunk + t), EIGHT), EIGHT), :] = piece
        return carry

    lax.fori_loop(0, tiles // chunk, body, 0)


def small_call(kernel, out_shape, specs, *args):
    return pl.pallas_call(
        kernel,
        out_shape=out_shape,
        in_specs=specs,
        out_specs=jax.tree.map(lambda _: VMEM, out_shape),
        compiler_params=pltpu.CompilerParams(vmem_limit_bytes=24 * 1024 * 1024),
    )(*args)


def whole(orbitals, potential):
    pair_count, orb_count = lax.axis_size("pair"), lax.axis_size("orb")
    slabs = 2 * pair_count
    side, orb = lax.axis_index("side"), lax.axis_index("orb")
    held, rows, cols, width = orbitals.shape
    kept = held // 2
    part = cols // orb_count

    slant = [(i, (i + (1 if i % 2 else -1)) % slabs) for i in range(slabs)]
    ahead = [(i, (i + (2 if i % 2 else -2)) % slabs) for i in range(slabs)]
    swap = [(0, 1), (1, 0)]
    slab_axes = ("pair", "side")

    group = 2 * orb_count
    me = 2 * orb + side

    def flat_of(index):
        return (index % 2) * orb_count + index // 2

    place = jnp.stack([side, me, orb]).astype(jnp.int32)
    mine, edge, *sent = packed(place, orbitals, potential, orb_count)

    pieces = [
        lax.ppermute(mine, "side", swap),
        lax.ppermute(edge, slab_axes, slant),
        lax.ppermute(edge, slab_axes, ahead),
    ]
    joined = pl.pallas_call(
        join_kernel,
        out_shape=jax.ShapeDtypeStruct((rows + 2 * WIDE, part, width), jnp.float32),
        in_specs=[VMEM] * 3,
        out_specs=VMEM,
        compiler_params=pltpu.CompilerParams(vmem_limit_bytes=16 * 1024 * 1024),
    )(*pieces)
    pot_far = [joined] + [
        lax.ppermute(joined, "orb", [(i, i ^ m) for i in range(orb_count)]) for m in range(1, orb_count)
    ]

    fetched = []
    for at in range(kept):
        fetched.append(
            (
                lax.ppermute(sent[3 * at], slab_axes, slant),
                lax.ppermute(sent[3 * at + 1], "side", swap),
                lax.ppermute(sent[3 * at + 2], slab_axes, ahead),
            )
        )

    early = tuple(sorted((m for m in range(1, group) if m != CORES), key=lambda m: (m < 2 * CORES, -(m % 2), m)))
    late = (0, CORES)
    spares = 4 if orb_count == 2 * CORES and kept == 2 else 0

    def to_partner(piece, m):
        if m == 0:
            return piece
        return lax.ppermute(piece, ("side", "orb"), [(flat_of(i), flat_of(i ^ m)) for i in range(group)])

    parts, before = [], []
    for at in range(kept):
        final = at == kept - 1
        outs = filtered_pieces(
            at,
            place,
            orbitals,
            fetched[at],
            potential,
            pot_far,
            group,
            before,
            early,
            late if final else (),
            spares if final else 0,
        )
        parts += [to_partner(piece, m) for piece, m in zip(outs, early)]
        before.append(outs[-1])
    parts += [to_partner(piece, m) for piece, m in zip(outs[len(early) :], late)]
    spare = outs[len(early) + len(late) : -1]
    total, devices = held * orb_count, slabs * orb_count
    cell_total = rows * part * width * devices
    block_shape = jax.ShapeDtypeStruct((total, rows * part, width), jnp.float32)
    message_shape = jax.ShapeDtypeStruct((devices, 1, total * total), jnp.float32)

    def exchanged(message):
        return lax.all_to_all(message, ALL, 0, 0)

    block, message = small_call(
        functools.partial(first_kernel, early, late, kept), [block_shape, message_shape], [SMEM] + [VMEM] * len(parts), place, *parts
    )
    if spares:
        up = [(i, i + CORES) for i in range(CORES)]
        slanted_up = [(s * orb_count + i, (1 - s) * orb_count + i + CORES) for s in range(2) for i in range(CORES)]
        cores = [(i, i ^ 1) for i in range(orb_count)]
        given = [
            spare[0],
            lax.ppermute(spare[1], "side", swap),
            lax.ppermute(spare[2], "orb", up),
            lax.ppermute(spare[3], ("side", "orb"), slanted_up),
        ]
        block_near = lax.ppermute(block, "orb", cores)
        bundle_shape = jax.ShapeDtypeStruct((2 * held, CORES * rows * part, width), jnp.float32)
        table_shape = jax.ShapeDtypeStruct((total, LANES), jnp.float32)
        bundle = small_call(bundle_kernel, bundle_shape, [SMEM] + [VMEM] * len(given), place, *given)
        bundle_near = lax.ppermute(bundle, "orb", cores)
        table, message = pl.pallas_call(
            functools.partial(table_kernel, cell_total),
            out_shape=[table_shape, message_shape],
            in_specs=[VMEM] * 2,
            out_specs=[VMEM] * 2,
            scratch_shapes=[pltpu.VMEM(block_shape.shape, jnp.float32)],
            compiler_params=pltpu.CompilerParams(vmem_limit_bytes=24 * 1024 * 1024),
        )(exchanged(message), block)
        return pl.pallas_call(
            functools.partial(last_kernel, cell_total),
            out_shape=jax.ShapeDtypeStruct((held, rows, cols, width), jnp.float32),
            in_specs=[SMEM] + [VMEM] * 6,
            out_specs=VMEM,
            scratch_shapes=[pltpu.VMEM((total, held, EIGHT, width), jnp.float32)],
            compiler_params=pltpu.CompilerParams(vmem_limit_bytes=24 * 1024 * 1024),
        )(place, exchanged(message), table, block, block_near, bundle, bundle_near)
    basis, message = small_call(
        functools.partial(second_kernel, cell_total), [block_shape, message_shape], [VMEM] * 2, exchanged(message), block
    )
    basis = small_call(functools.partial(third_kernel, cell_total), block_shape, [VMEM] * 2, exchanged(message), basis)
    basis = basis.reshape(total, rows, part, width)
    return lax.all_to_all(basis, "orb", split_axis=0, concat_axis=2, tiled=True)


def solution(mesh):
    slabs, orb_count = mesh.shape["dom"], mesh.shape["orb"]
    fine = Mesh(mesh.devices.reshape(slabs // 2, 2, orb_count), ALL)
    spec = P("orb", ("pair", "side"), None, None)
    return jax.shard_map(
        whole,
        mesh=fine,
        in_specs=(spec, P(("pair", "side"), None, None)),
        out_specs=spec,
        check_vma=False,
    )
```

```python
import functools

import jax
import jax.numpy as jnp
from jax import lax
from jax.experimental import pallas as pl
from jax.experimental.pallas import tpu as pltpu
from jax.sharding import Mesh
from jax.sharding import PartitionSpec as P

coefficients = (-49.0 / 18.0, 1.5, -0.15, 1.0 / 90.0)
spacing = 0.5
filter_centre = 23.0
filter_half = 23.0

REACH = 3
STEPS = 3
DEEP = REACH * STEPS
WIDE = REACH * (STEPS - 1)
EIGHT = 8
CORES = 2
WIDTH = 4
BLOCKS = 3
ALL = ("pair", "side", "orb")

VMEM = pl.BlockSpec(memory_space=pltpu.VMEM)
SMEM = pl.BlockSpec(memory_space=pltpu.SMEM)
HBM = pl.BlockSpec(memory_space=pltpu.HBM)

kinetic = -0.5 / (spacing * spacing)
taps = tuple(kinetic * c / filter_half for c in coefficients)
denominator = 180.0
whole_taps = tuple(round(denominator * c) for c in coefficients)
lane_scale = kinetic / filter_half / denominator
shift = (kinetic * 2.0 * coefficients[0] - filter_centre) / filter_half


def pack_kernel(place, orbitals, potential, *rest):
    outs, sems = rest[:-1], rest[-1]
    side, orb = place[0], place[2]
    kept, rows = orbitals.shape[0] // 2, orbitals.shape[1]
    part = outs[0].shape[1]
    columns = pl.ds(pl.multiple_of(orb * part, part), part)
    edge, shallow = pl.ds(side * (rows - DEEP), DEEP), pl.ds(side * (rows - WIDE), WIDE)
    sources = [potential.at[:, columns], potential.at[shallow, columns]]
    for at in range(kept):
        given, stays = orbitals.at[(1 - side) * kept + at], orbitals.at[side * kept + at]
        sources += [given.at[edge], given, stays.at[edge]]
    copies = [pltpu.make_async_copy(a, b, sems.at[i]) for i, (a, b) in enumerate(zip(sources, outs))]
    for copy in copies:
        copy.start()
    for copy in copies:
        copy.wait()


def packed(place, orbitals, potential, orb_count):
    held, rows, cols, width = orbitals.shape
    part = cols // orb_count
    shapes = [(rows, part, width), (WIDE, part, width)]
    shapes += [(DEEP, cols, width), (rows, cols, width), (DEEP, cols, width)] * (held // 2)
    return pl.pallas_call(
        pack_kernel,
        out_shape=[jax.ShapeDtypeStruct(shape, jnp.float32) for shape in shapes],
        in_specs=[SMEM, HBM, HBM],
        out_specs=[VMEM] * len(shapes),
        scratch_shapes=[pltpu.SemaphoreType.DMA((len(shapes),))],
        compiler_params=pltpu.CompilerParams(vmem_limit_bytes=16 * 1024 * 1024),
    )(place, *(pltpu.with_memory_space_constraint(array, pltpu.HBM) for array in (orbitals, potential)))


def join_kernel(swapped, slanted, straight, out):
    rows = swapped.shape[0]
    out[pl.ds(0, rows)] = swapped[...]
    out[pl.ds(rows, WIDE)] = slanted[...]
    out[pl.ds(rows + WIDE, WIDE)] = straight[...]


def split_dot(values, table):
    high = values.astype(jnp.bfloat16)
    rest = values - high.astype(jnp.float32)
    middle = rest.astype(jnp.bfloat16)
    low = (rest - middle.astype(jnp.float32)).astype(jnp.bfloat16)
    wide = jnp.concatenate([high, middle], axis=1)
    twice = jnp.concatenate([table, table], axis=0)
    return jnp.dot(wide, twice, preferred_element_type=jnp.float32) + jnp.dot(
        low, table, preferred_element_type=jnp.float32
    )


def filter_kernel(at, shares, early, late, place, own, swapped, slanted, straight, own_pot, lane_table, *rest):
    pot_far, before, outs = rest[:shares], rest[shares : shares + at], rest[shares + at : -4]
    field, first, second, weight = rest[-4:]
    outs, sorted_pieces = outs[:-1], outs[-1]
    side, me, orb = place[0], place[1], place[2]
    rows, cols, _ = swapped.shape
    both = 2 * rows
    strips = cols // EIGHT

    def keep(ref, row, strip, value):
        ref[row, pl.ds(EIGHT * (strip + 1), EIGHT), :] = value
        if strip == 0:
            ref[row, pl.ds(cols + EIGHT, EIGHT), :] = value
        if strip == strips - 1:
            ref[row, pl.ds(0, EIGHT), :] = value

    def gather(load, count, row_to):
        def body(row, carry):
            for strip in range(strips):
                keep(field, row_to + row, strip, load(row, pl.ds(EIGHT * strip, EIGHT)))
            return carry

        lax.fori_loop(0, count, body, 0, unroll=3)

    kept = own.shape[0] // 2
    gather(lambda row, span: own[side * kept + at, row, span, :], rows, DEEP + side * rows)
    gather(lambda row, span: swapped[row, span, :], rows, DEEP + (1 - side) * rows)
    gather(lambda row, span: slanted[row, span, :], DEEP, side * (both + DEEP))
    gather(lambda row, span: straight[row, span, :], DEEP, (1 - side) * (both + DEEP))

    def weigh(values):
        return values * (1.0 / filter_half) + shift

    weight[pl.ds(WIDE + side * rows, rows)] = weigh(own_pot[...])
    part = cols // shares
    for apart, far in enumerate(pot_far):
        columns = pl.ds(pl.multiple_of((orb ^ apart) * part, part), part)
        weight[pl.ds(WIDE + (1 - side) * rows, rows), columns] = weigh(far[pl.ds(0, rows)])
        weight[pl.ds(side * (both + WIDE), WIDE), columns] = weigh(far[pl.ds(rows, WIDE)])
        weight[pl.ds((1 - side) * (both + WIDE), WIDE), columns] = weigh(far[pl.ds(rows + WIDE, WIDE)])

    def step(source, before, before_at, weight_at, total, store):
        width = source.shape[2]
        count = total // BLOCKS

        def body(index, carry):
            base = index * count
            centres = source[pl.ds(base + REACH, count), pl.ds(EIGHT, cols), :]
            along = split_dot(centres.reshape(count * cols, width), lane_table[...])
            for strip in range(strips):
                start = EIGHT * (strip + 1)
                window = [source[base + i, pl.ds(start, EIGHT), :] for i in range(count + 2 * REACH)]
                for i in range(count):
                    row = base + i
                    value = window[i + REACH] * weight[weight_at + row, pl.ds(EIGHT * strip, EIGHT), :]
                    from_lanes = i * cols + EIGHT * strip
                    value = value + along[from_lanes : from_lanes + EIGHT] * lane_scale
                    for k in range(1, REACH + 1):
                        near = window[i + REACH - k] + window[i + REACH + k]
                        near = near + (
                            source[row + REACH, pl.ds(start - k, EIGHT), :]
                            + source[row + REACH, pl.ds(start + k, EIGHT), :]
                        )
                        value = value + taps[k] * near
                    if before is not None:
                        value = 2.0 * value - before[before_at + row, pl.ds(start, EIGHT), :]
                    store(row, strip, value)
            return carry

        lax.fori_loop(0, BLOCKS, body, 0)

    step(field, None, 0, 0, both + 2 * WIDE, functools.partial(keep, first))
    step(first, field, 2 * REACH, REACH, both + 2 * REACH, functools.partial(keep, second))
    piece = sorted_pieces.shape[2]

    def store_out(row, strip, value):
        to = (EIGHT * strip) // piece
        half = row // rows
        sorted_pieces[2 * to + half, row - half * rows, pl.ds(EIGHT * strip - to * piece, EIGHT), :] = value

    step(second, first, 2 * REACH, 2 * REACH, both, store_out)
    for apart, out in zip(early, outs):
        out[...] = sorted_pieces[me ^ apart]
    stages = (*before, sorted_pieces)
    for apart, out in zip(late, outs[len(early) :]):
        for stage, pieces in enumerate(stages):
            out[stage] = pieces[me ^ apart]
    for index, out in enumerate(outs[len(early) + len(late) :]):
        chip = orb // CORES ^ (1 if index < 2 else 0)
        slab = side ^ (index % 2)
        for stage, pieces in enumerate(stages):
            for core in range(CORES):
                out[stage, core] = pieces[2 * (CORES * chip + core) + slab]


def filtered_pieces(at, place, own, fetched, own_pot, pot_far, group, before, early, late, spares):
    slanted, swapped, straight = fetched
    rows, cols, width = own.shape[1:]
    both = 2 * rows
    apart = jnp.arange(width)[:, None] - jnp.arange(width)[None, :]
    lane_table = jnp.zeros((width, width), jnp.float32)
    for k, tap in enumerate(whole_taps):
        hit = (apart % width == k) | (-apart % width == k)
        lane_table = jnp.where(hit, float(tap), lane_table)

    def scratch(margin):
        return pltpu.VMEM((both + 2 * margin, cols + 2 * EIGHT, width), jnp.float32)

    piece = (rows, 2 * cols // group, width)
    shapes = [piece] * len(early) + [(at + 1, *piece)] * len(late) + [(at + 1, CORES, *piece)] * spares + [(group, *piece)]
    return pl.pallas_call(
        functools.partial(filter_kernel, at, len(pot_far), early, late),
        out_shape=[jax.ShapeDtypeStruct(shape, jnp.float32) for shape in shapes],
        in_specs=[SMEM] + [VMEM] * (6 + len(pot_far) + at),
        out_specs=[VMEM] * len(shapes),
        scratch_shapes=[
            scratch(DEEP),
            scratch(WIDE),
            scratch(REACH),
            pltpu.VMEM((both + 2 * WIDE, cols, width), jnp.float32),
        ],
        compiler_params=pltpu.CompilerParams(vmem_limit_bytes=24 * 1024 * 1024),
    )(place, own, swapped, slanted, straight, own_pot, lane_table.astype(jnp.bfloat16), *pot_far, *before)


LANES = 128


def exact_dot(a, b, contract=((1,), (0,))):
    return lax.dot_general(
        a, b, (contract, ((), ())), precision=lax.Precision.HIGHEST, preferred_element_type=jnp.float32
    )


def table_of(shape, test):
    rows = lax.broadcasted_iota(jnp.int32, shape, 0)
    columns = lax.broadcasted_iota(jnp.int32, shape, 1)
    return jnp.where(test(rows, columns), 1.0, 0.0).astype(jnp.float32)


def split(values):
    high = values.astype(jnp.bfloat16)
    rest = values - high.astype(jnp.float32)
    middle = rest.astype(jnp.bfloat16)
    return high, middle, (rest - middle.astype(jnp.float32)).astype(jnp.bfloat16)


def product(a, b, contract=((1,), (0,))):
    return lax.dot_general(a, b, (contract, ((), ())), preferred_element_type=jnp.float32)


def gram_message(wide, total):
    tall = total * EIGHT
    high, middle, low = split(wide)
    joined, doubled = jnp.concatenate([high, middle], axis=1), jnp.concatenate([high, high], axis=1)
    mixed = product(doubled, jnp.concatenate([middle, low], axis=1), ((1,), (1,)))
    sums = product(joined, joined, ((1,), (1,))) + (mixed + mixed.T)
    sums = sums * table_of((tall, tall), lambda r, c: r % EIGHT == c % EIGHT)
    partial = exact_dot(table_of((total, tall), lambda r, c: c // EIGHT == r), sums)
    spread = exact_dot(partial, table_of((tall, LANES), lambda r, c: r // EIGHT == c % total))
    per = LANES // total
    spread = spread * table_of((total, LANES), lambda r, c: c // total == r % per)
    return jnp.concatenate(
        [jnp.sum(spread[i * per : (i + 1) * per], axis=0, keepdims=True) for i in range(total // per)], axis=1
    )


def inverse_factor(copies, total, cell_total):
    row = jnp.sum(copies[...], axis=0) * (1.0 / cell_total)
    per = LANES // total
    wide = jnp.concatenate(
        [jnp.broadcast_to(row[:, i * LANES : (i + 1) * LANES], (per, LANES)) for i in range(total // per)], axis=0
    )
    wide = wide * table_of((total, LANES), lambda r, c: c // total == r % per)
    table = exact_dot(wide, table_of((LANES, LANES), lambda r, c: r % total == c))
    table = table + table_of((total, LANES), lambda r, c: c - total == r)
    index = lax.broadcasted_iota(jnp.int32, (total, LANES), 0)
    for start in range(0, total, WIDTH):
        block = range(start, min(start + WIDTH, total))
        columns = {j: jnp.broadcast_to(table[:, j : j + 1], (total, LANES)) for j in block}
        rows = {j: table[j : j + 1, :] for j in block}
        reduced = table
        for j in block:
            value = columns[j][j : j + 1, :]
            scale = lax.rsqrt(value)
            scale = scale * (1.5 - 0.5 * value * scale * scale)
            factor, rows[j] = columns[j] * scale, rows[j] * scale
            for later in block:
                if later > j:
                    share = factor[later : later + 1, :]
                    columns[later] = columns[later] - factor * share
                    rows[later] = rows[later] - share * rows[j]
            reduced = reduced - factor * rows[j]
        for j in block:
            table = jnp.where(index == j, rows[j], table)
        table = jnp.where(index > block[-1], reduced, table)
    return table


def by_tiles(table, total):
    tall = total * EIGHT
    wide = exact_dot(table, table_of((LANES, tall), lambda r, c: r - total == c // EIGHT))
    both = exact_dot(table_of((tall, total), lambda r, c: r // EIGHT == c), wide)
    return both * table_of((tall, tall), lambda r, c: r % EIGHT == c % EIGHT)


def side_by_side(ref):
    total, length, width = ref.shape
    tiles = [ref[:, start : start + EIGHT, :].reshape(total * EIGHT, width) for start in range(0, length, EIGHT)]
    return jnp.concatenate(tiles, axis=1)


def first_kernel(early, late, kept, place, *refs):
    given, (block, message) = refs[:-2], refs[-2:]
    me, shape = place[1], block.shape[1:]
    for at in range(kept):
        for index, apart in enumerate(early):
            block[(me ^ apart) * kept + at] = given[at * len(early) + index][...].reshape(shape)
        for index, apart in enumerate(late):
            block[(me ^ apart) * kept + at] = given[kept * len(early) + index][at].reshape(shape)
    message[...] = jnp.broadcast_to(gram_message(side_by_side(block), block.shape[0])[None], message.shape)


def applied(table, block):
    total = block.shape[0]
    tall = total * EIGHT
    high, middle, low = split(by_tiles(table, total))
    values_high, values_middle, values_low = split(side_by_side(block))
    left = jnp.concatenate(
        [jnp.concatenate([high, high], axis=1), jnp.concatenate([middle, middle], axis=1)], axis=0
    )
    main = product(left, jnp.concatenate([values_high, values_middle], axis=0))
    rest = product(jnp.concatenate([low, high], axis=1), jnp.concatenate([values_high, values_low], axis=0))
    return main[:tall] + (main[tall:] + rest)


def put(wide, basis):
    total, length, width = basis.shape
    for t in range(length // EIGHT):
        piece = wide[:, t * width : (t + 1) * width].reshape(total, EIGHT, width)
        basis[:, EIGHT * t : EIGHT * (t + 1), :] = piece


def second_kernel(cell_total, copies, block, basis, message):
    total = block.shape[0]
    wide = applied(inverse_factor(copies, total, cell_total), block)
    put(wide, basis)
    message[...] = jnp.broadcast_to(gram_message(wide, total)[None], message.shape)


def third_kernel(cell_total, copies, block, basis):
    put(applied(inverse_factor(copies, block.shape[0], cell_total), block), basis)


def table_kernel(cell_total, copies, block, table_out, message):
    total = block.shape[0]
    table = inverse_factor(copies, total, cell_total)
    table_out[...] = table
    message[...] = jnp.broadcast_to(gram_message(applied(table, block), total)[None], message.shape)


def last_kernel(cell_total, place, copies, table, block, block_near, *refs):
    spares, (out, splats) = refs[:-2], refs[-2:]
    total, length, width = block.shape
    held, rows = out.shape[:2]
    part = length // rows
    side, orb = place[0], place[2]
    core, chip = orb % CORES, orb // CORES
    second = inverse_factor(copies, total, cell_total)
    pick = table_of((LANES, total), lambda r, c: r - total == c)
    product = exact_dot(exact_dot(second, pick), exact_dot(table[...], pick))
    own = exact_dot(table_of((held * EIGHT, total), lambda r, c: orb * held + r // EIGHT == c), product)
    wide = exact_dot(own, table_of((total, total * width), lambda r, c: c // width == r))
    for orbital in range(total):
        splats[orbital] = wide[:, orbital * width : (orbital + 1) * width].reshape(held, EIGHT, width)

    def write(sources, first_column):
        def body(row, carry):
            for strip in range(part // EIGHT):
                sums = None
                for orbital, load in sources:
                    values = load(row, strip)
                    terms = [splats[orbital, i] * values for i in range(held)]
                    sums = terms if sums is None else [a + b for a, b in zip(sums, terms)]
                column = pl.multiple_of(first_column + strip * EIGHT, EIGHT)
                for i in range(held):
                    out[i, row, pl.ds(column, EIGHT), :] = sums[i]
            return carry

        lax.fori_loop(0, rows, body, 0, unroll=2)

    def at(ref, index):
        def load(row, strip):
            return ref[index, pl.ds(pl.multiple_of(row * part + strip * EIGHT, EIGHT), EIGHT), :]

        return load

    write([(j, at(block, j)) for j in range(total)], orb * part)
    write([(j, at(block_near, j)) for j in range(total)], (orb ^ 1) * part)

    def spare_at(ref, stage, share):
        return lambda row, strip: ref[stage, share, row, pl.ds(strip * EIGHT, EIGHT), :]

    kinds = len(spares) // 2
    for share in range(CORES):
        sources = []
        for index, ref in enumerate(spares):
            flip, kind = index // kinds, index % kinds
            quad = (core if kind // 2 else orb) ^ flip
            for stage in range(ref.shape[0]):
                orbital = quad * held + (side ^ (kind % 2)) * ref.shape[0] + stage
                sources.append((orbital, spare_at(ref, stage, share)))
        write(sources, ((1 - chip) * CORES + share) * part)


def small_call(kernel, out_shape, specs, *args):
    return pl.pallas_call(
        kernel,
        out_shape=out_shape,
        in_specs=specs,
        out_specs=jax.tree.map(lambda _: VMEM, out_shape),
        compiler_params=pltpu.CompilerParams(vmem_limit_bytes=24 * 1024 * 1024),
    )(*args)


def whole(orbitals, potential):
    pair_count, orb_count = lax.axis_size("pair"), lax.axis_size("orb")
    slabs = 2 * pair_count
    side, orb = lax.axis_index("side"), lax.axis_index("orb")
    held, rows, cols, width = orbitals.shape
    kept = held // 2
    part = cols // orb_count

    slant = [(i, (i + (1 if i % 2 else -1)) % slabs) for i in range(slabs)]
    ahead = [(i, (i + (2 if i % 2 else -2)) % slabs) for i in range(slabs)]
    swap = [(0, 1), (1, 0)]
    slab_axes = ("pair", "side")

    group = 2 * orb_count
    me = 2 * orb + side

    def flat_of(index):
        return (index % 2) * orb_count + index // 2

    place = jnp.stack([side, me, orb]).astype(jnp.int32)
    mine, edge, *sent = packed(place, orbitals, potential, orb_count)

    pieces = [
        lax.ppermute(mine, "side", swap),
        lax.ppermute(edge, slab_axes, slant),
        lax.ppermute(edge, slab_axes, ahead),
    ]
    joined = pl.pallas_call(
        join_kernel,
        out_shape=jax.ShapeDtypeStruct((rows + 2 * WIDE, part, width), jnp.float32),
        in_specs=[VMEM] * 3,
        out_specs=VMEM,
        compiler_params=pltpu.CompilerParams(vmem_limit_bytes=16 * 1024 * 1024),
    )(*pieces)
    pot_far = [joined] + [
        lax.ppermute(joined, "orb", [(i, i ^ m) for i in range(orb_count)]) for m in range(1, orb_count)
    ]

    fetched = []
    for at in range(kept):
        fetched.append(
            (
                lax.ppermute(sent[3 * at], slab_axes, slant),
                lax.ppermute(sent[3 * at + 1], "side", swap),
                lax.ppermute(sent[3 * at + 2], slab_axes, ahead),
            )
        )

    early = tuple(sorted((m for m in range(1, group) if m != CORES), key=lambda m: (m < 2 * CORES, -(m % 2), m)))
    late = (0, CORES)
    spares = 4 if orb_count == 2 * CORES and kept == 2 else 0

    def to_partner(piece, m):
        if m == 0:
            return piece
        return lax.ppermute(piece, ("side", "orb"), [(flat_of(i), flat_of(i ^ m)) for i in range(group)])

    parts, before = [], []
    for at in range(kept):
        final = at == kept - 1
        outs = filtered_pieces(
            at,
            place,
            orbitals,
            fetched[at],
            potential,
            pot_far,
            group,
            before,
            early,
            late if final else (),
            spares if final else 0,
        )
        parts += [to_partner(piece, m) for piece, m in zip(outs, early)]
        before.append(outs[-1])
    parts += [to_partner(piece, m) for piece, m in zip(outs[len(early) :], late)]
    spare = outs[len(early) + len(late) : -1]
    total, devices = held * orb_count, slabs * orb_count
    cell_total = rows * part * width * devices
    block_shape = jax.ShapeDtypeStruct((total, rows * part, width), jnp.float32)
    message_shape = jax.ShapeDtypeStruct((devices, 1, total * total), jnp.float32)

    def exchanged(message):
        return lax.all_to_all(message, ALL, 0, 0)

    block, message = small_call(
        functools.partial(first_kernel, early, late, kept),
        [block_shape, message_shape],
        [SMEM] + [VMEM] * len(parts),
        *(place, *parts),
    )
    if spares:
        up = [(i, i + CORES) for i in range(CORES)]
        slanted_up = [(s * orb_count + i, (1 - s) * orb_count + i + CORES) for s in range(2) for i in range(CORES)]
        cores = [(i, i ^ 1) for i in range(orb_count)]
        given = [
            spare[0],
            lax.ppermute(spare[1], "side", swap),
            lax.ppermute(spare[2], "orb", up),
            lax.ppermute(spare[3], ("side", "orb"), slanted_up),
        ]
        block_near = lax.ppermute(block, "orb", cores)
        table_shape = jax.ShapeDtypeStruct((total, LANES), jnp.float32)
        given += [lax.ppermute(piece, "orb", cores) for piece in given]
        table, message = pl.pallas_call(
            functools.partial(table_kernel, cell_total),
            out_shape=[table_shape, message_shape],
            in_specs=[VMEM] * 2,
            out_specs=[VMEM] * 2,
            compiler_params=pltpu.CompilerParams(vmem_limit_bytes=24 * 1024 * 1024),
        )(exchanged(message), block)
        return pl.pallas_call(
            functools.partial(last_kernel, cell_total),
            out_shape=jax.ShapeDtypeStruct((held, rows, cols, width), jnp.float32),
            in_specs=[SMEM] + [VMEM] * (4 + len(given)),
            out_specs=VMEM,
            scratch_shapes=[pltpu.VMEM((total, held, EIGHT, width), jnp.float32)],
            compiler_params=pltpu.CompilerParams(vmem_limit_bytes=24 * 1024 * 1024),
        )(place, exchanged(message), table, block, block_near, *given)
    basis, message = small_call(
        functools.partial(second_kernel, cell_total), [block_shape, message_shape], [VMEM] * 2, exchanged(message), block
    )
    basis = small_call(functools.partial(third_kernel, cell_total), block_shape, [VMEM] * 2, exchanged(message), basis)
    basis = basis.reshape(total, rows, part, width)
    return lax.all_to_all(basis, "orb", split_axis=0, concat_axis=2, tiled=True)


def solution(mesh):
    slabs, orb_count = mesh.shape["dom"], mesh.shape["orb"]
    fine = Mesh(mesh.devices.reshape(slabs // 2, 2, orb_count), ALL)
    spec = P("orb", ("pair", "side"), None, None)
    return jax.shard_map(
        whole,
        mesh=fine,
        in_specs=(spec, P(("pair", "side"), None, None)),
        out_specs=spec,
        check_vma=False,
    )
```

```python
import functools

import jax
import jax.numpy as jnp
from jax import lax
from jax.experimental import pallas as pl
from jax.experimental.pallas import tpu as pltpu
from jax.sharding import Mesh
from jax.sharding import PartitionSpec as P

coefficients = (-49.0 / 18.0, 1.5, -0.15, 1.0 / 90.0)
spacing = 0.5
filter_centre = 23.0
filter_half = 23.0

REACH = 3
STEPS = 3
DEEP = REACH * STEPS
WIDE = REACH * (STEPS - 1)
EIGHT = 8
CORES = 2
WIDTH = 4
BLOCKS = 3
ALL = ("pair", "side", "orb")

VMEM = pl.BlockSpec(memory_space=pltpu.VMEM)
SMEM = pl.BlockSpec(memory_space=pltpu.SMEM)
HBM = pl.BlockSpec(memory_space=pltpu.HBM)

kinetic = -0.5 / (spacing * spacing)
taps = tuple(kinetic * c / filter_half for c in coefficients)
denominator = 180.0
whole_taps = tuple(round(denominator * c) for c in coefficients)
lane_scale = kinetic / filter_half / denominator
shift = (kinetic * 2.0 * coefficients[0] - filter_centre) / filter_half


def pack_kernel(place, orbitals, potential, *rest):
    outs, sems = rest[:-1], rest[-1]
    side, orb = place[0], place[2]
    kept, rows = orbitals.shape[0] // 2, orbitals.shape[1]
    part = outs[0].shape[1]
    columns = pl.ds(pl.multiple_of(orb * part, part), part)
    edge, shallow = pl.ds(side * (rows - DEEP), DEEP), pl.ds(side * (rows - WIDE), WIDE)
    sources = [potential.at[:, columns], potential.at[shallow, columns]]
    for at in range(kept):
        given, stays = orbitals.at[(1 - side) * kept + at], orbitals.at[side * kept + at]
        sources += [given.at[edge], given, stays.at[edge]]
    copies = [pltpu.make_async_copy(a, b, sems.at[i]) for i, (a, b) in enumerate(zip(sources, outs))]
    for copy in copies:
        copy.start()
    for copy in copies:
        copy.wait()


def packed(place, orbitals, potential, orb_count):
    held, rows, cols, width = orbitals.shape
    part = cols // orb_count
    shapes = [(rows, part, width), (WIDE, part, width)]
    shapes += [(DEEP, cols, width), (rows, cols, width), (DEEP, cols, width)] * (held // 2)
    return pl.pallas_call(
        pack_kernel,
        out_shape=[jax.ShapeDtypeStruct(shape, jnp.float32) for shape in shapes],
        in_specs=[SMEM, HBM, HBM],
        out_specs=[VMEM] * len(shapes),
        scratch_shapes=[pltpu.SemaphoreType.DMA((len(shapes),))],
        compiler_params=pltpu.CompilerParams(vmem_limit_bytes=16 * 1024 * 1024),
    )(place, *(pltpu.with_memory_space_constraint(array, pltpu.HBM) for array in (orbitals, potential)))


def join_kernel(swapped, slanted, straight, out):
    rows = swapped.shape[0]
    out[pl.ds(0, rows)] = swapped[...]
    out[pl.ds(rows, WIDE)] = slanted[...]
    out[pl.ds(rows + WIDE, WIDE)] = straight[...]


def split_dot(values, table):
    high = values.astype(jnp.bfloat16)
    rest = values - high.astype(jnp.float32)
    middle = rest.astype(jnp.bfloat16)
    low = (rest - middle.astype(jnp.float32)).astype(jnp.bfloat16)
    wide = jnp.concatenate([high, middle], axis=1)
    twice = jnp.concatenate([table, table], axis=0)
    return jnp.dot(wide, twice, preferred_element_type=jnp.float32) + jnp.dot(
        low, table, preferred_element_type=jnp.float32
    )


def filter_kernel(at, shares, early, late, place, own, swapped, slanted, straight, own_pot, lane_table, *rest):
    pot_far, before, outs = rest[:shares], rest[shares : shares + at], rest[shares + at : -4]
    field, first, second, weight = rest[-4:]
    outs, sorted_pieces = outs[:-1], outs[-1]
    side, me, orb = place[0], place[1], place[2]
    rows, cols, _ = swapped.shape
    both = 2 * rows
    strips = cols // EIGHT

    def keep(ref, row, strip, value):
        ref[row, pl.ds(EIGHT * (strip + 1), EIGHT), :] = value
        if strip == 0:
            ref[row, pl.ds(cols + EIGHT, EIGHT), :] = value
        if strip == strips - 1:
            ref[row, pl.ds(0, EIGHT), :] = value

    def gather(load, count, row_to):
        def body(row, carry):
            for strip in range(strips):
                keep(field, row_to + row, strip, load(row, pl.ds(EIGHT * strip, EIGHT)))
            return carry

        lax.fori_loop(0, count, body, 0, unroll=3)

    kept = own.shape[0] // 2
    gather(lambda row, span: own[side * kept + at, row, span, :], rows, DEEP + side * rows)
    gather(lambda row, span: swapped[row, span, :], rows, DEEP + (1 - side) * rows)
    gather(lambda row, span: slanted[row, span, :], DEEP, side * (both + DEEP))
    gather(lambda row, span: straight[row, span, :], DEEP, (1 - side) * (both + DEEP))

    def weigh(values):
        return values * (1.0 / filter_half) + shift

    weight[pl.ds(WIDE + side * rows, rows)] = weigh(own_pot[...])
    part = cols // shares
    for apart, far in enumerate(pot_far):
        columns = pl.ds(pl.multiple_of((orb ^ apart) * part, part), part)
        weight[pl.ds(WIDE + (1 - side) * rows, rows), columns] = weigh(far[pl.ds(0, rows)])
        weight[pl.ds(side * (both + WIDE), WIDE), columns] = weigh(far[pl.ds(rows, WIDE)])
        weight[pl.ds((1 - side) * (both + WIDE), WIDE), columns] = weigh(far[pl.ds(rows + WIDE, WIDE)])

    def step(source, before, before_at, weight_at, total, store):
        width = source.shape[2]
        count = total // BLOCKS

        def body(index, carry):
            base = index * count
            centres = source[pl.ds(base + REACH, count), pl.ds(EIGHT, cols), :]
            along = split_dot(centres.reshape(count * cols, width), lane_table[...])
            for strip in range(strips):
                start = EIGHT * (strip + 1)
                window = [source[base + i, pl.ds(start, EIGHT), :] for i in range(count + 2 * REACH)]
                for i in range(count):
                    row = base + i
                    value = window[i + REACH] * weight[weight_at + row, pl.ds(EIGHT * strip, EIGHT), :]
                    from_lanes = i * cols + EIGHT * strip
                    value = value + along[from_lanes : from_lanes + EIGHT] * lane_scale
                    for k in range(1, REACH + 1):
                        near = window[i + REACH - k] + window[i + REACH + k]
                        near = near + (
                            source[row + REACH, pl.ds(start - k, EIGHT), :]
                            + source[row + REACH, pl.ds(start + k, EIGHT), :]
                        )
                        value = value + taps[k] * near
                    if before is not None:
                        value = 2.0 * value - before[before_at + row, pl.ds(start, EIGHT), :]
                    store(row, strip, value)
            return carry

        lax.fori_loop(0, BLOCKS, body, 0)

    step(field, None, 0, 0, both + 2 * WIDE, functools.partial(keep, first))
    step(first, field, 2 * REACH, REACH, both + 2 * REACH, functools.partial(keep, second))
    piece = sorted_pieces.shape[2]

    def store_out(row, strip, value):
        to = (EIGHT * strip) // piece
        half = row // rows
        sorted_pieces[2 * to + half, row - half * rows, pl.ds(EIGHT * strip - to * piece, EIGHT), :] = value

    step(second, first, 2 * REACH, 2 * REACH, both, store_out)
    for apart, out in zip(early, outs):
        out[...] = sorted_pieces[me ^ apart]
    stages = (*before, sorted_pieces)
    for apart, out in zip(late, outs[len(early) :]):
        for stage, pieces in enumerate(stages):
            out[stage] = pieces[me ^ apart]
    for index, out in enumerate(outs[len(early) + len(late) :]):
        chip = orb // CORES ^ (1 if index < 2 else 0)
        slab = side ^ (index % 2)
        for stage, pieces in enumerate(stages):
            for core in range(CORES):
                out[stage, core] = pieces[2 * (CORES * chip + core) + slab]


def filtered_pieces(at, place, own, fetched, own_pot, pot_far, group, before, early, late, spares):
    slanted, swapped, straight = fetched
    rows, cols, width = own.shape[1:]
    both = 2 * rows
    apart = jnp.arange(width)[:, None] - jnp.arange(width)[None, :]
    lane_table = jnp.zeros((width, width), jnp.float32)
    for k, tap in enumerate(whole_taps):
        hit = (apart % width == k) | (-apart % width == k)
        lane_table = jnp.where(hit, float(tap), lane_table)

    def scratch(margin):
        return pltpu.VMEM((both + 2 * margin, cols + 2 * EIGHT, width), jnp.float32)

    piece = (rows, 2 * cols // group, width)
    shapes = [piece] * len(early) + [(at + 1, *piece)] * len(late) + [(at + 1, CORES, *piece)] * spares + [(group, *piece)]
    return pl.pallas_call(
        functools.partial(filter_kernel, at, len(pot_far), early, late),
        out_shape=[jax.ShapeDtypeStruct(shape, jnp.float32) for shape in shapes],
        in_specs=[SMEM] + [VMEM] * (6 + len(pot_far) + at),
        out_specs=[VMEM] * len(shapes),
        scratch_shapes=[
            scratch(DEEP),
            scratch(WIDE),
            scratch(REACH),
            pltpu.VMEM((both + 2 * WIDE, cols, width), jnp.float32),
        ],
        compiler_params=pltpu.CompilerParams(vmem_limit_bytes=24 * 1024 * 1024),
    )(place, own, swapped, slanted, straight, own_pot, lane_table.astype(jnp.bfloat16), *pot_far, *before)


LANES = 128


def exact_dot(a, b, contract=((1,), (0,))):
    return lax.dot_general(
        a, b, (contract, ((), ())), precision=lax.Precision.HIGHEST, preferred_element_type=jnp.float32
    )


def table_of(shape, test):
    rows = lax.broadcasted_iota(jnp.int32, shape, 0)
    columns = lax.broadcasted_iota(jnp.int32, shape, 1)
    return jnp.where(test(rows, columns), 1.0, 0.0).astype(jnp.float32)


def split(values):
    high = values.astype(jnp.bfloat16)
    rest = values - high.astype(jnp.float32)
    middle = rest.astype(jnp.bfloat16)
    return high, middle, (rest - middle.astype(jnp.float32)).astype(jnp.bfloat16)


def product(a, b, contract=((1,), (0,))):
    return lax.dot_general(a, b, (contract, ((), ())), preferred_element_type=jnp.float32)


def gram_message(wide, total):
    tall = total * EIGHT
    high, middle, low = split(wide)
    joined, doubled = jnp.concatenate([high, middle], axis=1), jnp.concatenate([high, high], axis=1)
    mixed = product(doubled, jnp.concatenate([middle, low], axis=1), ((1,), (1,)))
    sums = product(joined, joined, ((1,), (1,))) + (mixed + mixed.T)
    sums = sums * table_of((tall, tall), lambda r, c: r % EIGHT == c % EIGHT)
    partial = exact_dot(table_of((total, tall), lambda r, c: c // EIGHT == r), sums)
    spread = exact_dot(partial, table_of((tall, LANES), lambda r, c: r // EIGHT == c % total))
    per = LANES // total
    spread = spread * table_of((total, LANES), lambda r, c: c // total == r % per)
    return jnp.concatenate(
        [jnp.sum(spread[i * per : (i + 1) * per], axis=0, keepdims=True) for i in range(total // per)], axis=1
    )


def inverse_factor(copies, total, cell_total):
    row = jnp.sum(copies[...], axis=0) * (1.0 / cell_total)
    per = LANES // total
    wide = jnp.concatenate(
        [jnp.broadcast_to(row[:, i * LANES : (i + 1) * LANES], (per, LANES)) for i in range(total // per)], axis=0
    )
    wide = wide * table_of((total, LANES), lambda r, c: c // total == r % per)
    table = exact_dot(wide, table_of((LANES, LANES), lambda r, c: r % total == c))
    table = table + table_of((total, LANES), lambda r, c: c - total == r)
    index = lax.broadcasted_iota(jnp.int32, (total, LANES), 0)
    for start in range(0, total, WIDTH):
        block = range(start, min(start + WIDTH, total))
        columns = {j: jnp.broadcast_to(table[:, j : j + 1], (total, LANES)) for j in block}
        rows = {j: table[j : j + 1, :] for j in block}
        reduced = table
        for j in block:
            value = columns[j][j : j + 1, :]
            scale = lax.rsqrt(value)
            scale = scale * (1.5 - 0.5 * value * scale * scale)
            factor, rows[j] = columns[j] * scale, rows[j] * scale
            for later in block:
                if later > j:
                    share = factor[later : later + 1, :]
                    columns[later] = columns[later] - factor * share
                    rows[later] = rows[later] - share * rows[j]
            reduced = reduced - factor * rows[j]
        for j in block:
            table = jnp.where(index == j, rows[j], table)
        table = jnp.where(index > block[-1], reduced, table)
    return table


def by_tiles(table, total):
    tall = total * EIGHT
    wide = exact_dot(table, table_of((LANES, tall), lambda r, c: r - total == c // EIGHT))
    both = exact_dot(table_of((tall, total), lambda r, c: r // EIGHT == c), wide)
    return both * table_of((tall, tall), lambda r, c: r % EIGHT == c % EIGHT)


def side_by_side(ref):
    total, length, width = ref.shape
    tiles = [ref[:, start : start + EIGHT, :].reshape(total * EIGHT, width) for start in range(0, length, EIGHT)]
    return jnp.concatenate(tiles, axis=1)


def first_kernel(early, late, kept, place, *refs):
    given, (block, message) = refs[:-2], refs[-2:]
    me, shape = place[1], block.shape[1:]
    for at in range(kept):
        for index, apart in enumerate(early):
            block[(me ^ apart) * kept + at] = given[at * len(early) + index][...].reshape(shape)
        for index, apart in enumerate(late):
            block[(me ^ apart) * kept + at] = given[kept * len(early) + index][at].reshape(shape)
    message[...] = jnp.broadcast_to(gram_message(side_by_side(block), block.shape[0])[None], message.shape)


def applied(table, block):
    total = block.shape[0]
    tall = total * EIGHT
    high, middle, low = split(by_tiles(table, total))
    values_high, values_middle, values_low = split(side_by_side(block))
    left = jnp.concatenate(
        [jnp.concatenate([high, high], axis=1), jnp.concatenate([middle, middle], axis=1)], axis=0
    )
    main = product(left, jnp.concatenate([values_high, values_middle], axis=0))
    rest = product(jnp.concatenate([low, high], axis=1), jnp.concatenate([values_high, values_low], axis=0))
    return main[:tall] + (main[tall:] + rest)


def put(wide, basis):
    total, length, width = basis.shape
    for t in range(length // EIGHT):
        piece = wide[:, t * width : (t + 1) * width].reshape(total, EIGHT, width)
        basis[:, EIGHT * t : EIGHT * (t + 1), :] = piece


def second_kernel(cell_total, copies, block, basis, message):
    total = block.shape[0]
    wide = applied(inverse_factor(copies, total, cell_total), block)
    put(wide, basis)
    message[...] = jnp.broadcast_to(gram_message(wide, total)[None], message.shape)


def third_kernel(cell_total, copies, block, basis):
    put(applied(inverse_factor(copies, block.shape[0], cell_total), block), basis)


def table_kernel(cell_total, copies, block, table_out, message):
    total = block.shape[0]
    table = inverse_factor(copies, total, cell_total)
    table_out[...] = table
    message[...] = jnp.broadcast_to(gram_message(applied(table, block), total)[None], message.shape)


def last_kernel(cell_total, place, copies, table, block, block_near, *refs):
    spares, (out, splats) = refs[:-2], refs[-2:]
    total, length, width = block.shape
    held, rows = out.shape[:2]
    part = length // rows
    side, orb = place[0], place[2]
    core, chip = orb % CORES, orb // CORES
    second = inverse_factor(copies, total, cell_total)
    pick = table_of((LANES, total), lambda r, c: r - total == c)
    product = exact_dot(exact_dot(second, pick), exact_dot(table[...], pick))
    own = exact_dot(table_of((held * EIGHT, total), lambda r, c: orb * held + r // EIGHT == c), product)
    wide = exact_dot(own, table_of((total, total * width), lambda r, c: c // width == r))
    for orbital in range(total):
        splats[orbital] = wide[:, orbital * width : (orbital + 1) * width].reshape(held, EIGHT, width)

    def write(sources, first_column):
        def body(row, carry):
            for strip in range(part // EIGHT):
                sums = None
                for orbital, load in sources:
                    values = load(row, strip)
                    terms = [splats[orbital, i] * values for i in range(held)]
                    sums = terms if sums is None else [a + b for a, b in zip(sums, terms)]
                column = pl.multiple_of(first_column + strip * EIGHT, EIGHT)
                for i in range(held):
                    out[i, row, pl.ds(column, EIGHT), :] = sums[i]
            return carry

        lax.fori_loop(0, rows, body, 0, unroll=2)

    def at(ref, index):
        def load(row, strip):
            return ref[index, pl.ds(pl.multiple_of(row * part + strip * EIGHT, EIGHT), EIGHT), :]

        return load

    write([(j, at(block, j)) for j in range(total)], orb * part)
    write([(j, at(block_near, j)) for j in range(total)], (orb ^ 1) * part)

    def spare_at(ref, stage, share):
        return lambda row, strip: ref[stage, share, row, pl.ds(strip * EIGHT, EIGHT), :]

    kinds = len(spares) // 2
    for share in range(CORES):
        sources = []
        for index, ref in enumerate(spares):
            flip, kind = index // kinds, index % kinds
            quad = (core if kind // 2 else orb) ^ flip
            for stage in range(ref.shape[0]):
                orbital = quad * held + (side ^ (kind % 2)) * ref.shape[0] + stage
                sources.append((orbital, spare_at(ref, stage, share)))
        write(sources, ((1 - chip) * CORES + share) * part)


def small_call(kernel, out_shape, specs, *args):
    return pl.pallas_call(
        kernel,
        out_shape=out_shape,
        in_specs=specs,
        out_specs=jax.tree.map(lambda _: VMEM, out_shape),
        compiler_params=pltpu.CompilerParams(vmem_limit_bytes=24 * 1024 * 1024),
    )(*args)


def whole(orbitals, potential):
    pair_count, orb_count = lax.axis_size("pair"), lax.axis_size("orb")
    slabs = 2 * pair_count
    side, orb = lax.axis_index("side"), lax.axis_index("orb")
    held, rows, cols, width = orbitals.shape
    kept = held // 2
    part = cols // orb_count

    slant = [(i, (i + (1 if i % 2 else -1)) % slabs) for i in range(slabs)]
    ahead = [(i, (i + (2 if i % 2 else -2)) % slabs) for i in range(slabs)]
    swap = [(0, 1), (1, 0)]
    slab_axes = ("pair", "side")

    group = 2 * orb_count
    me = 2 * orb + side

    def flat_of(index):
        return (index % 2) * orb_count + index // 2

    place = jnp.stack([side, me, orb]).astype(jnp.int32)
    mine, edge, *sent = packed(place, orbitals, potential, orb_count)

    pieces = [
        lax.ppermute(mine, "side", swap),
        lax.ppermute(edge, slab_axes, slant),
        lax.ppermute(edge, slab_axes, ahead),
    ]
    joined = pl.pallas_call(
        join_kernel,
        out_shape=jax.ShapeDtypeStruct((rows + 2 * WIDE, part, width), jnp.float32),
        in_specs=[VMEM] * 3,
        out_specs=VMEM,
        compiler_params=pltpu.CompilerParams(vmem_limit_bytes=16 * 1024 * 1024),
    )(*pieces)
    pot_far = [joined] + [
        lax.ppermute(joined, "orb", [(i, i ^ m) for i in range(orb_count)]) for m in range(1, orb_count)
    ]

    fetched = []
    for at in range(kept):
        fetched.append(
            (
                lax.ppermute(sent[3 * at], slab_axes, slant),
                lax.ppermute(sent[3 * at + 1], "side", swap),
                lax.ppermute(sent[3 * at + 2], slab_axes, ahead),
            )
        )

    early = tuple(sorted((m for m in range(1, group) if m != CORES), key=lambda m: (m < 2 * CORES, -(m % 2), m)))
    late = (0, CORES)
    spares = 4 if orb_count == 2 * CORES and kept == 2 else 0

    def to_partner(piece, m):
        if m == 0:
            return piece
        return lax.ppermute(piece, ("side", "orb"), [(flat_of(i), flat_of(i ^ m)) for i in range(group)])

    parts, before = [], []
    for at in range(kept):
        final = at == kept - 1
        outs = filtered_pieces(
            at,
            place,
            orbitals,
            fetched[at],
            potential,
            pot_far,
            group,
            before,
            early,
            late if final else (),
            spares if final else 0,
        )
        parts += [to_partner(piece, m) for piece, m in zip(outs, early)]
        before.append(outs[-1])
    parts += [to_partner(piece, m) for piece, m in zip(outs[len(early) :], late)]
    spare = outs[len(early) + len(late) : -1]
    total, devices = held * orb_count, slabs * orb_count
    cell_total = rows * part * width * devices
    block_shape = jax.ShapeDtypeStruct((total, rows * part, width), jnp.float32)
    message_shape = jax.ShapeDtypeStruct((devices, 1, total * total), jnp.float32)

    def exchanged(message):
        return lax.all_to_all(message, ALL, 0, 0)

    block, message = small_call(
        functools.partial(first_kernel, early, late, kept),
        [block_shape, message_shape],
        [SMEM] + [VMEM] * len(parts),
        *(place, *parts),
    )
    if spares:
        up = [(i, i + CORES) for i in range(CORES)]
        slanted_up = [(s * orb_count + i, (1 - s) * orb_count + i + CORES) for s in range(2) for i in range(CORES)]
        cores = [(i, i ^ 1) for i in range(orb_count)]
        given = [
            spare[0],
            lax.ppermute(spare[1], "side", swap),
            lax.ppermute(spare[2], "orb", up),
        ]
        given.append(lax.ppermute(spare[3], ("side", "orb"), slanted_up))
        block_near = lax.ppermute(block, "orb", cores)
        table_shape = jax.ShapeDtypeStruct((total, LANES), jnp.float32)
        near = [lax.ppermute(piece, "orb", cores) for piece in given[:-1]]
        given = given + near + [lax.ppermute(given[-1], "orb", cores)]
        copies = exchanged(message)
        table, message = small_call(
            functools.partial(table_kernel, cell_total), [table_shape, message_shape], [VMEM] * 2, copies, block
        )
        return pl.pallas_call(
            functools.partial(last_kernel, cell_total),
            out_shape=jax.ShapeDtypeStruct((held, rows, cols, width), jnp.float32),
            in_specs=[SMEM] + [VMEM] * (4 + len(given)),
            out_specs=VMEM,
            scratch_shapes=[pltpu.VMEM((total, held, EIGHT, width), jnp.float32)],
            compiler_params=pltpu.CompilerParams(vmem_limit_bytes=24 * 1024 * 1024),
        )(place, exchanged(message), table, block, block_near, *given)
    basis, message = small_call(
        functools.partial(second_kernel, cell_total), [block_shape, message_shape], [VMEM] * 2, exchanged(message), block
    )
    basis = small_call(functools.partial(third_kernel, cell_total), block_shape, [VMEM] * 2, exchanged(message), basis)
    basis = basis.reshape(total, rows, part, width)
    return lax.all_to_all(basis, "orb", split_axis=0, concat_axis=2, tiled=True)


def solution(mesh):
    slabs, orb_count = mesh.shape["dom"], mesh.shape["orb"]
    fine = Mesh(mesh.devices.reshape(slabs // 2, 2, orb_count), ALL)
    spec = P("orb", ("pair", "side"), None, None)
    return jax.shard_map(
        whole,
        mesh=fine,
        in_specs=(spec, P(("pair", "side"), None, None)),
        out_specs=spec,
        check_vma=False,
    )
```

```python
import functools

import jax
import jax.numpy as jnp
from jax import lax
from jax.experimental import pallas as pl
from jax.experimental.pallas import tpu as pltpu
from jax.sharding import Mesh
from jax.sharding import PartitionSpec as P

coefficients = (-49.0 / 18.0, 1.5, -0.15, 1.0 / 90.0)
spacing = 0.5
filter_centre = 23.0
filter_half = 23.0

REACH = 3
STEPS = 3
DEEP = REACH * STEPS
WIDE = REACH * (STEPS - 1)
EIGHT = 8
CORES = 2
WIDTH = 4
BLOCKS = 3
ALL = ("pair", "side", "orb")

VMEM = pl.BlockSpec(memory_space=pltpu.VMEM)
SMEM = pl.BlockSpec(memory_space=pltpu.SMEM)
HBM = pl.BlockSpec(memory_space=pltpu.HBM)

kinetic = -0.5 / (spacing * spacing)
taps = tuple(kinetic * c / filter_half for c in coefficients)
denominator = 180.0
whole_taps = tuple(round(denominator * c) for c in coefficients)
lane_scale = kinetic / filter_half / denominator
shift = (kinetic * 2.0 * coefficients[0] - filter_centre) / filter_half


def pack_kernel(place, orbitals, potential, *rest):
    outs, sems = rest[:-1], rest[-1]
    side, orb = place[0], place[2]
    kept, rows = orbitals.shape[0] // 2, orbitals.shape[1]
    part = outs[0].shape[1]
    columns = pl.ds(pl.multiple_of(orb * part, part), part)
    edge, shallow = pl.ds(side * (rows - DEEP), DEEP), pl.ds(side * (rows - WIDE), WIDE)
    sources = [potential.at[:, columns], potential.at[shallow, columns]]
    for at in range(kept):
        given, stays = orbitals.at[(1 - side) * kept + at], orbitals.at[side * kept + at]
        sources += [given.at[edge], given, stays.at[edge]]
    copies = [pltpu.make_async_copy(a, b, sems.at[i]) for i, (a, b) in enumerate(zip(sources, outs))]
    for copy in copies:
        copy.start()
    for copy in copies:
        copy.wait()


def packed(place, orbitals, potential, orb_count):
    held, rows, cols, width = orbitals.shape
    part = cols // orb_count
    shapes = [(rows, part, width), (WIDE, part, width)]
    shapes += [(DEEP, cols, width), (rows, cols, width), (DEEP, cols, width)] * (held // 2)
    return pl.pallas_call(
        pack_kernel,
        out_shape=[jax.ShapeDtypeStruct(shape, jnp.float32) for shape in shapes],
        in_specs=[SMEM, HBM, HBM],
        out_specs=[VMEM] * len(shapes),
        scratch_shapes=[pltpu.SemaphoreType.DMA((len(shapes),))],
        compiler_params=pltpu.CompilerParams(vmem_limit_bytes=16 * 1024 * 1024),
    )(place, *(pltpu.with_memory_space_constraint(array, pltpu.HBM) for array in (orbitals, potential)))


def join_kernel(swapped, slanted, straight, out):
    rows = swapped.shape[0]
    out[pl.ds(0, rows)] = swapped[...]
    out[pl.ds(rows, WIDE)] = slanted[...]
    out[pl.ds(rows + WIDE, WIDE)] = straight[...]


def split_dot(values, table):
    high = values.astype(jnp.bfloat16)
    rest = values - high.astype(jnp.float32)
    middle = rest.astype(jnp.bfloat16)
    low = (rest - middle.astype(jnp.float32)).astype(jnp.bfloat16)
    wide = jnp.concatenate([high, middle], axis=1)
    twice = jnp.concatenate([table, table], axis=0)
    return jnp.dot(wide, twice, preferred_element_type=jnp.float32) + jnp.dot(
        low, table, preferred_element_type=jnp.float32
    )


def filter_kernel(at, shares, early, late, place, own, swapped, slanted, straight, own_pot, lane_table, *rest):
    pot_far, before, outs = rest[:shares], rest[shares : shares + at], rest[shares + at : -4]
    field, first, second, weight = rest[-4:]
    outs, sorted_pieces = outs[:-1], outs[-1]
    side, me, orb = place[0], place[1], place[2]
    rows, cols, _ = swapped.shape
    both = 2 * rows
    strips = cols // EIGHT

    def keep(ref, row, strip, value):
        ref[row, pl.ds(EIGHT * (strip + 1), EIGHT), :] = value
        if strip == 0:
            ref[row, pl.ds(cols + EIGHT, EIGHT), :] = value
        if strip == strips - 1:
            ref[row, pl.ds(0, EIGHT), :] = value

    def gather(load, count, row_to):
        def body(row, carry):
            for strip in range(strips):
                keep(field, row_to + row, strip, load(row, pl.ds(EIGHT * strip, EIGHT)))
            return carry

        lax.fori_loop(0, count, body, 0, unroll=3)

    kept = own.shape[0] // 2
    gather(lambda row, span: own[side * kept + at, row, span, :], rows, DEEP + side * rows)
    gather(lambda row, span: swapped[row, span, :], rows, DEEP + (1 - side) * rows)
    gather(lambda row, span: slanted[row, span, :], DEEP, side * (both + DEEP))
    gather(lambda row, span: straight[row, span, :], DEEP, (1 - side) * (both + DEEP))

    def weigh(values):
        return values * (1.0 / filter_half) + shift

    weight[pl.ds(WIDE + side * rows, rows)] = weigh(own_pot[...])
    part = cols // shares
    for apart, far in enumerate(pot_far):
        columns = pl.ds(pl.multiple_of((orb ^ apart) * part, part), part)
        weight[pl.ds(WIDE + (1 - side) * rows, rows), columns] = weigh(far[pl.ds(0, rows)])
        weight[pl.ds(side * (both + WIDE), WIDE), columns] = weigh(far[pl.ds(rows, WIDE)])
        weight[pl.ds((1 - side) * (both + WIDE), WIDE), columns] = weigh(far[pl.ds(rows + WIDE, WIDE)])

    def step(source, before, before_at, weight_at, total, store):
        width = source.shape[2]
        count = total // BLOCKS

        def body(index, carry):
            base = index * count
            centres = source[pl.ds(base + REACH, count), pl.ds(EIGHT, cols), :]
            along = split_dot(centres.reshape(count * cols, width), lane_table[...])
            for strip in range(strips):
                start = EIGHT * (strip + 1)
                window = [source[base + i, pl.ds(start, EIGHT), :] for i in range(count + 2 * REACH)]
                for i in range(count):
                    row = base + i
                    value = window[i + REACH] * weight[weight_at + row, pl.ds(EIGHT * strip, EIGHT), :]
                    from_lanes = i * cols + EIGHT * strip
                    value = value + along[from_lanes : from_lanes + EIGHT] * lane_scale
                    for k in range(1, REACH + 1):
                        near = window[i + REACH - k] + window[i + REACH + k]
                        near = near + (
                            source[row + REACH, pl.ds(start - k, EIGHT), :]
                            + source[row + REACH, pl.ds(start + k, EIGHT), :]
                        )
                        value = value + taps[k] * near
                    if before is not None:
                        value = 2.0 * value - before[before_at + row, pl.ds(start, EIGHT), :]
                    store(row, strip, value)
            return carry

        lax.fori_loop(0, BLOCKS, body, 0)

    step(field, None, 0, 0, both + 2 * WIDE, functools.partial(keep, first))
    step(first, field, 2 * REACH, REACH, both + 2 * REACH, functools.partial(keep, second))
    piece = sorted_pieces.shape[2]

    def store_out(row, strip, value):
        to = (EIGHT * strip) // piece
        half = row // rows
        sorted_pieces[2 * to + half, row - half * rows, pl.ds(EIGHT * strip - to * piece, EIGHT), :] = value

    step(second, first, 2 * REACH, 2 * REACH, both, store_out)
    for apart, out in zip(early, outs):
        out[...] = sorted_pieces[me ^ apart]
    stages = (*before, sorted_pieces)
    for apart, out in zip(late, outs[len(early) :]):
        for stage, pieces in enumerate(stages):
            out[stage] = pieces[me ^ apart]
    for index, out in enumerate(outs[len(early) + len(late) :]):
        chip = orb // CORES ^ (1 if index < 2 else 0)
        slab = side ^ (index % 2)
        for stage, pieces in enumerate(stages):
            for core in range(CORES):
                out[stage, core] = pieces[2 * (CORES * chip + core) + slab]


def filtered_pieces(at, place, own, fetched, own_pot, pot_far, group, before, early, late, spares):
    slanted, swapped, straight = fetched
    rows, cols, width = own.shape[1:]
    both = 2 * rows
    apart = jnp.arange(width)[:, None] - jnp.arange(width)[None, :]
    lane_table = jnp.zeros((width, width), jnp.float32)
    for k, tap in enumerate(whole_taps):
        hit = (apart % width == k) | (-apart % width == k)
        lane_table = jnp.where(hit, float(tap), lane_table)

    def scratch(margin):
        return pltpu.VMEM((both + 2 * margin, cols + 2 * EIGHT, width), jnp.float32)

    piece = (rows, 2 * cols // group, width)
    shapes = [piece] * len(early) + [(at + 1, *piece)] * len(late) + [(at + 1, CORES, *piece)] * spares + [(group, *piece)]
    return pl.pallas_call(
        functools.partial(filter_kernel, at, len(pot_far), early, late),
        out_shape=[jax.ShapeDtypeStruct(shape, jnp.float32) for shape in shapes],
        in_specs=[SMEM] + [VMEM] * (6 + len(pot_far) + at),
        out_specs=[VMEM] * len(shapes),
        scratch_shapes=[
            scratch(DEEP),
            scratch(WIDE),
            scratch(REACH),
            pltpu.VMEM((both + 2 * WIDE, cols, width), jnp.float32),
        ],
        compiler_params=pltpu.CompilerParams(vmem_limit_bytes=24 * 1024 * 1024),
    )(place, own, swapped, slanted, straight, own_pot, lane_table.astype(jnp.bfloat16), *pot_far, *before)


LANES = 128


def exact_dot(a, b, contract=((1,), (0,))):
    return lax.dot_general(
        a, b, (contract, ((), ())), precision=lax.Precision.HIGHEST, preferred_element_type=jnp.float32
    )


def table_of(shape, test):
    rows = lax.broadcasted_iota(jnp.int32, shape, 0)
    columns = lax.broadcasted_iota(jnp.int32, shape, 1)
    return jnp.where(test(rows, columns), 1.0, 0.0).astype(jnp.float32)


def split(values):
    high = values.astype(jnp.bfloat16)
    rest = values - high.astype(jnp.float32)
    middle = rest.astype(jnp.bfloat16)
    return high, middle, (rest - middle.astype(jnp.float32)).astype(jnp.bfloat16)


def product(a, b, contract=((1,), (0,))):
    return lax.dot_general(a, b, (contract, ((), ())), preferred_element_type=jnp.float32)


def gram_message(wide, total):
    tall = total * EIGHT
    high, middle, low = split(wide)
    joined, doubled = jnp.concatenate([high, middle], axis=1), jnp.concatenate([high, high], axis=1)
    mixed = product(doubled, jnp.concatenate([middle, low], axis=1), ((1,), (1,)))
    sums = product(joined, joined, ((1,), (1,))) + (mixed + mixed.T)
    sums = sums * table_of((tall, tall), lambda r, c: r % EIGHT == c % EIGHT)
    partial = exact_dot(table_of((total, tall), lambda r, c: c // EIGHT == r), sums)
    spread = exact_dot(partial, table_of((tall, LANES), lambda r, c: r // EIGHT == c % total))
    per = LANES // total
    spread = spread * table_of((total, LANES), lambda r, c: c // total == r % per)
    return jnp.concatenate(
        [jnp.sum(spread[i * per : (i + 1) * per], axis=0, keepdims=True) for i in range(total // per)], axis=1
    )


def inverse_factor(copies, total, cell_total):
    row = jnp.sum(copies[...], axis=0) * (1.0 / cell_total)
    per = LANES // total
    wide = jnp.concatenate(
        [jnp.broadcast_to(row[:, i * LANES : (i + 1) * LANES], (per, LANES)) for i in range(total // per)], axis=0
    )
    wide = wide * table_of((total, LANES), lambda r, c: c // total == r % per)
    table = exact_dot(wide, table_of((LANES, LANES), lambda r, c: r % total == c))
    table = table + table_of((total, LANES), lambda r, c: c - total == r)
    index = lax.broadcasted_iota(jnp.int32, (total, LANES), 0)
    for start in range(0, total, WIDTH):
        block = range(start, min(start + WIDTH, total))
        columns = {j: jnp.broadcast_to(table[:, j : j + 1], (total, LANES)) for j in block}
        rows = {j: table[j : j + 1, :] for j in block}
        reduced = table
        for j in block:
            value = columns[j][j : j + 1, :]
            scale = lax.rsqrt(value)
            scale = scale * (1.5 - 0.5 * value * scale * scale)
            factor, rows[j] = columns[j] * scale, rows[j] * scale
            for later in block:
                if later > j:
                    share = factor[later : later + 1, :]
                    columns[later] = columns[later] - factor * share
                    rows[later] = rows[later] - share * rows[j]
            reduced = reduced - factor * rows[j]
        for j in block:
            table = jnp.where(index == j, rows[j], table)
        table = jnp.where(index > block[-1], reduced, table)
    return table


def by_tiles(table, total):
    tall = total * EIGHT
    wide = exact_dot(table, table_of((LANES, tall), lambda r, c: r - total == c // EIGHT))
    both = exact_dot(table_of((tall, total), lambda r, c: r // EIGHT == c), wide)
    return both * table_of((tall, tall), lambda r, c: r % EIGHT == c % EIGHT)


def side_by_side(ref):
    total, length, width = ref.shape
    tiles = [ref[:, start : start + EIGHT, :].reshape(total * EIGHT, width) for start in range(0, length, EIGHT)]
    return jnp.concatenate(tiles, axis=1)


def first_kernel(early, late, kept, place, *refs):
    given, (block, message) = refs[:-2], refs[-2:]
    me, shape = place[1], block.shape[1:]
    for at in range(kept):
        for index, apart in enumerate(early):
            block[(me ^ apart) * kept + at] = given[at * len(early) + index][...].reshape(shape)
        for index, apart in enumerate(late):
            block[(me ^ apart) * kept + at] = given[kept * len(early) + index][at].reshape(shape)
    message[...] = jnp.broadcast_to(gram_message(side_by_side(block), block.shape[0])[None], message.shape)


def applied(table, block):
    total = block.shape[0]
    tall = total * EIGHT
    high, middle, low = split(by_tiles(table, total))
    values_high, values_middle, values_low = split(side_by_side(block))
    left = jnp.concatenate(
        [jnp.concatenate([high, high], axis=1), jnp.concatenate([middle, middle], axis=1)], axis=0
    )
    main = product(left, jnp.concatenate([values_high, values_middle], axis=0))
    rest = product(jnp.concatenate([low, high], axis=1), jnp.concatenate([values_high, values_low], axis=0))
    return main[:tall] + (main[tall:] + rest)


def put(wide, basis):
    total, length, width = basis.shape
    for t in range(length // EIGHT):
        piece = wide[:, t * width : (t + 1) * width].reshape(total, EIGHT, width)
        basis[:, EIGHT * t : EIGHT * (t + 1), :] = piece


def second_kernel(cell_total, copies, block, basis, message):
    total = block.shape[0]
    wide = applied(inverse_factor(copies, total, cell_total), block)
    put(wide, basis)
    message[...] = jnp.broadcast_to(gram_message(wide, total)[None], message.shape)


def third_kernel(cell_total, copies, block, basis):
    put(applied(inverse_factor(copies, block.shape[0], cell_total), block), basis)


def table_kernel(cell_total, copies, block, table_out, message_far, message, sem):
    total = block.shape[0]
    table = inverse_factor(copies, total, cell_total)
    table_out[...] = table
    message[...] = jnp.broadcast_to(gram_message(applied(table, block), total)[None], message.shape)
    leave = pltpu.make_async_copy(message, message_far, sem)
    leave.start()
    leave.wait()


def last_kernel(cell_total, place, copies, table, block, block_near, *refs):
    count = (len(refs) - 5) // 2
    far, (out_far, splats, out), spares = refs[:count], refs[count : count + 3], refs[count + 3 : 2 * count + 3]
    sems, sems_out = refs[2 * count + 3 :]
    total, length, width = block.shape
    held, rows = out.shape[:2]
    part = length // rows
    side, orb = place[0], place[2]
    chip = orb // CORES
    fetches = [pltpu.make_async_copy(a, b, sems.at[i]) for i, (a, b) in enumerate(zip(far, spares))]
    for fetch in fetches:
        fetch.start()
    second = inverse_factor(copies, total, cell_total)
    pick = table_of((LANES, total), lambda r, c: r - total == c)
    product = exact_dot(exact_dot(second, pick), exact_dot(table[...], pick))
    own = exact_dot(table_of((held * EIGHT, total), lambda r, c: orb * held + r // EIGHT == c), product)
    wide = exact_dot(own, table_of((total, total * width), lambda r, c: c // width == r))
    for orbital in range(total):
        splats[orbital] = wide[:, orbital * width : (orbital + 1) * width].reshape(held, EIGHT, width)

    def write(sources, first_column):
        def body(row, carry):
            for strip in range(part // EIGHT):
                sums = None
                for orbital, load in sources:
                    values = load(row, strip)
                    terms = [splats[orbital, i] * values for i in range(held)]
                    sums = terms if sums is None else [a + b for a, b in zip(sums, terms)]
                column = pl.multiple_of(first_column + strip * EIGHT, EIGHT)
                for i in range(held):
                    out[i, row, pl.ds(column, EIGHT), :] = sums[i]
            return carry

        lax.fori_loop(0, rows, body, 0, unroll=2)

    def at(ref, index):
        def load(row, strip):
            return ref[index, pl.ds(pl.multiple_of(row * part + strip * EIGHT, EIGHT), EIGHT), :]

        return load

    write([(j, at(block, j)) for j in range(total)], orb * part)
    write([(j, at(block_near, j)) for j in range(total)], (orb ^ 1) * part)

    def leave(which, index):
        columns = pl.ds(pl.multiple_of(which * CORES * part, EIGHT), CORES * part)
        return pltpu.make_async_copy(out.at[:, :, columns], out_far.at[:, :, columns], sems_out.at[index])

    leave(chip, 0).start()
    for fetch in fetches:
        fetch.wait()

    def spare_at(ref, stage, share):
        return lambda row, strip: ref[stage, share, row, pl.ds(strip * EIGHT, EIGHT), :]

    kinds = len(spares) // 2
    for share in range(CORES):
        sources = []
        for index, ref in enumerate(spares):
            flip, kind = index // kinds, index % kinds
            quad = (orb ^ CORES if kind // 2 else orb) ^ flip
            for stage in range(ref.shape[0]):
                orbital = quad * held + (side ^ (kind % 2)) * ref.shape[0] + stage
                sources.append((orbital, spare_at(ref, stage, share)))
        write(sources, ((1 - chip) * CORES + share) * part)
    leave(1 - chip, 1).start()
    leave(chip, 0).wait()
    leave(1 - chip, 1).wait()


def small_call(kernel, out_shape, specs, *args):
    return pl.pallas_call(
        kernel,
        out_shape=out_shape,
        in_specs=specs,
        out_specs=jax.tree.map(lambda _: VMEM, out_shape),
        compiler_params=pltpu.CompilerParams(vmem_limit_bytes=24 * 1024 * 1024),
    )(*args)


def whole(orbitals, potential):
    pair_count, orb_count = lax.axis_size("pair"), lax.axis_size("orb")
    slabs = 2 * pair_count
    side, orb = lax.axis_index("side"), lax.axis_index("orb")
    held, rows, cols, width = orbitals.shape
    kept = held // 2
    part = cols // orb_count

    slant = [(i, (i + (1 if i % 2 else -1)) % slabs) for i in range(slabs)]
    ahead = [(i, (i + (2 if i % 2 else -2)) % slabs) for i in range(slabs)]
    swap = [(0, 1), (1, 0)]
    slab_axes = ("pair", "side")

    group = 2 * orb_count
    me = 2 * orb + side

    def flat_of(index):
        return (index % 2) * orb_count + index // 2

    place = jnp.stack([side, me, orb]).astype(jnp.int32)
    mine, edge, *sent = packed(place, orbitals, potential, orb_count)

    pieces = [
        lax.ppermute(mine, "side", swap),
        lax.ppermute(edge, slab_axes, slant),
        lax.ppermute(edge, slab_axes, ahead),
    ]
    joined = pl.pallas_call(
        join_kernel,
        out_shape=jax.ShapeDtypeStruct((rows + 2 * WIDE, part, width), jnp.float32),
        in_specs=[VMEM] * 3,
        out_specs=VMEM,
        compiler_params=pltpu.CompilerParams(vmem_limit_bytes=16 * 1024 * 1024),
    )(*pieces)
    pot_far = [joined] + [
        lax.ppermute(joined, "orb", [(i, i ^ m) for i in range(orb_count)]) for m in range(1, orb_count)
    ]

    fetched = []
    for at in range(kept):
        fetched.append(
            (
                lax.ppermute(sent[3 * at], slab_axes, slant),
                lax.ppermute(sent[3 * at + 1], "side", swap),
                lax.ppermute(sent[3 * at + 2], slab_axes, ahead),
            )
        )

    early = tuple(sorted((m for m in range(1, group) if m != CORES), key=lambda m: (m < 2 * CORES, -(m % 2), m)))
    late = (0, CORES)
    spares = 4 if orb_count == 2 * CORES and kept == 2 else 0

    def to_partner(piece, m):
        if m == 0:
            return piece
        return lax.ppermute(piece, ("side", "orb"), [(flat_of(i), flat_of(i ^ m)) for i in range(group)])

    parts, before = [], []
    for at in range(kept):
        final = at == kept - 1
        outs = filtered_pieces(
            at,
            place,
            orbitals,
            fetched[at],
            potential,
            pot_far,
            group,
            before,
            early,
            late if final else (),
            spares if final else 0,
        )
        parts += [to_partner(piece, m) for piece, m in zip(outs, early)]
        before.append(outs[-1])
    parts += [to_partner(piece, m) for piece, m in zip(outs[len(early) :], late)]
    spare = outs[len(early) + len(late) : -1]
    total, devices = held * orb_count, slabs * orb_count
    cell_total = rows * part * width * devices
    block_shape = jax.ShapeDtypeStruct((total, rows * part, width), jnp.float32)
    message_shape = jax.ShapeDtypeStruct((devices, 1, total * total), jnp.float32)

    def exchanged(message):
        return lax.all_to_all(message, ALL, 0, 0)

    block, message = small_call(
        functools.partial(first_kernel, early, late, kept),
        [block_shape, message_shape],
        [SMEM] + [VMEM] * len(parts),
        *(place, *parts),
    )
    if spares:
        across = [(i, i ^ CORES) for i in range(orb_count)]
        slanted_across = [(t * orb_count + i, (1 - t) * orb_count + (i ^ CORES)) for t in range(2) for i in range(orb_count)]
        cores = [(i, i ^ 1) for i in range(orb_count)]
        given = [
            spare[0],
            lax.ppermute(spare[1], "side", swap),
            lax.ppermute(spare[2], "orb", across),
        ]
        given.append(lax.ppermute(spare[3], ("side", "orb"), slanted_across))
        block_near = lax.ppermute(block, "orb", cores)
        table_shape = jax.ShapeDtypeStruct((total, LANES), jnp.float32)
        near = [lax.ppermute(piece, "orb", cores) for piece in given[:-1]]
        given = given + near + [lax.ppermute(given[-1], "orb", cores)]
        copies = exchanged(message)
        table, message = pl.pallas_call(
            functools.partial(table_kernel, cell_total),
            out_shape=[table_shape, message_shape],
            in_specs=[VMEM] * 2,
            out_specs=[VMEM, HBM],
            scratch_shapes=[pltpu.VMEM(message_shape.shape, jnp.float32), pltpu.SemaphoreType.DMA],
            compiler_params=pltpu.CompilerParams(vmem_limit_bytes=24 * 1024 * 1024),
        )(copies, block)
        return pl.pallas_call(
            functools.partial(last_kernel, cell_total),
            out_shape=jax.ShapeDtypeStruct((held, rows, cols, width), jnp.float32),
            in_specs=[SMEM] + [VMEM] * 4 + [HBM] * len(given),
            out_specs=HBM,
            scratch_shapes=[
                pltpu.VMEM((total, held, EIGHT, width), jnp.float32),
                pltpu.VMEM((held, rows, cols, width), jnp.float32),
                *(pltpu.VMEM(piece.shape, jnp.float32) for piece in given),
                pltpu.SemaphoreType.DMA((len(given),)),
                pltpu.SemaphoreType.DMA((2,)),
            ],
            compiler_params=pltpu.CompilerParams(vmem_limit_bytes=24 * 1024 * 1024),
        )(place, exchanged(message), table, block, block_near, *given)
    basis, message = small_call(
        functools.partial(second_kernel, cell_total), [block_shape, message_shape], [VMEM] * 2, exchanged(message), block
    )
    basis = small_call(functools.partial(third_kernel, cell_total), block_shape, [VMEM] * 2, exchanged(message), basis)
    basis = basis.reshape(total, rows, part, width)
    return lax.all_to_all(basis, "orb", split_axis=0, concat_axis=2, tiled=True)


def solution(mesh):
    slabs, orb_count = mesh.shape["dom"], mesh.shape["orb"]
    fine = Mesh(mesh.devices.reshape(slabs // 2, 2, orb_count), ALL)
    spec = P("orb", ("pair", "side"), None, None)
    return jax.shard_map(
        whole,
        mesh=fine,
        in_specs=(spec, P(("pair", "side"), None, None)),
        out_specs=spec,
        check_vma=False,
    )
```

```python
import functools

import jax
import jax.numpy as jnp
from jax import lax
from jax.experimental import pallas as pl
from jax.experimental.pallas import tpu as pltpu
from jax.sharding import Mesh
from jax.sharding import PartitionSpec as P

coefficients = (-49.0 / 18.0, 1.5, -0.15, 1.0 / 90.0)
spacing = 0.5
filter_centre = 23.0
filter_half = 23.0

REACH = 3
STEPS = 3
DEEP = REACH * STEPS
WIDE = REACH * (STEPS - 1)
EIGHT = 8
CORES = 2
WIDTH = 4
BLOCKS = 3
ALL = ("pair", "side", "orb")

VMEM = pl.BlockSpec(memory_space=pltpu.VMEM)
SMEM = pl.BlockSpec(memory_space=pltpu.SMEM)
HBM = pl.BlockSpec(memory_space=pltpu.HBM)

kinetic = -0.5 / (spacing * spacing)
taps = tuple(kinetic * c / filter_half for c in coefficients)
denominator = 180.0
whole_taps = tuple(round(denominator * c) for c in coefficients)
lane_scale = kinetic / filter_half / denominator
shift = (kinetic * 2.0 * coefficients[0] - filter_centre) / filter_half


def pack_kernel(place, orbitals, potential, *rest):
    outs, sems = rest[:-1], rest[-1]
    side, orb = place[0], place[2]
    kept, rows = orbitals.shape[0] // 2, orbitals.shape[1]
    part = outs[0].shape[1]
    columns = pl.ds(pl.multiple_of(orb * part, part), part)
    edge, shallow = pl.ds(side * (rows - DEEP), DEEP), pl.ds(side * (rows - WIDE), WIDE)
    sources = [potential.at[:, columns], potential.at[shallow, columns]]
    for at in range(kept):
        given, stays = orbitals.at[(1 - side) * kept + at], orbitals.at[side * kept + at]
        sources += [given.at[edge], given, stays.at[edge]]
    copies = [pltpu.make_async_copy(a, b, sems.at[i]) for i, (a, b) in enumerate(zip(sources, outs))]
    for copy in copies:
        copy.start()
    for copy in copies:
        copy.wait()


def packed(place, orbitals, potential, orb_count):
    held, rows, cols, width = orbitals.shape
    part = cols // orb_count
    shapes = [(rows, part, width), (WIDE, part, width)]
    shapes += [(DEEP, cols, width), (rows, cols, width), (DEEP, cols, width)] * (held // 2)
    return pl.pallas_call(
        pack_kernel,
        out_shape=[jax.ShapeDtypeStruct(shape, jnp.float32) for shape in shapes],
        in_specs=[SMEM, HBM, HBM],
        out_specs=[VMEM] * len(shapes),
        scratch_shapes=[pltpu.SemaphoreType.DMA((len(shapes),))],
        compiler_params=pltpu.CompilerParams(vmem_limit_bytes=16 * 1024 * 1024),
    )(place, *(pltpu.with_memory_space_constraint(array, pltpu.HBM) for array in (orbitals, potential)))


def join_kernel(swapped, slanted, straight, out):
    rows = swapped.shape[0]
    out[pl.ds(0, rows)] = swapped[...]
    out[pl.ds(rows, WIDE)] = slanted[...]
    out[pl.ds(rows + WIDE, WIDE)] = straight[...]


def split_dot(values, table):
    high = values.astype(jnp.bfloat16)
    rest = values - high.astype(jnp.float32)
    middle = rest.astype(jnp.bfloat16)
    low = (rest - middle.astype(jnp.float32)).astype(jnp.bfloat16)
    wide = jnp.concatenate([high, middle], axis=1)
    twice = jnp.concatenate([table, table], axis=0)
    return jnp.dot(wide, twice, preferred_element_type=jnp.float32) + jnp.dot(
        low, table, preferred_element_type=jnp.float32
    )


def filter_kernel(at, shares, early, late, place, own, swapped, slanted, straight, own_pot, lane_table, *rest):
    pot_far, before, outs = rest[:shares], rest[shares : shares + at], rest[shares + at : -4]
    field, first, second, weight = rest[-4:]
    outs, sorted_pieces = outs[:-1], outs[-1]
    side, me, orb = place[0], place[1], place[2]
    rows, cols, _ = swapped.shape
    both = 2 * rows
    strips = cols // EIGHT

    def keep(ref, row, strip, value):
        ref[row, pl.ds(EIGHT * (strip + 1), EIGHT), :] = value
        if strip == 0:
            ref[row, pl.ds(cols + EIGHT, EIGHT), :] = value
        if strip == strips - 1:
            ref[row, pl.ds(0, EIGHT), :] = value

    def gather(load, count, row_to):
        def body(row, carry):
            for strip in range(strips):
                keep(field, row_to + row, strip, load(row, pl.ds(EIGHT * strip, EIGHT)))
            return carry

        lax.fori_loop(0, count, body, 0, unroll=3)

    kept = own.shape[0] // 2
    gather(lambda row, span: own[side * kept + at, row, span, :], rows, DEEP + side * rows)
    gather(lambda row, span: swapped[row, span, :], rows, DEEP + (1 - side) * rows)
    gather(lambda row, span: slanted[row, span, :], DEEP, side * (both + DEEP))
    gather(lambda row, span: straight[row, span, :], DEEP, (1 - side) * (both + DEEP))

    def weigh(values):
        return values * (1.0 / filter_half) + shift

    weight[pl.ds(WIDE + side * rows, rows)] = weigh(own_pot[...])
    part = cols // shares
    for apart, far in enumerate(pot_far):
        columns = pl.ds(pl.multiple_of((orb ^ apart) * part, part), part)
        weight[pl.ds(WIDE + (1 - side) * rows, rows), columns] = weigh(far[pl.ds(0, rows)])
        weight[pl.ds(side * (both + WIDE), WIDE), columns] = weigh(far[pl.ds(rows, WIDE)])
        weight[pl.ds((1 - side) * (both + WIDE), WIDE), columns] = weigh(far[pl.ds(rows + WIDE, WIDE)])

    def step(source, before, before_at, weight_at, total, store):
        width = source.shape[2]
        count = total // BLOCKS

        def body(index, carry):
            base = index * count
            centres = source[pl.ds(base + REACH, count), pl.ds(EIGHT, cols), :]
            along = split_dot(centres.reshape(count * cols, width), lane_table[...])
            for strip in range(strips):
                start = EIGHT * (strip + 1)
                window = [source[base + i, pl.ds(start, EIGHT), :] for i in range(count + 2 * REACH)]
                for i in range(count):
                    row = base + i
                    value = window[i + REACH] * weight[weight_at + row, pl.ds(EIGHT * strip, EIGHT), :]
                    from_lanes = i * cols + EIGHT * strip
                    value = value + along[from_lanes : from_lanes + EIGHT] * lane_scale
                    for k in range(1, REACH + 1):
                        near = window[i + REACH - k] + window[i + REACH + k]
                        near = near + (
                            source[row + REACH, pl.ds(start - k, EIGHT), :]
                            + source[row + REACH, pl.ds(start + k, EIGHT), :]
                        )
                        value = value + taps[k] * near
                    if before is not None:
                        value = 2.0 * value - before[before_at + row, pl.ds(start, EIGHT), :]
                    store(row, strip, value)
            return carry

        lax.fori_loop(0, BLOCKS, body, 0)

    step(field, None, 0, 0, both + 2 * WIDE, functools.partial(keep, first))
    step(first, field, 2 * REACH, REACH, both + 2 * REACH, functools.partial(keep, second))
    piece = sorted_pieces.shape[2]

    def store_out(row, strip, value):
        to = (EIGHT * strip) // piece
        half = row // rows
        sorted_pieces[2 * to + half, row - half * rows, pl.ds(EIGHT * strip - to * piece, EIGHT), :] = value

    step(second, first, 2 * REACH, 2 * REACH, both, store_out)
    for apart, out in zip(early, outs):
        out[...] = sorted_pieces[me ^ apart]
    stages = (*before, sorted_pieces)
    for apart, out in zip(late, outs[len(early) :]):
        for stage, pieces in enumerate(stages):
            out[stage] = pieces[me ^ apart]
    for index, out in enumerate(outs[len(early) + len(late) :]):
        chip = orb // CORES ^ (1 if index < 2 else 0)
        slab = side ^ (index % 2)
        for stage, pieces in enumerate(stages):
            for core in range(CORES):
                out[stage, core] = pieces[2 * (CORES * chip + core) + slab]


def filtered_pieces(at, place, own, fetched, own_pot, pot_far, group, before, early, late, spares):
    slanted, swapped, straight = fetched
    rows, cols, width = own.shape[1:]
    both = 2 * rows
    apart = jnp.arange(width)[:, None] - jnp.arange(width)[None, :]
    lane_table = jnp.zeros((width, width), jnp.float32)
    for k, tap in enumerate(whole_taps):
        hit = (apart % width == k) | (-apart % width == k)
        lane_table = jnp.where(hit, float(tap), lane_table)

    def scratch(margin):
        return pltpu.VMEM((both + 2 * margin, cols + 2 * EIGHT, width), jnp.float32)

    piece = (rows, 2 * cols // group, width)
    shapes = [piece] * len(early) + [(at + 1, *piece)] * len(late) + [(at + 1, CORES, *piece)] * spares + [(group, *piece)]
    return pl.pallas_call(
        functools.partial(filter_kernel, at, len(pot_far), early, late),
        out_shape=[jax.ShapeDtypeStruct(shape, jnp.float32) for shape in shapes],
        in_specs=[SMEM] + [VMEM] * (6 + len(pot_far) + at),
        out_specs=[VMEM] * len(shapes),
        scratch_shapes=[
            scratch(DEEP),
            scratch(WIDE),
            scratch(REACH),
            pltpu.VMEM((both + 2 * WIDE, cols, width), jnp.float32),
        ],
        compiler_params=pltpu.CompilerParams(vmem_limit_bytes=24 * 1024 * 1024),
    )(place, own, swapped, slanted, straight, own_pot, lane_table.astype(jnp.bfloat16), *pot_far, *before)


LANES = 128


def exact_dot(a, b, contract=((1,), (0,))):
    return lax.dot_general(
        a, b, (contract, ((), ())), precision=lax.Precision.HIGHEST, preferred_element_type=jnp.float32
    )


def table_of(shape, test):
    rows = lax.broadcasted_iota(jnp.int32, shape, 0)
    columns = lax.broadcasted_iota(jnp.int32, shape, 1)
    return jnp.where(test(rows, columns), 1.0, 0.0).astype(jnp.float32)


def split(values):
    high = values.astype(jnp.bfloat16)
    rest = values - high.astype(jnp.float32)
    middle = rest.astype(jnp.bfloat16)
    return high, middle, (rest - middle.astype(jnp.float32)).astype(jnp.bfloat16)


def product(a, b, contract=((1,), (0,))):
    return lax.dot_general(a, b, (contract, ((), ())), preferred_element_type=jnp.float32)


def gram_message(wide, total):
    tall = total * EIGHT
    high, middle, low = split(wide)
    joined, doubled = jnp.concatenate([high, middle], axis=1), jnp.concatenate([high, high], axis=1)
    mixed = product(doubled, jnp.concatenate([middle, low], axis=1), ((1,), (1,)))
    sums = product(joined, joined, ((1,), (1,))) + (mixed + mixed.T)
    sums = sums * table_of((tall, tall), lambda r, c: r % EIGHT == c % EIGHT)
    partial = exact_dot(table_of((total, tall), lambda r, c: c // EIGHT == r), sums)
    spread = exact_dot(partial, table_of((tall, LANES), lambda r, c: r // EIGHT == c % total))
    per = LANES // total
    spread = spread * table_of((total, LANES), lambda r, c: c // total == r % per)
    return jnp.concatenate(
        [jnp.sum(spread[i * per : (i + 1) * per], axis=0, keepdims=True) for i in range(total // per)], axis=1
    )


def inverse_factor(copies, total, cell_total):
    row = jnp.sum(copies[...], axis=0) * (1.0 / cell_total)
    per = LANES // total
    wide = jnp.concatenate(
        [jnp.broadcast_to(row[:, i * LANES : (i + 1) * LANES], (per, LANES)) for i in range(total // per)], axis=0
    )
    wide = wide * table_of((total, LANES), lambda r, c: c // total == r % per)
    table = exact_dot(wide, table_of((LANES, LANES), lambda r, c: r % total == c))
    table = table + table_of((total, LANES), lambda r, c: c - total == r)
    index = lax.broadcasted_iota(jnp.int32, (total, LANES), 0)
    for start in range(0, total, WIDTH):
        block = range(start, min(start + WIDTH, total))
        columns = {j: jnp.broadcast_to(table[:, j : j + 1], (total, LANES)) for j in block}
        rows = {j: table[j : j + 1, :] for j in block}
        reduced = table
        for j in block:
            value = columns[j][j : j + 1, :]
            scale = lax.rsqrt(value)
            scale = scale * (1.5 - 0.5 * value * scale * scale)
            factor, rows[j] = columns[j] * scale, rows[j] * scale
            for later in block:
                if later > j:
                    share = factor[later : later + 1, :]
                    columns[later] = columns[later] - factor * share
                    rows[later] = rows[later] - share * rows[j]
            reduced = reduced - factor * rows[j]
        for j in block:
            table = jnp.where(index == j, rows[j], table)
        table = jnp.where(index > block[-1], reduced, table)
    return table


def by_tiles(table, total):
    tall = total * EIGHT
    wide = exact_dot(table, table_of((LANES, tall), lambda r, c: r - total == c // EIGHT))
    both = exact_dot(table_of((tall, total), lambda r, c: r // EIGHT == c), wide)
    return both * table_of((tall, tall), lambda r, c: r % EIGHT == c % EIGHT)


def side_by_side(ref):
    total, length, width = ref.shape
    tiles = [ref[:, start : start + EIGHT, :].reshape(total * EIGHT, width) for start in range(0, length, EIGHT)]
    return jnp.concatenate(tiles, axis=1)


def first_kernel(early, late, kept, forwards, place, *refs):
    outs = 2 + len(forwards[:1])
    given, (block, message, *forward) = refs[:-outs], refs[-outs:]
    if forward:
        for slot, apart in enumerate(forwards):
            for at in range(kept):
                forward[0][slot, at] = given[at * len(early) + early.index(apart)][...]
    me, shape = place[1], block.shape[1:]
    for at in range(kept):
        for index, apart in enumerate(early):
            block[(me ^ apart) * kept + at] = given[at * len(early) + index][...].reshape(shape)
        for index, apart in enumerate(late):
            block[(me ^ apart) * kept + at] = given[kept * len(early) + index][at].reshape(shape)
    message[...] = jnp.broadcast_to(gram_message(side_by_side(block), block.shape[0])[None], message.shape)


def applied(table, block):
    total = block.shape[0]
    tall = total * EIGHT
    high, middle, low = split(by_tiles(table, total))
    values_high, values_middle, values_low = split(side_by_side(block))
    left = jnp.concatenate(
        [jnp.concatenate([high, high], axis=1), jnp.concatenate([middle, middle], axis=1)], axis=0
    )
    main = product(left, jnp.concatenate([values_high, values_middle], axis=0))
    rest = product(jnp.concatenate([low, high], axis=1), jnp.concatenate([values_high, values_low], axis=0))
    return main[:tall] + (main[tall:] + rest)


def put(wide, basis):
    total, length, width = basis.shape
    for t in range(length // EIGHT):
        piece = wide[:, t * width : (t + 1) * width].reshape(total, EIGHT, width)
        basis[:, EIGHT * t : EIGHT * (t + 1), :] = piece


def second_kernel(cell_total, copies, block, basis, message):
    total = block.shape[0]
    wide = applied(inverse_factor(copies, total, cell_total), block)
    put(wide, basis)
    message[...] = jnp.broadcast_to(gram_message(wide, total)[None], message.shape)


def third_kernel(cell_total, copies, block, basis):
    put(applied(inverse_factor(copies, block.shape[0], cell_total), block), basis)


def table_kernel(cell_total, copies, block, table_out, message_far, message, sem):
    total = block.shape[0]
    table = inverse_factor(copies, total, cell_total)
    table_out[...] = table
    message[...] = jnp.broadcast_to(gram_message(applied(table, block), total)[None], message.shape)
    leave = pltpu.make_async_copy(message, message_far, sem)
    leave.start()
    leave.wait()


def last_kernel(cell_total, place, copies, table, block, block_near, *refs):
    count = (len(refs) - 5) // 2
    far, (out_far, splats, out), spares = refs[:count], refs[count : count + 3], refs[count + 3 : 2 * count + 3]
    sems, sems_out = refs[2 * count + 3 :]
    total, length, width = block.shape
    held, rows = out.shape[:2]
    part = length // rows
    side, orb = place[0], place[2]
    chip = orb // CORES
    fetches = [pltpu.make_async_copy(a, b, sems.at[i]) for i, (a, b) in enumerate(zip(far, spares))]
    for fetch in fetches:
        fetch.start()
    second = inverse_factor(copies, total, cell_total)
    pick = table_of((LANES, total), lambda r, c: r - total == c)
    product = exact_dot(exact_dot(second, pick), exact_dot(table[...], pick))
    own = exact_dot(table_of((held * EIGHT, total), lambda r, c: orb * held + r // EIGHT == c), product)
    wide = exact_dot(own, table_of((total, total * width), lambda r, c: c // width == r))
    for orbital in range(total):
        splats[orbital] = wide[:, orbital * width : (orbital + 1) * width].reshape(held, EIGHT, width)

    def write(sources, first_column):
        def body(row, carry):
            for strip in range(part // EIGHT):
                sums = None
                for orbital, load in sources:
                    values = load(row, strip)
                    terms = [splats[orbital, i] * values for i in range(held)]
                    sums = terms if sums is None else [a + b for a, b in zip(sums, terms)]
                column = pl.multiple_of(first_column + strip * EIGHT, EIGHT)
                for i in range(held):
                    out[i, row, pl.ds(column, EIGHT), :] = sums[i]
            return carry

        lax.fori_loop(0, rows, body, 0, unroll=2)

    def at(ref, index):
        def load(row, strip):
            return ref[index, pl.ds(pl.multiple_of(row * part + strip * EIGHT, EIGHT), EIGHT), :]

        return load

    write([(j, at(block, j)) for j in range(total)], orb * part)
    write([(j, at(block_near, j)) for j in range(total)], (orb ^ 1) * part)

    def leave(which, index):
        columns = pl.ds(pl.multiple_of(which * CORES * part, EIGHT), CORES * part)
        return pltpu.make_async_copy(out.at[:, :, columns], out_far.at[:, :, columns], sems_out.at[index])

    leave(chip, 0).start()
    for fetch in fetches:
        fetch.wait()

    def piece_at(ref, first, second):
        return lambda row, strip: ref[first, second, row, pl.ds(strip * EIGHT, EIGHT), :]

    kinds, kept = count // 2, held // 2
    core = orb % CORES
    for turn in range(CORES):
        share = core ^ turn
        sources = []
        for flip in range(2):
            for kind in range(kinds - 1):
                quad = (orb ^ CORES if kind // 2 else orb) ^ flip
                for stage in range(kept):
                    orbital = quad * held + (side ^ (kind % 2)) * kept + stage
                    sources.append((orbital, piece_at(spares[flip * kinds + kind], stage, share)))
            quad = orb ^ CORES ^ turn ^ flip
            for stage in range(kept):
                orbital = quad * held + (side ^ 1) * kept + stage
                sources.append((orbital, piece_at(spares[turn * kinds + kinds - 1], flip, stage)))
        write(sources, ((1 - chip) * CORES + share) * part)
    leave(1 - chip, 1).start()
    leave(chip, 0).wait()
    leave(1 - chip, 1).wait()


def small_call(kernel, out_shape, specs, *args):
    return pl.pallas_call(
        kernel,
        out_shape=out_shape,
        in_specs=specs,
        out_specs=jax.tree.map(lambda _: VMEM, out_shape),
        compiler_params=pltpu.CompilerParams(vmem_limit_bytes=24 * 1024 * 1024),
    )(*args)


def whole(orbitals, potential):
    pair_count, orb_count = lax.axis_size("pair"), lax.axis_size("orb")
    slabs = 2 * pair_count
    side, orb = lax.axis_index("side"), lax.axis_index("orb")
    held, rows, cols, width = orbitals.shape
    kept = held // 2
    part = cols // orb_count

    slant = [(i, (i + (1 if i % 2 else -1)) % slabs) for i in range(slabs)]
    ahead = [(i, (i + (2 if i % 2 else -2)) % slabs) for i in range(slabs)]
    swap = [(0, 1), (1, 0)]
    slab_axes = ("pair", "side")

    group = 2 * orb_count
    me = 2 * orb + side

    def flat_of(index):
        return (index % 2) * orb_count + index // 2

    place = jnp.stack([side, me, orb]).astype(jnp.int32)
    mine, edge, *sent = packed(place, orbitals, potential, orb_count)

    pieces = [
        lax.ppermute(mine, "side", swap),
        lax.ppermute(edge, slab_axes, slant),
        lax.ppermute(edge, slab_axes, ahead),
    ]
    joined = pl.pallas_call(
        join_kernel,
        out_shape=jax.ShapeDtypeStruct((rows + 2 * WIDE, part, width), jnp.float32),
        in_specs=[VMEM] * 3,
        out_specs=VMEM,
        compiler_params=pltpu.CompilerParams(vmem_limit_bytes=16 * 1024 * 1024),
    )(*pieces)
    pot_far = [joined] + [
        lax.ppermute(joined, "orb", [(i, i ^ m) for i in range(orb_count)]) for m in range(1, orb_count)
    ]

    fetched = []
    for at in range(kept):
        swapped = lax.ppermute(sent[3 * at + 1], "side", swap)
        slanted = lax.ppermute(sent[3 * at], slab_axes, slant)
        straight = lax.ppermute(sent[3 * at + 2], slab_axes, ahead)
        fetched.append((slanted, swapped, straight))

    early = tuple(sorted((m for m in range(1, group) if m != CORES), key=lambda m: (m < 2 * CORES, -(m % 2), m)))
    late = (0, CORES)
    spares = 3 if orb_count == 2 * CORES and kept == 2 else 0

    def to_partner(piece, m):
        if m == 0:
            return piece
        return lax.ppermute(piece, ("side", "orb"), [(flat_of(i), flat_of(i ^ m)) for i in range(group)])

    parts, before = [], []
    for at in range(kept):
        final = at == kept - 1
        outs = filtered_pieces(
            at,
            place,
            orbitals,
            fetched[at],
            potential,
            pot_far,
            group,
            before,
            early,
            late if final else (),
            spares if final else 0,
        )
        parts += [to_partner(piece, m) for piece, m in zip(outs, early)]
        before.append(outs[-1])
    parts += [to_partner(piece, m) for piece, m in zip(outs[len(early) :], late)]
    spare = outs[len(early) + len(late) : -1]
    total, devices = held * orb_count, slabs * orb_count
    cell_total = rows * part * width * devices
    block_shape = jax.ShapeDtypeStruct((total, rows * part, width), jnp.float32)
    message_shape = jax.ShapeDtypeStruct((devices, 1, total * total), jnp.float32)

    def exchanged(message):
        return lax.all_to_all(message, ALL, 0, 0)

    forwards = (1, 1 + CORES) if spares else ()
    forward_shape = jax.ShapeDtypeStruct((CORES, kept, rows, part, width), jnp.float32)
    block, message, *forward = small_call(
        functools.partial(first_kernel, early, late, kept, forwards),
        [block_shape, message_shape] + [forward_shape] * len(forwards[:1]),
        [SMEM] + [VMEM] * len(parts),
        *(place, *parts),
    )
    if spares:
        across = [(i, i ^ CORES) for i in range(orb_count)]
        cores = [(i, i ^ 1) for i in range(orb_count)]
        given = [
            spare[0],
            lax.ppermute(spare[1], "side", swap),
            lax.ppermute(spare[2], "orb", across),
        ]
        given.append(lax.ppermute(forward[0], "orb", across))
        block_near = lax.ppermute(block, "orb", cores)
        table_shape = jax.ShapeDtypeStruct((total, LANES), jnp.float32)
        near = [lax.ppermute(piece, "orb", cores) for piece in given[:-1]]
        given = given + near + [lax.ppermute(given[-1], "orb", cores)]
        copies = exchanged(message)
        table, message = pl.pallas_call(
            functools.partial(table_kernel, cell_total),
            out_shape=[table_shape, message_shape],
            in_specs=[VMEM] * 2,
            out_specs=[VMEM, HBM],
            scratch_shapes=[pltpu.VMEM(message_shape.shape, jnp.float32), pltpu.SemaphoreType.DMA],
            compiler_params=pltpu.CompilerParams(vmem_limit_bytes=24 * 1024 * 1024),
        )(copies, block)
        return pl.pallas_call(
            functools.partial(last_kernel, cell_total),
            out_shape=jax.ShapeDtypeStruct((held, rows, cols, width), jnp.float32),
            in_specs=[SMEM] + [VMEM] * 4 + [HBM] * len(given),
            out_specs=HBM,
            scratch_shapes=[
                pltpu.VMEM((total, held, EIGHT, width), jnp.float32),
                pltpu.VMEM((held, rows, cols, width), jnp.float32),
                *(pltpu.VMEM(piece.shape, jnp.float32) for piece in given),
                pltpu.SemaphoreType.DMA((len(given),)),
                pltpu.SemaphoreType.DMA((2,)),
            ],
            compiler_params=pltpu.CompilerParams(vmem_limit_bytes=24 * 1024 * 1024),
        )(place, exchanged(message), table, block, block_near, *given)
    basis, message = small_call(
        functools.partial(second_kernel, cell_total), [block_shape, message_shape], [VMEM] * 2, exchanged(message), block
    )
    basis = small_call(functools.partial(third_kernel, cell_total), block_shape, [VMEM] * 2, exchanged(message), basis)
    basis = basis.reshape(total, rows, part, width)
    return lax.all_to_all(basis, "orb", split_axis=0, concat_axis=2, tiled=True)


def solution(mesh):
    slabs, orb_count = mesh.shape["dom"], mesh.shape["orb"]
    fine = Mesh(mesh.devices.reshape(slabs // 2, 2, orb_count), ALL)
    spec = P("orb", ("pair", "side"), None, None)
    return jax.shard_map(
        whole,
        mesh=fine,
        in_specs=(spec, P(("pair", "side"), None, None)),
        out_specs=spec,
        check_vma=False,
    )
```

```python
import functools

import jax
import jax.numpy as jnp
from jax import lax
from jax.experimental import pallas as pl
from jax.experimental.pallas import tpu as pltpu
from jax.sharding import Mesh
from jax.sharding import PartitionSpec as P

coefficients = (-49.0 / 18.0, 1.5, -0.15, 1.0 / 90.0)
spacing = 0.5
filter_centre = 23.0
filter_half = 23.0

REACH = 3
STEPS = 3
DEEP = REACH * STEPS
WIDE = REACH * (STEPS - 1)
EIGHT = 8
CORES = 2
WIDTH = 4
BLOCKS = 3
ALL = ("pair", "side", "orb")

VMEM = pl.BlockSpec(memory_space=pltpu.VMEM)
SMEM = pl.BlockSpec(memory_space=pltpu.SMEM)
HBM = pl.BlockSpec(memory_space=pltpu.HBM)

kinetic = -0.5 / (spacing * spacing)
taps = tuple(kinetic * c / filter_half for c in coefficients)
denominator = 180.0
whole_taps = tuple(round(denominator * c) for c in coefficients)
lane_scale = kinetic / filter_half / denominator
shift = (kinetic * 2.0 * coefficients[0] - filter_centre) / filter_half


def pack_kernel(place, orbitals, potential, *rest):
    outs, sems = rest[:-1], rest[-1]
    side, orb = place[0], place[2]
    kept, rows = orbitals.shape[0] // 2, orbitals.shape[1]
    part = outs[0].shape[1]
    columns = pl.ds(pl.multiple_of(orb * part, part), part)
    edge, shallow = pl.ds(side * (rows - DEEP), DEEP), pl.ds(side * (rows - WIDE), WIDE)
    sources = [potential.at[:, columns], potential.at[shallow, columns]]
    for at in range(kept):
        given, stays = orbitals.at[(1 - side) * kept + at], orbitals.at[side * kept + at]
        sources += [given.at[edge], given, stays.at[edge]]
    copies = [pltpu.make_async_copy(a, b, sems.at[i]) for i, (a, b) in enumerate(zip(sources, outs))]
    for copy in copies:
        copy.start()
    for copy in copies:
        copy.wait()


def packed(place, orbitals, potential, orb_count):
    held, rows, cols, width = orbitals.shape
    part = cols // orb_count
    shapes = [(rows, part, width), (WIDE, part, width)]
    shapes += [(DEEP, cols, width), (rows, cols, width), (DEEP, cols, width)] * (held // 2)
    return pl.pallas_call(
        pack_kernel,
        out_shape=[jax.ShapeDtypeStruct(shape, jnp.float32) for shape in shapes],
        in_specs=[SMEM, HBM, HBM],
        out_specs=[VMEM] * len(shapes),
        scratch_shapes=[pltpu.SemaphoreType.DMA((len(shapes),))],
        compiler_params=pltpu.CompilerParams(vmem_limit_bytes=16 * 1024 * 1024),
    )(place, *(pltpu.with_memory_space_constraint(array, pltpu.HBM) for array in (orbitals, potential)))


def join_kernel(swapped, slanted, straight, out):
    rows = swapped.shape[0]
    out[pl.ds(0, rows)] = swapped[...]
    out[pl.ds(rows, WIDE)] = slanted[...]
    out[pl.ds(rows + WIDE, WIDE)] = straight[...]


def split_dot(values, table):
    high = values.astype(jnp.bfloat16)
    rest = values - high.astype(jnp.float32)
    middle = rest.astype(jnp.bfloat16)
    low = (rest - middle.astype(jnp.float32)).astype(jnp.bfloat16)
    wide = jnp.concatenate([high, middle], axis=1)
    twice = jnp.concatenate([table, table], axis=0)
    return jnp.dot(wide, twice, preferred_element_type=jnp.float32) + jnp.dot(
        low, table, preferred_element_type=jnp.float32
    )


def filter_kernel(at, shares, early, place, own, swapped, slanted, straight, own_pot, lane_table, *rest):
    pot_far, outs = rest[:shares], rest[shares:-4]
    field, first, second, weight = rest[-4:]
    outs, sorted_pieces = outs[:-1], outs[-1]
    side, me, orb = place[0], place[1], place[2]
    rows, cols, _ = swapped.shape
    both = 2 * rows
    strips = cols // EIGHT

    def keep(ref, row, strip, value):
        ref[row, pl.ds(EIGHT * (strip + 1), EIGHT), :] = value
        if strip == 0:
            ref[row, pl.ds(cols + EIGHT, EIGHT), :] = value
        if strip == strips - 1:
            ref[row, pl.ds(0, EIGHT), :] = value

    def gather(load, count, row_to):
        def body(row, carry):
            for strip in range(strips):
                keep(field, row_to + row, strip, load(row, pl.ds(EIGHT * strip, EIGHT)))
            return carry

        lax.fori_loop(0, count, body, 0, unroll=3)

    kept = own.shape[0] // 2
    gather(lambda row, span: own[side * kept + at, row, span, :], rows, DEEP + side * rows)
    gather(lambda row, span: swapped[row, span, :], rows, DEEP + (1 - side) * rows)
    gather(lambda row, span: slanted[row, span, :], DEEP, side * (both + DEEP))
    gather(lambda row, span: straight[row, span, :], DEEP, (1 - side) * (both + DEEP))

    def weigh(values):
        return values * (1.0 / filter_half) + shift

    weight[pl.ds(WIDE + side * rows, rows)] = weigh(own_pot[...])
    part = cols // shares
    for apart, far in enumerate(pot_far):
        columns = pl.ds(pl.multiple_of((orb ^ apart) * part, part), part)
        weight[pl.ds(WIDE + (1 - side) * rows, rows), columns] = weigh(far[pl.ds(0, rows)])
        weight[pl.ds(side * (both + WIDE), WIDE), columns] = weigh(far[pl.ds(rows, WIDE)])
        weight[pl.ds((1 - side) * (both + WIDE), WIDE), columns] = weigh(far[pl.ds(rows + WIDE, WIDE)])

    def step(source, before, before_at, weight_at, total, store):
        width = source.shape[2]
        count = total // BLOCKS

        def body(index, carry):
            base = index * count
            centres = source[pl.ds(base + REACH, count), pl.ds(EIGHT, cols), :]
            along = split_dot(centres.reshape(count * cols, width), lane_table[...])
            for strip in range(strips):
                start = EIGHT * (strip + 1)
                window = [source[base + i, pl.ds(start, EIGHT), :] for i in range(count + 2 * REACH)]
                for i in range(count):
                    row = base + i
                    value = window[i + REACH] * weight[weight_at + row, pl.ds(EIGHT * strip, EIGHT), :]
                    from_lanes = i * cols + EIGHT * strip
                    value = value + along[from_lanes : from_lanes + EIGHT] * lane_scale
                    for k in range(1, REACH + 1):
                        near = window[i + REACH - k] + window[i + REACH + k]
                        near = near + (
                            source[row + REACH, pl.ds(start - k, EIGHT), :]
                            + source[row + REACH, pl.ds(start + k, EIGHT), :]
                        )
                        value = value + taps[k] * near
                    if before is not None:
                        value = 2.0 * value - before[before_at + row, pl.ds(start, EIGHT), :]
                    store(row, strip, value)
            return carry

        lax.fori_loop(0, BLOCKS, body, 0)

    step(field, None, 0, 0, both + 2 * WIDE, functools.partial(keep, first))
    step(first, field, 2 * REACH, REACH, both + 2 * REACH, functools.partial(keep, second))
    piece = sorted_pieces.shape[2]

    def store_out(row, strip, value):
        to = (EIGHT * strip) // piece
        half = row // rows
        sorted_pieces[2 * to + half, row - half * rows, pl.ds(EIGHT * strip - to * piece, EIGHT), :] = value

    step(second, first, 2 * REACH, 2 * REACH, both, store_out)
    for apart, out in zip(early, outs):
        out[...] = sorted_pieces[me ^ apart]


def late_kernel(stages, late, place, *refs):
    given, outs = refs[:stages], refs[stages:]
    side, me, orb = place[0], place[1], place[2]
    for stage, pieces in enumerate(given):
        for apart, out in zip(late, outs):
            out[stage] = pieces[me ^ apart]
        for index, out in enumerate(outs[len(late) :]):
            chip = orb // CORES ^ (1 if index < 2 else 0)
            for core in range(CORES):
                out[stage, core] = pieces[2 * (CORES * chip + core) + (side ^ (index % 2))]


def filtered_pieces(at, place, own, fetched, own_pot, pot_far, group, early):
    slanted, swapped, straight = fetched
    rows, cols, width = own.shape[1:]
    both = 2 * rows
    apart = jnp.arange(width)[:, None] - jnp.arange(width)[None, :]
    lane_table = jnp.zeros((width, width), jnp.float32)
    for k, tap in enumerate(whole_taps):
        hit = (apart % width == k) | (-apart % width == k)
        lane_table = jnp.where(hit, float(tap), lane_table)

    def scratch(margin):
        return pltpu.VMEM((both + 2 * margin, cols + 2 * EIGHT, width), jnp.float32)

    piece = (rows, 2 * cols // group, width)
    shapes = [piece] * len(early) + [(group, *piece)]
    return pl.pallas_call(
        functools.partial(filter_kernel, at, len(pot_far), early),
        out_shape=[jax.ShapeDtypeStruct(shape, jnp.float32) for shape in shapes],
        in_specs=[SMEM] + [VMEM] * (6 + len(pot_far)),
        out_specs=[VMEM] * len(shapes),
        scratch_shapes=[
            scratch(DEEP),
            scratch(WIDE),
            scratch(REACH),
            pltpu.VMEM((both + 2 * WIDE, cols, width), jnp.float32),
        ],
        compiler_params=pltpu.CompilerParams(vmem_limit_bytes=24 * 1024 * 1024),
    )(place, own, swapped, slanted, straight, own_pot, lane_table.astype(jnp.bfloat16), *pot_far)


LANES = 128


def exact_dot(a, b, contract=((1,), (0,))):
    return lax.dot_general(
        a, b, (contract, ((), ())), precision=lax.Precision.HIGHEST, preferred_element_type=jnp.float32
    )


def table_of(shape, test):
    rows = lax.broadcasted_iota(jnp.int32, shape, 0)
    columns = lax.broadcasted_iota(jnp.int32, shape, 1)
    return jnp.where(test(rows, columns), 1.0, 0.0).astype(jnp.float32)


def split(values):
    high = values.astype(jnp.bfloat16)
    rest = values - high.astype(jnp.float32)
    middle = rest.astype(jnp.bfloat16)
    return high, middle, (rest - middle.astype(jnp.float32)).astype(jnp.bfloat16)


def product(a, b, contract=((1,), (0,))):
    return lax.dot_general(a, b, (contract, ((), ())), preferred_element_type=jnp.float32)


def gram_message(wide, total):
    tall = total * EIGHT
    high, middle, low = split(wide)
    joined, doubled = jnp.concatenate([high, middle], axis=1), jnp.concatenate([high, high], axis=1)
    mixed = product(doubled, jnp.concatenate([middle, low], axis=1), ((1,), (1,)))
    sums = product(joined, joined, ((1,), (1,))) + (mixed + mixed.T)
    sums = sums * table_of((tall, tall), lambda r, c: r % EIGHT == c % EIGHT)
    partial = exact_dot(table_of((total, tall), lambda r, c: c // EIGHT == r), sums)
    spread = exact_dot(partial, table_of((tall, LANES), lambda r, c: r // EIGHT == c % total))
    per = LANES // total
    spread = spread * table_of((total, LANES), lambda r, c: c // total == r % per)
    return jnp.concatenate(
        [jnp.sum(spread[i * per : (i + 1) * per], axis=0, keepdims=True) for i in range(total // per)], axis=1
    )


def inverse_factor(copies, total, cell_total):
    row = jnp.sum(copies[...], axis=0) * (1.0 / cell_total)
    per = LANES // total
    wide = jnp.concatenate(
        [jnp.broadcast_to(row[:, i * LANES : (i + 1) * LANES], (per, LANES)) for i in range(total // per)], axis=0
    )
    wide = wide * table_of((total, LANES), lambda r, c: c // total == r % per)
    table = exact_dot(wide, table_of((LANES, LANES), lambda r, c: r % total == c))
    table = table + table_of((total, LANES), lambda r, c: c - total == r)
    index = lax.broadcasted_iota(jnp.int32, (total, LANES), 0)
    for start in range(0, total, WIDTH):
        block = range(start, min(start + WIDTH, total))
        columns = {j: jnp.broadcast_to(table[:, j : j + 1], (total, LANES)) for j in block}
        rows = {j: table[j : j + 1, :] for j in block}
        reduced = table
        for j in block:
            value = columns[j][j : j + 1, :]
            scale = lax.rsqrt(value)
            scale = scale * (1.5 - 0.5 * value * scale * scale)
            factor, rows[j] = columns[j] * scale, rows[j] * scale
            for later in block:
                if later > j:
                    share = factor[later : later + 1, :]
                    columns[later] = columns[later] - factor * share
                    rows[later] = rows[later] - share * rows[j]
            reduced = reduced - factor * rows[j]
        for j in block:
            table = jnp.where(index == j, rows[j], table)
        table = jnp.where(index > block[-1], reduced, table)
    return table


def by_tiles(table, total):
    tall = total * EIGHT
    wide = exact_dot(table, table_of((LANES, tall), lambda r, c: r - total == c // EIGHT))
    both = exact_dot(table_of((tall, total), lambda r, c: r // EIGHT == c), wide)
    return both * table_of((tall, tall), lambda r, c: r % EIGHT == c % EIGHT)


def side_by_side(ref):
    total, length, width = ref.shape
    tiles = [ref[:, start : start + EIGHT, :].reshape(total * EIGHT, width) for start in range(0, length, EIGHT)]
    return jnp.concatenate(tiles, axis=1)


def forward_kernel(place, block, out):
    kept, held = out.shape[1], 2 * out.shape[1]
    for flip in range(CORES):
        for at in range(kept):
            out[flip, at] = block[(place[2] ^ flip) * held + (place[0] ^ 1) * kept + at].reshape(out.shape[2:])


def first_kernel(early, late, kept, place, *refs):
    given, (block, message) = refs[:-2], refs[-2:]
    me, shape = place[1], block.shape[1:]
    for at in range(kept):
        for index, apart in enumerate(early):
            block[(me ^ apart) * kept + at] = given[at * len(early) + index][...].reshape(shape)
        for index, apart in enumerate(late):
            block[(me ^ apart) * kept + at] = given[kept * len(early) + index][at].reshape(shape)
    message[...] = jnp.broadcast_to(gram_message(side_by_side(block), block.shape[0])[None], message.shape)


def applied(table, block):
    total = block.shape[0]
    tall = total * EIGHT
    high, middle, low = split(by_tiles(table, total))
    values_high, values_middle, values_low = split(side_by_side(block))
    left = jnp.concatenate(
        [jnp.concatenate([high, high], axis=1), jnp.concatenate([middle, middle], axis=1)], axis=0
    )
    main = product(left, jnp.concatenate([values_high, values_middle], axis=0))
    rest = product(jnp.concatenate([low, high], axis=1), jnp.concatenate([values_high, values_low], axis=0))
    return main[:tall] + (main[tall:] + rest)


def put(wide, basis):
    total, length, width = basis.shape
    for t in range(length // EIGHT):
        piece = wide[:, t * width : (t + 1) * width].reshape(total, EIGHT, width)
        basis[:, EIGHT * t : EIGHT * (t + 1), :] = piece


def second_kernel(cell_total, copies, block, basis, message):
    total = block.shape[0]
    wide = applied(inverse_factor(copies, total, cell_total), block)
    put(wide, basis)
    message[...] = jnp.broadcast_to(gram_message(wide, total)[None], message.shape)


def third_kernel(cell_total, copies, block, basis):
    put(applied(inverse_factor(copies, block.shape[0], cell_total), block), basis)


def table_kernel(cell_total, copies, block, table_out, message_far, message, sem):
    total = block.shape[0]
    table = inverse_factor(copies, total, cell_total)
    table_out[...] = table
    message[...] = jnp.broadcast_to(gram_message(applied(table, block), total)[None], message.shape)
    leave = pltpu.make_async_copy(message, message_far, sem)
    leave.start()
    leave.wait()


def last_kernel(cell_total, place, copies, table, block, block_near, *refs):
    count = (len(refs) - 5) // 2
    far, (out_far, splats, out), spares = refs[:count], refs[count : count + 3], refs[count + 3 : 2 * count + 3]
    sems, sems_out = refs[2 * count + 3 :]
    total, length, width = block.shape
    held, rows = out.shape[:2]
    part = length // rows
    side, orb = place[0], place[2]
    chip = orb // CORES
    fetches = [pltpu.make_async_copy(a, b, sems.at[i]) for i, (a, b) in enumerate(zip(far, spares))]
    for fetch in fetches:
        fetch.start()
    second = inverse_factor(copies, total, cell_total)
    pick = table_of((LANES, total), lambda r, c: r - total == c)
    product = exact_dot(exact_dot(second, pick), exact_dot(table[...], pick))
    own = exact_dot(table_of((held * EIGHT, total), lambda r, c: orb * held + r // EIGHT == c), product)
    wide = exact_dot(own, table_of((total, total * width), lambda r, c: c // width == r))
    for orbital in range(total):
        splats[orbital] = wide[:, orbital * width : (orbital + 1) * width].reshape(held, EIGHT, width)

    def write(sources, first_column):
        def body(row, carry):
            for strip in range(part // EIGHT):
                sums = None
                for orbital, load in sources:
                    values = load(row, strip)
                    terms = [splats[orbital, i] * values for i in range(held)]
                    sums = terms if sums is None else [a + b for a, b in zip(sums, terms)]
                column = pl.multiple_of(first_column + strip * EIGHT, EIGHT)
                for i in range(held):
                    out[i, row, pl.ds(column, EIGHT), :] = sums[i]
            return carry

        lax.fori_loop(0, rows, body, 0, unroll=2)

    def at(ref, index):
        def load(row, strip):
            return ref[index, pl.ds(pl.multiple_of(row * part + strip * EIGHT, EIGHT), EIGHT), :]

        return load

    write([(j, at(block, j)) for j in range(total)], orb * part)
    write([(j, at(block_near, j)) for j in range(total)], (orb ^ 1) * part)

    def leave(which, index):
        columns = pl.ds(pl.multiple_of(which * CORES * part, EIGHT), CORES * part)
        return pltpu.make_async_copy(out.at[:, :, columns], out_far.at[:, :, columns], sems_out.at[index])

    leave(chip, 0).start()
    for fetch in fetches:
        fetch.wait()

    def piece_at(ref, first, second):
        return lambda row, strip: ref[first, second, row, pl.ds(strip * EIGHT, EIGHT), :]

    kinds, kept = count // 2, held // 2
    core = orb % CORES
    for turn in range(CORES):
        share = core ^ turn
        sources = []
        for flip in range(2):
            for kind in range(kinds - 1):
                quad = (orb ^ CORES if kind // 2 else orb) ^ flip
                for stage in range(kept):
                    orbital = quad * held + (side ^ (kind % 2)) * kept + stage
                    sources.append((orbital, piece_at(spares[flip * kinds + kind], stage, share)))
            quad = orb ^ CORES ^ turn ^ flip
            for stage in range(kept):
                orbital = quad * held + (side ^ 1) * kept + stage
                sources.append((orbital, piece_at(spares[turn * kinds + kinds - 1], flip, stage)))
        write(sources, ((1 - chip) * CORES + share) * part)
    leave(1 - chip, 1).start()
    leave(chip, 0).wait()
    leave(1 - chip, 1).wait()


def small_call(kernel, out_shape, specs, *args):
    return pl.pallas_call(
        kernel,
        out_shape=out_shape,
        in_specs=specs,
        out_specs=jax.tree.map(lambda _: VMEM, out_shape),
        compiler_params=pltpu.CompilerParams(vmem_limit_bytes=24 * 1024 * 1024),
    )(*args)


def whole(orbitals, potential):
    pair_count, orb_count = lax.axis_size("pair"), lax.axis_size("orb")
    slabs = 2 * pair_count
    side, orb = lax.axis_index("side"), lax.axis_index("orb")
    held, rows, cols, width = orbitals.shape
    kept = held // 2
    part = cols // orb_count

    slant = [(i, (i + (1 if i % 2 else -1)) % slabs) for i in range(slabs)]
    ahead = [(i, (i + (2 if i % 2 else -2)) % slabs) for i in range(slabs)]
    swap = [(0, 1), (1, 0)]
    slab_axes = ("pair", "side")

    group = 2 * orb_count
    me = 2 * orb + side

    def flat_of(index):
        return (index % 2) * orb_count + index // 2

    place = jnp.stack([side, me, orb]).astype(jnp.int32)
    mine, edge, *sent = packed(place, orbitals, potential, orb_count)

    pieces = [
        lax.ppermute(mine, "side", swap),
        lax.ppermute(edge, slab_axes, slant),
        lax.ppermute(edge, slab_axes, ahead),
    ]
    joined = pl.pallas_call(
        join_kernel,
        out_shape=jax.ShapeDtypeStruct((rows + 2 * WIDE, part, width), jnp.float32),
        in_specs=[VMEM] * 3,
        out_specs=VMEM,
        compiler_params=pltpu.CompilerParams(vmem_limit_bytes=16 * 1024 * 1024),
    )(*pieces)
    pot_far = [joined] + [
        lax.ppermute(joined, "orb", [(i, i ^ m) for i in range(orb_count)]) for m in range(1, orb_count)
    ]

    fetched = []
    for at in range(kept):
        swapped = lax.ppermute(sent[3 * at + 1], "side", swap)
        slanted = lax.ppermute(sent[3 * at], slab_axes, slant)
        straight = lax.ppermute(sent[3 * at + 2], slab_axes, ahead)
        fetched.append((slanted, swapped, straight))

    early = tuple(sorted((m for m in range(1, group) if m != CORES), key=lambda m: (m < 2 * CORES, -(m % 2), m)))
    late = (0, CORES)
    spares = 3 if orb_count == 2 * CORES and kept == 2 else 0

    def to_partner(piece, m):
        if m == 0:
            return piece
        return lax.ppermute(piece, ("side", "orb"), [(flat_of(i), flat_of(i ^ m)) for i in range(group)])

    parts, stages = [], []
    for at in range(kept):
        *outs, pieces = filtered_pieces(at, place, orbitals, fetched[at], potential, pot_far, group, early)
        parts += [to_partner(piece, m) for piece, m in zip(outs, early)]
        stages.append(pieces)
    piece = (rows, part, width)
    shapes = [(kept, *piece)] * len(late) + [(kept, CORES, *piece)] * spares
    outs = small_call(
        functools.partial(late_kernel, kept, late),
        [jax.ShapeDtypeStruct(shape, jnp.float32) for shape in shapes],
        [SMEM] + [VMEM] * kept,
        *(place, *stages),
    )
    parts += [to_partner(piece, m) for piece, m in zip(outs, late)]
    spare = outs[len(late) :]
    total, devices = held * orb_count, slabs * orb_count
    cell_total = rows * part * width * devices
    block_shape = jax.ShapeDtypeStruct((total, rows * part, width), jnp.float32)
    message_shape = jax.ShapeDtypeStruct((devices, 1, total * total), jnp.float32)

    def exchanged(message):
        return lax.all_to_all(message, ALL, 0, 0)

    block, message = small_call(
        functools.partial(first_kernel, early, late, kept),
        [block_shape, message_shape],
        [SMEM] + [VMEM] * len(parts),
        *(place, *parts),
    )
    if spares:
        across = [(i, i ^ CORES) for i in range(orb_count)]
        cores = [(i, i ^ 1) for i in range(orb_count)]
        given = [
            spare[0],
            lax.ppermute(spare[1], "side", swap),
            lax.ppermute(spare[2], "orb", across),
        ]
        forward = small_call(
            forward_kernel, jax.ShapeDtypeStruct((CORES, kept, rows, part, width), jnp.float32), [SMEM, VMEM], place, block
        )
        given.append(lax.ppermute(forward, "orb", across))
        block_near = lax.ppermute(block, "orb", cores)
        table_shape = jax.ShapeDtypeStruct((total, LANES), jnp.float32)
        near = [lax.ppermute(piece, "orb", cores) for piece in given[:-1]]
        given = given + near + [lax.ppermute(given[-1], "orb", cores)]
        copies = exchanged(message)
        table, message = pl.pallas_call(
            functools.partial(table_kernel, cell_total),
            out_shape=[table_shape, message_shape],
            in_specs=[VMEM] * 2,
            out_specs=[VMEM, HBM],
            scratch_shapes=[pltpu.VMEM(message_shape.shape, jnp.float32), pltpu.SemaphoreType.DMA],
            compiler_params=pltpu.CompilerParams(vmem_limit_bytes=24 * 1024 * 1024),
        )(copies, block)
        return pl.pallas_call(
            functools.partial(last_kernel, cell_total),
            out_shape=jax.ShapeDtypeStruct((held, rows, cols, width), jnp.float32),
            in_specs=[SMEM] + [VMEM] * 4 + [HBM] * len(given),
            out_specs=HBM,
            scratch_shapes=[
                pltpu.VMEM((total, held, EIGHT, width), jnp.float32),
                pltpu.VMEM((held, rows, cols, width), jnp.float32),
                *(pltpu.VMEM(piece.shape, jnp.float32) for piece in given),
                pltpu.SemaphoreType.DMA((len(given),)),
                pltpu.SemaphoreType.DMA((2,)),
            ],
            compiler_params=pltpu.CompilerParams(vmem_limit_bytes=24 * 1024 * 1024),
        )(place, exchanged(message), table, block, block_near, *given)
    basis, message = small_call(
        functools.partial(second_kernel, cell_total), [block_shape, message_shape], [VMEM] * 2, exchanged(message), block
    )
    basis = small_call(functools.partial(third_kernel, cell_total), block_shape, [VMEM] * 2, exchanged(message), basis)
    basis = basis.reshape(total, rows, part, width)
    return lax.all_to_all(basis, "orb", split_axis=0, concat_axis=2, tiled=True)


def solution(mesh):
    slabs, orb_count = mesh.shape["dom"], mesh.shape["orb"]
    fine = Mesh(mesh.devices.reshape(slabs // 2, 2, orb_count), ALL)
    spec = P("orb", ("pair", "side"), None, None)
    return jax.shard_map(
        whole,
        mesh=fine,
        in_specs=(spec, P(("pair", "side"), None, None)),
        out_specs=spec,
        check_vma=False,
    )
```

```python
import functools

import jax
import jax.numpy as jnp
from jax import lax
from jax.experimental import pallas as pl
from jax.experimental.pallas import tpu as pltpu
from jax.sharding import Mesh
from jax.sharding import PartitionSpec as P

coefficients = (-49.0 / 18.0, 1.5, -0.15, 1.0 / 90.0)
spacing = 0.5
filter_centre = 23.0
filter_half = 23.0

REACH = 3
STEPS = 3
DEEP = REACH * STEPS
WIDE = REACH * (STEPS - 1)
EIGHT = 8
CORES = 2
WIDTH = 4
BLOCKS = 3
ALL = ("pair", "side", "orb")

VMEM = pl.BlockSpec(memory_space=pltpu.VMEM)
SMEM = pl.BlockSpec(memory_space=pltpu.SMEM)
HBM = pl.BlockSpec(memory_space=pltpu.HBM)

kinetic = -0.5 / (spacing * spacing)
taps = tuple(kinetic * c / filter_half for c in coefficients)
denominator = 180.0
whole_taps = tuple(round(denominator * c) for c in coefficients)
lane_scale = kinetic / filter_half / denominator
shift = (kinetic * 2.0 * coefficients[0] - filter_centre) / filter_half


def pack_kernel(place, orbitals, potential, *rest):
    outs, sems = rest[:-1], rest[-1]
    side, orb = place[0], place[2]
    kept, rows = orbitals.shape[0] // 2, orbitals.shape[1]
    part = outs[0].shape[1]
    columns = pl.ds(pl.multiple_of(orb * part, part), part)
    edge, shallow = pl.ds(side * (rows - DEEP), DEEP), pl.ds(side * (rows - WIDE), WIDE)
    sources = [potential.at[:, columns], potential.at[shallow, columns]]
    for at in range(kept):
        given, stays = orbitals.at[(1 - side) * kept + at], orbitals.at[side * kept + at]
        sources += [given.at[edge], given, stays.at[edge]]
    copies = [pltpu.make_async_copy(a, b, sems.at[i]) for i, (a, b) in enumerate(zip(sources, outs))]
    for copy in copies:
        copy.start()
    for copy in copies:
        copy.wait()


def packed(place, orbitals, potential, orb_count):
    held, rows, cols, width = orbitals.shape
    part = cols // orb_count
    shapes = [(rows, part, width), (WIDE, part, width)]
    shapes += [(DEEP, cols, width), (rows, cols, width), (DEEP, cols, width)] * (held // 2)
    return pl.pallas_call(
        pack_kernel,
        out_shape=[jax.ShapeDtypeStruct(shape, jnp.float32) for shape in shapes],
        in_specs=[SMEM, HBM, HBM],
        out_specs=[VMEM] * len(shapes),
        scratch_shapes=[pltpu.SemaphoreType.DMA((len(shapes),))],
        compiler_params=pltpu.CompilerParams(vmem_limit_bytes=16 * 1024 * 1024),
    )(place, *(pltpu.with_memory_space_constraint(array, pltpu.HBM) for array in (orbitals, potential)))


def join_kernel(swapped, slanted, straight, out):
    rows = swapped.shape[0]
    out[pl.ds(0, rows)] = swapped[...]
    out[pl.ds(rows, WIDE)] = slanted[...]
    out[pl.ds(rows + WIDE, WIDE)] = straight[...]


def split_dot(values, table):
    high = values.astype(jnp.bfloat16)
    rest = values - high.astype(jnp.float32)
    middle = rest.astype(jnp.bfloat16)
    low = (rest - middle.astype(jnp.float32)).astype(jnp.bfloat16)
    wide = jnp.concatenate([high, middle], axis=1)
    twice = jnp.concatenate([table, table], axis=0)
    return jnp.dot(wide, twice, preferred_element_type=jnp.float32) + jnp.dot(
        low, table, preferred_element_type=jnp.float32
    )


def filter_kernel(at, shares, early, place, own, swapped, slanted, straight, own_pot, lane_table, *rest):
    pot_far, outs = rest[:shares], rest[shares:-4]
    field, first, second, weight = rest[-4:]
    outs, sorted_pieces = outs[:-1], outs[-1]
    side, me, orb = place[0], place[1], place[2]
    rows, cols, _ = swapped.shape
    both = 2 * rows
    strips = cols // EIGHT

    def keep(ref, row, strip, value):
        ref[row, pl.ds(EIGHT * (strip + 1), EIGHT), :] = value
        if strip == 0:
            ref[row, pl.ds(cols + EIGHT, EIGHT), :] = value
        if strip == strips - 1:
            ref[row, pl.ds(0, EIGHT), :] = value

    def gather(load, count, row_to):
        def body(row, carry):
            for strip in range(strips):
                keep(field, row_to + row, strip, load(row, pl.ds(EIGHT * strip, EIGHT)))
            return carry

        lax.fori_loop(0, count, body, 0, unroll=3)

    kept = own.shape[0] // 2
    gather(lambda row, span: own[side * kept + at, row, span, :], rows, DEEP + side * rows)
    gather(lambda row, span: swapped[row, span, :], rows, DEEP + (1 - side) * rows)
    gather(lambda row, span: slanted[row, span, :], DEEP, side * (both + DEEP))
    gather(lambda row, span: straight[row, span, :], DEEP, (1 - side) * (both + DEEP))

    def weigh(values):
        return values * (1.0 / filter_half) + shift

    weight[pl.ds(WIDE + side * rows, rows)] = weigh(own_pot[...])
    part = cols // shares
    for apart, far in enumerate(pot_far):
        columns = pl.ds(pl.multiple_of((orb ^ apart) * part, part), part)
        weight[pl.ds(WIDE + (1 - side) * rows, rows), columns] = weigh(far[pl.ds(0, rows)])
        weight[pl.ds(side * (both + WIDE), WIDE), columns] = weigh(far[pl.ds(rows, WIDE)])
        weight[pl.ds((1 - side) * (both + WIDE), WIDE), columns] = weigh(far[pl.ds(rows + WIDE, WIDE)])

    def step(source, before, before_at, weight_at, total, store):
        width = source.shape[2]
        count = total // BLOCKS

        def body(index, carry):
            base = index * count
            centres = source[pl.ds(base + REACH, count), pl.ds(EIGHT, cols), :]
            along = split_dot(centres.reshape(count * cols, width), lane_table[...])
            for strip in range(strips):
                start = EIGHT * (strip + 1)
                window = [source[base + i, pl.ds(start, EIGHT), :] for i in range(count + 2 * REACH)]
                for i in range(count):
                    row = base + i
                    value = window[i + REACH] * weight[weight_at + row, pl.ds(EIGHT * strip, EIGHT), :]
                    from_lanes = i * cols + EIGHT * strip
                    value = value + along[from_lanes : from_lanes + EIGHT] * lane_scale
                    for k in range(1, REACH + 1):
                        near = window[i + REACH - k] + window[i + REACH + k]
                        near = near + (
                            source[row + REACH, pl.ds(start - k, EIGHT), :]
                            + source[row + REACH, pl.ds(start + k, EIGHT), :]
                        )
                        value = value + taps[k] * near
                    if before is not None:
                        value = 2.0 * value - before[before_at + row, pl.ds(start, EIGHT), :]
                    store(row, strip, value)
            return carry

        lax.fori_loop(0, BLOCKS, body, 0)

    step(field, None, 0, 0, both + 2 * WIDE, functools.partial(keep, first))
    step(first, field, 2 * REACH, REACH, both + 2 * REACH, functools.partial(keep, second))
    piece = sorted_pieces.shape[2]

    def store_out(row, strip, value):
        to = (EIGHT * strip) // piece
        half = row // rows
        sorted_pieces[2 * to + half, row - half * rows, pl.ds(EIGHT * strip - to * piece, EIGHT), :] = value

    step(second, first, 2 * REACH, 2 * REACH, both, store_out)
    for apart, out in zip(early, outs):
        out[...] = sorted_pieces[me ^ apart]


def late_kernel(stages, late, place, *refs):
    given, outs = refs[:stages], refs[stages:]
    side, me, orb = place[0], place[1], place[2]
    for stage, pieces in enumerate(given):
        for apart, out in zip(late, outs):
            out[stage] = pieces[me ^ apart]
        for index, out in enumerate(outs[len(late) :]):
            chip = orb // CORES ^ (1 if index < 2 else 0)
            for core in range(CORES):
                out[stage, core] = pieces[2 * (CORES * chip + core) + (side ^ (index % 2))]


def filtered_pieces(at, place, own, fetched, own_pot, pot_far, group, early):
    slanted, swapped, straight = fetched
    rows, cols, width = own.shape[1:]
    both = 2 * rows
    apart = jnp.arange(width)[:, None] - jnp.arange(width)[None, :]
    lane_table = jnp.zeros((width, width), jnp.float32)
    for k, tap in enumerate(whole_taps):
        hit = (apart % width == k) | (-apart % width == k)
        lane_table = jnp.where(hit, float(tap), lane_table)

    def scratch(margin):
        return pltpu.VMEM((both + 2 * margin, cols + 2 * EIGHT, width), jnp.float32)

    piece = (rows, 2 * cols // group, width)
    shapes = [piece] * len(early) + [(group, *piece)]
    return pl.pallas_call(
        functools.partial(filter_kernel, at, len(pot_far), early),
        out_shape=[jax.ShapeDtypeStruct(shape, jnp.float32) for shape in shapes],
        in_specs=[SMEM] + [VMEM] * (6 + len(pot_far)),
        out_specs=[VMEM] * len(shapes),
        scratch_shapes=[
            scratch(DEEP),
            scratch(WIDE),
            scratch(REACH),
            pltpu.VMEM((both + 2 * WIDE, cols, width), jnp.float32),
        ],
        compiler_params=pltpu.CompilerParams(vmem_limit_bytes=24 * 1024 * 1024),
    )(place, own, swapped, slanted, straight, own_pot, lane_table.astype(jnp.bfloat16), *pot_far)


LANES = 128


def exact_dot(a, b, contract=((1,), (0,))):
    return lax.dot_general(
        a, b, (contract, ((), ())), precision=lax.Precision.HIGHEST, preferred_element_type=jnp.float32
    )


def table_of(shape, test):
    rows = lax.broadcasted_iota(jnp.int32, shape, 0)
    columns = lax.broadcasted_iota(jnp.int32, shape, 1)
    return jnp.where(test(rows, columns), 1.0, 0.0).astype(jnp.float32)


def split(values):
    high = values.astype(jnp.bfloat16)
    rest = values - high.astype(jnp.float32)
    middle = rest.astype(jnp.bfloat16)
    return high, middle, (rest - middle.astype(jnp.float32)).astype(jnp.bfloat16)


def product(a, b, contract=((1,), (0,))):
    return lax.dot_general(a, b, (contract, ((), ())), preferred_element_type=jnp.float32)


def picked(values, table):
    chosen = table.astype(jnp.bfloat16)
    return sum(product(part, chosen) for part in split(values))


def gathered(table, values):
    chosen = table.astype(jnp.bfloat16)
    return sum(product(chosen, part) for part in split(values))


def gram_message(wide, total):
    tall = total * EIGHT
    high, middle, low = split(wide)
    joined, doubled = jnp.concatenate([high, middle], axis=1), jnp.concatenate([high, high], axis=1)
    mixed = product(doubled, jnp.concatenate([middle, low], axis=1), ((1,), (1,)))
    sums = product(joined, joined, ((1,), (1,))) + (mixed + mixed.T)
    sums = sums * table_of((tall, tall), lambda r, c: r % EIGHT == c % EIGHT)
    partial = gathered(table_of((total, tall), lambda r, c: c // EIGHT == r), sums)
    spread = picked(partial, table_of((tall, LANES), lambda r, c: r // EIGHT == c % total))
    per = LANES // total
    spread = spread * table_of((total, LANES), lambda r, c: c // total == r % per)
    return jnp.concatenate(
        [jnp.sum(spread[i * per : (i + 1) * per], axis=0, keepdims=True) for i in range(total // per)], axis=1
    )


def inverse_factor(copies, total, cell_total):
    row = jnp.sum(copies[...], axis=0) * (1.0 / cell_total)
    per = LANES // total
    wide = jnp.concatenate(
        [jnp.broadcast_to(row[:, i * LANES : (i + 1) * LANES], (per, LANES)) for i in range(total // per)], axis=0
    )
    wide = wide * table_of((total, LANES), lambda r, c: c // total == r % per)
    table = picked(wide, table_of((LANES, LANES), lambda r, c: r % total == c))
    table = table + table_of((total, LANES), lambda r, c: c - total == r)
    index = lax.broadcasted_iota(jnp.int32, (total, LANES), 0)
    for start in range(0, total, WIDTH):
        block = range(start, min(start + WIDTH, total))
        columns = {j: jnp.broadcast_to(table[:, j : j + 1], (total, LANES)) for j in block}
        rows = {j: table[j : j + 1, :] for j in block}
        reduced = table
        for j in block:
            value = columns[j][j : j + 1, :]
            scale = lax.rsqrt(value)
            scale = scale * (1.5 - 0.5 * value * scale * scale)
            factor, rows[j] = columns[j] * scale, rows[j] * scale
            for later in block:
                if later > j:
                    share = factor[later : later + 1, :]
                    columns[later] = columns[later] - factor * share
                    rows[later] = rows[later] - share * rows[j]
            reduced = reduced - factor * rows[j]
        for j in block:
            table = jnp.where(index == j, rows[j], table)
        table = jnp.where(index > block[-1], reduced, table)
    return table


def by_tiles(table, total):
    tall = total * EIGHT
    wide = picked(table, table_of((LANES, tall), lambda r, c: r - total == c // EIGHT))
    both = gathered(table_of((tall, total), lambda r, c: r // EIGHT == c), wide)
    return both * table_of((tall, tall), lambda r, c: r % EIGHT == c % EIGHT)


def side_by_side(ref):
    total, length, width = ref.shape
    tiles = [ref[:, start : start + EIGHT, :].reshape(total * EIGHT, width) for start in range(0, length, EIGHT)]
    return jnp.concatenate(tiles, axis=1)


def forward_kernel(place, block, out):
    kept, held = out.shape[1], 2 * out.shape[1]
    for flip in range(CORES):
        for at in range(kept):
            out[flip, at] = block[(place[2] ^ flip) * held + (place[0] ^ 1) * kept + at].reshape(out.shape[2:])


def first_kernel(early, late, kept, place, *refs):
    given, (block, message) = refs[:-2], refs[-2:]
    me, shape = place[1], block.shape[1:]
    for at in range(kept):
        for index, apart in enumerate(early):
            block[(me ^ apart) * kept + at] = given[at * len(early) + index][...].reshape(shape)
        for index, apart in enumerate(late):
            block[(me ^ apart) * kept + at] = given[kept * len(early) + index][at].reshape(shape)
    message[...] = jnp.broadcast_to(gram_message(side_by_side(block), block.shape[0])[None], message.shape)


def applied(table, block):
    total = block.shape[0]
    tall = total * EIGHT
    high, middle, low = split(by_tiles(table, total))
    values_high, values_middle, values_low = split(side_by_side(block))
    left = jnp.concatenate(
        [jnp.concatenate([high, high], axis=1), jnp.concatenate([middle, middle], axis=1)], axis=0
    )
    main = product(left, jnp.concatenate([values_high, values_middle], axis=0))
    rest = product(jnp.concatenate([low, high], axis=1), jnp.concatenate([values_high, values_low], axis=0))
    return main[:tall] + (main[tall:] + rest)


def put(wide, basis):
    total, length, width = basis.shape
    for t in range(length // EIGHT):
        piece = wide[:, t * width : (t + 1) * width].reshape(total, EIGHT, width)
        basis[:, EIGHT * t : EIGHT * (t + 1), :] = piece


def second_kernel(cell_total, copies, block, basis, message):
    total = block.shape[0]
    wide = applied(inverse_factor(copies, total, cell_total), block)
    put(wide, basis)
    message[...] = jnp.broadcast_to(gram_message(wide, total)[None], message.shape)


def third_kernel(cell_total, copies, block, basis):
    put(applied(inverse_factor(copies, block.shape[0], cell_total), block), basis)


def table_kernel(cell_total, copies, block, table_out, message_far, message, sem):
    total = block.shape[0]
    table = inverse_factor(copies, total, cell_total)
    table_out[...] = table
    message[...] = jnp.broadcast_to(gram_message(applied(table, block), total)[None], message.shape)
    leave = pltpu.make_async_copy(message, message_far, sem)
    leave.start()
    leave.wait()


def last_kernel(cell_total, place, copies, table, block, block_near, *refs):
    count = (len(refs) - 5) // 2
    far, (out_far, splats, out), spares = refs[:count], refs[count : count + 3], refs[count + 3 : 2 * count + 3]
    sems, sems_out = refs[2 * count + 3 :]
    total, length, width = block.shape
    held, rows = out.shape[:2]
    part = length // rows
    side, orb = place[0], place[2]
    chip = orb // CORES
    fetches = [pltpu.make_async_copy(a, b, sems.at[i]) for i, (a, b) in enumerate(zip(far, spares))]
    for fetch in fetches:
        fetch.start()
    second = inverse_factor(copies, total, cell_total)
    pick = table_of((LANES, total), lambda r, c: r - total == c)
    both = exact_dot(picked(second, pick), picked(table[...], pick))
    own = gathered(table_of((held * EIGHT, total), lambda r, c: orb * held + r // EIGHT == c), both)
    wide = picked(own, table_of((total, total * width), lambda r, c: c // width == r))
    for orbital in range(total):
        splats[orbital] = wide[:, orbital * width : (orbital + 1) * width].reshape(held, EIGHT, width)

    def write(sources, first_column):
        def body(row, carry):
            for strip in range(part // EIGHT):
                sums = None
                for orbital, load in sources:
                    values = load(row, strip)
                    terms = [splats[orbital, i] * values for i in range(held)]
                    sums = terms if sums is None else [a + b for a, b in zip(sums, terms)]
                column = pl.multiple_of(first_column + strip * EIGHT, EIGHT)
                for i in range(held):
                    out[i, row, pl.ds(column, EIGHT), :] = sums[i]
            return carry

        lax.fori_loop(0, rows, body, 0, unroll=2)

    def at(ref, index):
        def load(row, strip):
            return ref[index, pl.ds(pl.multiple_of(row * part + strip * EIGHT, EIGHT), EIGHT), :]

        return load

    write([(j, at(block, j)) for j in range(total)], orb * part)
    write([(j, at(block_near, j)) for j in range(total)], (orb ^ 1) * part)

    def leave(which, index):
        columns = pl.ds(pl.multiple_of(which * CORES * part, EIGHT), CORES * part)
        return pltpu.make_async_copy(out.at[:, :, columns], out_far.at[:, :, columns], sems_out.at[index])

    leave(chip, 0).start()
    for fetch in fetches:
        fetch.wait()

    def piece_at(ref, first, second):
        return lambda row, strip: ref[first, second, row, pl.ds(strip * EIGHT, EIGHT), :]

    kinds, kept = count // 2, held // 2
    core = orb % CORES
    for turn in range(CORES):
        share = core ^ turn
        sources = []
        for flip in range(2):
            for kind in range(kinds - 1):
                quad = (orb ^ CORES if kind // 2 else orb) ^ flip
                for stage in range(kept):
                    orbital = quad * held + (side ^ (kind % 2)) * kept + stage
                    sources.append((orbital, piece_at(spares[flip * kinds + kind], stage, share)))
            quad = orb ^ CORES ^ turn ^ flip
            for stage in range(kept):
                orbital = quad * held + (side ^ 1) * kept + stage
                sources.append((orbital, piece_at(spares[turn * kinds + kinds - 1], flip, stage)))
        write(sources, ((1 - chip) * CORES + share) * part)
    leave(1 - chip, 1).start()
    leave(chip, 0).wait()
    leave(1 - chip, 1).wait()


def small_call(kernel, out_shape, specs, *args):
    return pl.pallas_call(
        kernel,
        out_shape=out_shape,
        in_specs=specs,
        out_specs=jax.tree.map(lambda _: VMEM, out_shape),
        compiler_params=pltpu.CompilerParams(vmem_limit_bytes=24 * 1024 * 1024),
    )(*args)


def whole(orbitals, potential):
    pair_count, orb_count = lax.axis_size("pair"), lax.axis_size("orb")
    slabs = 2 * pair_count
    side, orb = lax.axis_index("side"), lax.axis_index("orb")
    held, rows, cols, width = orbitals.shape
    kept = held // 2
    part = cols // orb_count

    slant = [(i, (i + (1 if i % 2 else -1)) % slabs) for i in range(slabs)]
    ahead = [(i, (i + (2 if i % 2 else -2)) % slabs) for i in range(slabs)]
    swap = [(0, 1), (1, 0)]
    slab_axes = ("pair", "side")

    group = 2 * orb_count
    me = 2 * orb + side

    def flat_of(index):
        return (index % 2) * orb_count + index // 2

    place = jnp.stack([side, me, orb]).astype(jnp.int32)
    mine, edge, *sent = packed(place, orbitals, potential, orb_count)

    pieces = [
        lax.ppermute(mine, "side", swap),
        lax.ppermute(edge, slab_axes, slant),
        lax.ppermute(edge, slab_axes, ahead),
    ]
    joined = pl.pallas_call(
        join_kernel,
        out_shape=jax.ShapeDtypeStruct((rows + 2 * WIDE, part, width), jnp.float32),
        in_specs=[VMEM] * 3,
        out_specs=VMEM,
        compiler_params=pltpu.CompilerParams(vmem_limit_bytes=16 * 1024 * 1024),
    )(*pieces)
    pot_far = [joined] + [
        lax.ppermute(joined, "orb", [(i, i ^ m) for i in range(orb_count)]) for m in range(1, orb_count)
    ]

    fetched = []
    for at in range(kept):
        swapped = lax.ppermute(sent[3 * at + 1], "side", swap)
        slanted = lax.ppermute(sent[3 * at], slab_axes, slant)
        straight = lax.ppermute(sent[3 * at + 2], slab_axes, ahead)
        fetched.append((slanted, swapped, straight))

    early = tuple(sorted((m for m in range(1, group) if m != CORES), key=lambda m: (m < 2 * CORES, -(m % 2), m)))
    late = (0, CORES)
    spares = 3 if orb_count == 2 * CORES and kept == 2 else 0

    def to_partner(piece, m):
        if m == 0:
            return piece
        return lax.ppermute(piece, ("side", "orb"), [(flat_of(i), flat_of(i ^ m)) for i in range(group)])

    parts, stages = [], []
    for at in range(kept):
        *outs, pieces = filtered_pieces(at, place, orbitals, fetched[at], potential, pot_far, group, early)
        parts += [to_partner(piece, m) for piece, m in zip(outs, early)]
        stages.append(pieces)
    piece = (rows, part, width)
    shapes = [(kept, *piece)] * len(late) + [(kept, CORES, *piece)] * spares
    outs = small_call(
        functools.partial(late_kernel, kept, late),
        [jax.ShapeDtypeStruct(shape, jnp.float32) for shape in shapes],
        [SMEM] + [VMEM] * kept,
        *(place, *stages),
    )
    parts += [to_partner(piece, m) for piece, m in zip(outs, late)]
    spare = outs[len(late) :]
    total, devices = held * orb_count, slabs * orb_count
    cell_total = rows * part * width * devices
    block_shape = jax.ShapeDtypeStruct((total, rows * part, width), jnp.float32)
    message_shape = jax.ShapeDtypeStruct((devices, 1, total * total), jnp.float32)

    def exchanged(message):
        return lax.all_to_all(message, ALL, 0, 0)

    block, message = small_call(
        functools.partial(first_kernel, early, late, kept),
        [block_shape, message_shape],
        [SMEM] + [VMEM] * len(parts),
        *(place, *parts),
    )
    if spares:
        across = [(i, i ^ CORES) for i in range(orb_count)]
        cores = [(i, i ^ 1) for i in range(orb_count)]
        given = [
            spare[0],
            lax.ppermute(spare[1], "side", swap),
            lax.ppermute(spare[2], "orb", across),
        ]
        forward = small_call(
            forward_kernel, jax.ShapeDtypeStruct((CORES, kept, rows, part, width), jnp.float32), [SMEM, VMEM], place, block
        )
        given.append(lax.ppermute(forward, "orb", across))
        block_near = lax.ppermute(block, "orb", cores)
        table_shape = jax.ShapeDtypeStruct((total, LANES), jnp.float32)
        near = [lax.ppermute(piece, "orb", cores) for piece in given[:-1]]
        given = given + near + [lax.ppermute(given[-1], "orb", cores)]
        copies = exchanged(message)
        table, message = pl.pallas_call(
            functools.partial(table_kernel, cell_total),
            out_shape=[table_shape, message_shape],
            in_specs=[VMEM] * 2,
            out_specs=[VMEM, HBM],
            scratch_shapes=[pltpu.VMEM(message_shape.shape, jnp.float32), pltpu.SemaphoreType.DMA],
            compiler_params=pltpu.CompilerParams(vmem_limit_bytes=24 * 1024 * 1024),
        )(copies, block)
        return pl.pallas_call(
            functools.partial(last_kernel, cell_total),
            out_shape=jax.ShapeDtypeStruct((held, rows, cols, width), jnp.float32),
            in_specs=[SMEM] + [VMEM] * 4 + [HBM] * len(given),
            out_specs=HBM,
            scratch_shapes=[
                pltpu.VMEM((total, held, EIGHT, width), jnp.float32),
                pltpu.VMEM((held, rows, cols, width), jnp.float32),
                *(pltpu.VMEM(piece.shape, jnp.float32) for piece in given),
                pltpu.SemaphoreType.DMA((len(given),)),
                pltpu.SemaphoreType.DMA((2,)),
            ],
            compiler_params=pltpu.CompilerParams(vmem_limit_bytes=24 * 1024 * 1024),
        )(place, exchanged(message), table, block, block_near, *given)
    basis, message = small_call(
        functools.partial(second_kernel, cell_total), [block_shape, message_shape], [VMEM] * 2, exchanged(message), block
    )
    basis = small_call(functools.partial(third_kernel, cell_total), block_shape, [VMEM] * 2, exchanged(message), basis)
    basis = basis.reshape(total, rows, part, width)
    return lax.all_to_all(basis, "orb", split_axis=0, concat_axis=2, tiled=True)


def solution(mesh):
    slabs, orb_count = mesh.shape["dom"], mesh.shape["orb"]
    fine = Mesh(mesh.devices.reshape(slabs // 2, 2, orb_count), ALL)
    spec = P("orb", ("pair", "side"), None, None)
    return jax.shard_map(
        whole,
        mesh=fine,
        in_specs=(spec, P(("pair", "side"), None, None)),
        out_specs=spec,
        check_vma=False,
    )
```

```python
import functools

import jax
import jax.numpy as jnp
from jax import lax
from jax.experimental import pallas as pl
from jax.experimental.pallas import tpu as pltpu
from jax.sharding import Mesh
from jax.sharding import PartitionSpec as P

coefficients = (-49.0 / 18.0, 1.5, -0.15, 1.0 / 90.0)
spacing = 0.5
filter_centre = 23.0
filter_half = 23.0

REACH = 3
STEPS = 3
DEEP = REACH * STEPS
WIDE = REACH * (STEPS - 1)
EIGHT = 8
CORES = 2
WIDTH = 4
BLOCKS = 3
ALL = ("pair", "side", "orb")

VMEM = pl.BlockSpec(memory_space=pltpu.VMEM)
SMEM = pl.BlockSpec(memory_space=pltpu.SMEM)
HBM = pl.BlockSpec(memory_space=pltpu.HBM)

kinetic = -0.5 / (spacing * spacing)
taps = tuple(kinetic * c / filter_half for c in coefficients)
denominator = 180.0
whole_taps = tuple(round(denominator * c) for c in coefficients)
lane_scale = kinetic / filter_half / denominator
shift = (kinetic * 2.0 * coefficients[0] - filter_centre) / filter_half


def pack_kernel(place, orbitals, potential, *rest):
    outs, sems = rest[:-1], rest[-1]
    side, orb = place[0], place[2]
    kept, rows = orbitals.shape[0] // 2, orbitals.shape[1]
    part = outs[0].shape[1]
    columns = pl.ds(pl.multiple_of(orb * part, part), part)
    edge, shallow = pl.ds(side * (rows - DEEP), DEEP), pl.ds(side * (rows - WIDE), WIDE)
    sources = [potential.at[:, columns], potential.at[shallow, columns]]
    for at in range(kept):
        given, stays = orbitals.at[(1 - side) * kept + at], orbitals.at[side * kept + at]
        sources += [given.at[edge], given, stays.at[edge]]
    copies = [pltpu.make_async_copy(a, b, sems.at[i]) for i, (a, b) in enumerate(zip(sources, outs))]
    for copy in copies:
        copy.start()
    for copy in copies:
        copy.wait()


def packed(place, orbitals, potential, orb_count):
    held, rows, cols, width = orbitals.shape
    part = cols // orb_count
    shapes = [(rows, part, width), (WIDE, part, width)]
    shapes += [(DEEP, cols, width), (rows, cols, width), (DEEP, cols, width)] * (held // 2)
    return pl.pallas_call(
        pack_kernel,
        out_shape=[jax.ShapeDtypeStruct(shape, jnp.float32) for shape in shapes],
        in_specs=[SMEM, HBM, HBM],
        out_specs=[VMEM] * len(shapes),
        scratch_shapes=[pltpu.SemaphoreType.DMA((len(shapes),))],
        compiler_params=pltpu.CompilerParams(vmem_limit_bytes=16 * 1024 * 1024),
    )(place, *(pltpu.with_memory_space_constraint(array, pltpu.HBM) for array in (orbitals, potential)))


def join_kernel(swapped, slanted, straight, out):
    rows = swapped.shape[0]
    out[pl.ds(0, rows)] = swapped[...]
    out[pl.ds(rows, WIDE)] = slanted[...]
    out[pl.ds(rows + WIDE, WIDE)] = straight[...]


def split_dot(values, table):
    high = values.astype(jnp.bfloat16)
    rest = values - high.astype(jnp.float32)
    middle = rest.astype(jnp.bfloat16)
    low = (rest - middle.astype(jnp.float32)).astype(jnp.bfloat16)
    wide = jnp.concatenate([high, middle], axis=1)
    twice = jnp.concatenate([table, table], axis=0)
    return jnp.dot(wide, twice, preferred_element_type=jnp.float32) + jnp.dot(
        low, table, preferred_element_type=jnp.float32
    )


def filter_kernel(at, shares, early, place, own, swapped, slanted, straight, own_pot, lane_table, *rest):
    pot_far, outs = rest[:shares], rest[shares:-4]
    field, first, second, weight = rest[-4:]
    outs, sorted_pieces = outs[:-1], outs[-1]
    side, me, orb = place[0], place[1], place[2]
    rows, cols, _ = swapped.shape
    both = 2 * rows
    strips = cols // EIGHT

    def keep(ref, row, strip, value):
        ref[row, pl.ds(EIGHT * (strip + 1), EIGHT), :] = value
        if strip == 0:
            ref[row, pl.ds(cols + EIGHT, EIGHT), :] = value
        if strip == strips - 1:
            ref[row, pl.ds(0, EIGHT), :] = value

    def gather(load, count, row_to):
        def body(row, carry):
            for strip in range(strips):
                keep(field, row_to + row, strip, load(row, pl.ds(EIGHT * strip, EIGHT)))
            return carry

        lax.fori_loop(0, count, body, 0, unroll=3)

    kept = own.shape[0] // 2
    gather(lambda row, span: own[side * kept + at, row, span, :], rows, DEEP + side * rows)
    gather(lambda row, span: swapped[row, span, :], rows, DEEP + (1 - side) * rows)
    gather(lambda row, span: slanted[row, span, :], DEEP, side * (both + DEEP))
    gather(lambda row, span: straight[row, span, :], DEEP, (1 - side) * (both + DEEP))

    def weigh(values):
        return values * (1.0 / filter_half) + shift

    weight[pl.ds(WIDE + side * rows, rows)] = weigh(own_pot[...])
    part = cols // shares
    for apart, far in enumerate(pot_far):
        columns = pl.ds(pl.multiple_of((orb ^ apart) * part, part), part)
        weight[pl.ds(WIDE + (1 - side) * rows, rows), columns] = weigh(far[pl.ds(0, rows)])
        weight[pl.ds(side * (both + WIDE), WIDE), columns] = weigh(far[pl.ds(rows, WIDE)])
        weight[pl.ds((1 - side) * (both + WIDE), WIDE), columns] = weigh(far[pl.ds(rows + WIDE, WIDE)])

    def step(source, before, before_at, weight_at, total, store):
        width = source.shape[2]
        count = total // BLOCKS

        def body(index, carry):
            base = index * count
            centres = source[pl.ds(base + REACH, count), pl.ds(EIGHT, cols), :]
            along = split_dot(centres.reshape(count * cols, width), lane_table[...])
            for strip in range(strips):
                start = EIGHT * (strip + 1)
                window = [source[base + i, pl.ds(start, EIGHT), :] for i in range(count + 2 * REACH)]
                for i in range(count):
                    row = base + i
                    value = window[i + REACH] * weight[weight_at + row, pl.ds(EIGHT * strip, EIGHT), :]
                    from_lanes = i * cols + EIGHT * strip
                    value = value + along[from_lanes : from_lanes + EIGHT] * lane_scale
                    for k in range(1, REACH + 1):
                        near = window[i + REACH - k] + window[i + REACH + k]
                        near = near + (
                            source[row + REACH, pl.ds(start - k, EIGHT), :]
                            + source[row + REACH, pl.ds(start + k, EIGHT), :]
                        )
                        value = value + taps[k] * near
                    if before is not None:
                        value = 2.0 * value - before[before_at + row, pl.ds(start, EIGHT), :]
                    store(row, strip, value)
            return carry

        lax.fori_loop(0, BLOCKS, body, 0)

    step(field, None, 0, 0, both + 2 * WIDE, functools.partial(keep, first))
    step(first, field, 2 * REACH, REACH, both + 2 * REACH, functools.partial(keep, second))
    piece = sorted_pieces.shape[2]

    def store_out(row, strip, value):
        to = (EIGHT * strip) // piece
        half = row // rows
        sorted_pieces[2 * to + half, row - half * rows, pl.ds(EIGHT * strip - to * piece, EIGHT), :] = value

    step(second, first, 2 * REACH, 2 * REACH, both, store_out)
    for apart, out in zip(early, outs):
        out[...] = sorted_pieces[me ^ apart]


def late_kernel(stages, late, place, *refs):
    given, outs = refs[:stages], refs[stages:]
    side, me, orb = place[0], place[1], place[2]
    for stage, pieces in enumerate(given):
        for apart, out in zip(late, outs):
            out[stage] = pieces[me ^ apart]
        for index, out in enumerate(outs[len(late) :]):
            chip = orb // CORES ^ (1 if index < 2 else 0)
            for core in range(CORES):
                out[stage, core] = pieces[2 * (CORES * chip + core) + (side ^ (index % 2))]


def filtered_pieces(at, place, own, fetched, own_pot, pot_far, group, early):
    slanted, swapped, straight = fetched
    rows, cols, width = own.shape[1:]
    both = 2 * rows
    apart = jnp.arange(width)[:, None] - jnp.arange(width)[None, :]
    lane_table = jnp.zeros((width, width), jnp.float32)
    for k, tap in enumerate(whole_taps):
        hit = (apart % width == k) | (-apart % width == k)
        lane_table = jnp.where(hit, float(tap), lane_table)

    def scratch(margin):
        return pltpu.VMEM((both + 2 * margin, cols + 2 * EIGHT, width), jnp.float32)

    piece = (rows, 2 * cols // group, width)
    shapes = [piece] * len(early) + [(group, *piece)]
    return pl.pallas_call(
        functools.partial(filter_kernel, at, len(pot_far), early),
        out_shape=[jax.ShapeDtypeStruct(shape, jnp.float32) for shape in shapes],
        in_specs=[SMEM] + [VMEM] * (6 + len(pot_far)),
        out_specs=[VMEM] * len(shapes),
        scratch_shapes=[
            scratch(DEEP),
            scratch(WIDE),
            scratch(REACH),
            pltpu.VMEM((both + 2 * WIDE, cols, width), jnp.float32),
        ],
        compiler_params=pltpu.CompilerParams(vmem_limit_bytes=24 * 1024 * 1024),
    )(place, own, swapped, slanted, straight, own_pot, lane_table.astype(jnp.bfloat16), *pot_far)


LANES = 128


def exact_dot(a, b, contract=((1,), (0,))):
    return lax.dot_general(
        a, b, (contract, ((), ())), precision=lax.Precision.HIGHEST, preferred_element_type=jnp.float32
    )


def table_of(shape, test):
    rows = lax.broadcasted_iota(jnp.int32, shape, 0)
    columns = lax.broadcasted_iota(jnp.int32, shape, 1)
    return jnp.where(test(rows, columns), 1.0, 0.0).astype(jnp.float32)


def split(values):
    high = values.astype(jnp.bfloat16)
    rest = values - high.astype(jnp.float32)
    middle = rest.astype(jnp.bfloat16)
    return high, middle, (rest - middle.astype(jnp.float32)).astype(jnp.bfloat16)


def product(a, b, contract=((1,), (0,))):
    return lax.dot_general(a, b, (contract, ((), ())), preferred_element_type=jnp.float32)


def picked(values, table):
    chosen = table.astype(jnp.bfloat16)
    return sum(product(part, chosen) for part in split(values))


def gathered(table, values):
    chosen = table.astype(jnp.bfloat16)
    return sum(product(chosen, part) for part in split(values))


def gram_message(wide, total):
    tall = total * EIGHT
    high, middle, low = split(wide)
    joined, doubled = jnp.concatenate([high, middle], axis=1), jnp.concatenate([high, high], axis=1)
    mixed = product(doubled, jnp.concatenate([middle, low], axis=1), ((1,), (1,)))
    sums = product(joined, joined, ((1,), (1,))) + (mixed + mixed.T)
    sums = sums * table_of((tall, tall), lambda r, c: r % EIGHT == c % EIGHT)
    partial = gathered(table_of((total, tall), lambda r, c: c // EIGHT == r), sums)
    spread = picked(partial, table_of((tall, LANES), lambda r, c: r // EIGHT == c % total))
    per = LANES // total
    spread = spread * table_of((total, LANES), lambda r, c: c // total == r % per)
    return jnp.concatenate(
        [jnp.sum(spread[i * per : (i + 1) * per], axis=0, keepdims=True) for i in range(total // per)], axis=1
    )


def inverse_factor(copies, total, cell_total):
    row = jnp.sum(copies[...], axis=0) * (1.0 / cell_total)
    per = LANES // total
    wide = jnp.concatenate(
        [jnp.broadcast_to(row[:, i * LANES : (i + 1) * LANES], (per, LANES)) for i in range(total // per)], axis=0
    )
    wide = wide * table_of((total, LANES), lambda r, c: c // total == r % per)
    table = picked(wide, table_of((LANES, LANES), lambda r, c: r % total == c))
    table = table + table_of((total, LANES), lambda r, c: c - total == r)
    index = lax.broadcasted_iota(jnp.int32, (total, LANES), 0)
    for start in range(0, total, WIDTH):
        block = range(start, min(start + WIDTH, total))
        columns = {j: jnp.broadcast_to(table[:, j : j + 1], (total, LANES)) for j in block}
        rows = {j: table[j : j + 1, :] for j in block}
        reduced = table
        for j in block:
            value = columns[j][j : j + 1, :]
            scale = lax.rsqrt(value)
            scale = scale * (1.5 - 0.5 * value * scale * scale)
            factor, rows[j] = columns[j] * scale, rows[j] * scale
            for later in block:
                if later > j:
                    share = factor[later : later + 1, :]
                    columns[later] = columns[later] - factor * share
                    rows[later] = rows[later] - share * rows[j]
            reduced = reduced - factor * rows[j]
        for j in block:
            table = jnp.where(index == j, rows[j], table)
        table = jnp.where(index > block[-1], reduced, table)
    return table


def by_tiles(table, total):
    tall = total * EIGHT
    wide = picked(table, table_of((LANES, tall), lambda r, c: r - total == c // EIGHT))
    both = gathered(table_of((tall, total), lambda r, c: r // EIGHT == c), wide)
    return both * table_of((tall, tall), lambda r, c: r % EIGHT == c % EIGHT)


def side_by_side(ref):
    total, length, width = ref.shape
    tiles = [ref[:, start : start + EIGHT, :].reshape(total * EIGHT, width) for start in range(0, length, EIGHT)]
    return jnp.concatenate(tiles, axis=1)


def forward_kernel(place, block, out):
    kept, held = out.shape[1], 2 * out.shape[1]
    for flip in range(CORES):
        for at in range(kept):
            out[flip, at] = block[(place[2] ^ flip) * held + (place[0] ^ 1) * kept + at].reshape(out.shape[2:])


def first_kernel(early, late, kept, place, *refs):
    given, (block, message) = refs[:-2], refs[-2:]
    me, shape = place[1], block.shape[1:]
    for at in range(kept):
        for index, apart in enumerate(early):
            block[(me ^ apart) * kept + at] = given[at * len(early) + index][...].reshape(shape)
        for index, apart in enumerate(late):
            block[(me ^ apart) * kept + at] = given[kept * len(early) + index][at].reshape(shape)
    message[...] = jnp.broadcast_to(gram_message(side_by_side(block), block.shape[0])[None], message.shape)


def applied(table, block):
    total = block.shape[0]
    tall = total * EIGHT
    high, middle, low = split(by_tiles(table, total))
    values_high, values_middle, values_low = split(side_by_side(block))
    left = jnp.concatenate(
        [jnp.concatenate([high, high], axis=1), jnp.concatenate([middle, middle], axis=1)], axis=0
    )
    main = product(left, jnp.concatenate([values_high, values_middle], axis=0))
    rest = product(jnp.concatenate([low, high], axis=1), jnp.concatenate([values_high, values_low], axis=0))
    return main[:tall] + (main[tall:] + rest)


def put(wide, basis):
    total, length, width = basis.shape
    for t in range(length // EIGHT):
        piece = wide[:, t * width : (t + 1) * width].reshape(total, EIGHT, width)
        basis[:, EIGHT * t : EIGHT * (t + 1), :] = piece


def second_kernel(cell_total, copies, block, basis, message):
    total = block.shape[0]
    wide = applied(inverse_factor(copies, total, cell_total), block)
    put(wide, basis)
    message[...] = jnp.broadcast_to(gram_message(wide, total)[None], message.shape)


def third_kernel(cell_total, copies, block, basis):
    put(applied(inverse_factor(copies, block.shape[0], cell_total), block), basis)


def table_kernel(cell_total, copies, block, table_out, message):
    total = block.shape[0]
    table = inverse_factor(copies, total, cell_total)
    table_out[...] = table
    message[...] = jnp.broadcast_to(gram_message(applied(table, block), total)[None], message.shape)


def last_kernel(cell_total, place, copies, table, block, block_near, *refs):
    count = (len(refs) - 5) // 2
    far, (out_far, splats, out), spares = refs[:count], refs[count : count + 3], refs[count + 3 : 2 * count + 3]
    sems, sems_out = refs[2 * count + 3 :]
    total, length, width = block.shape
    held, rows = out.shape[:2]
    part = length // rows
    side, orb = place[0], place[2]
    chip = orb // CORES
    fetches = [pltpu.make_async_copy(a, b, sems.at[i]) for i, (a, b) in enumerate(zip(far, spares))]
    for fetch in fetches:
        fetch.start()
    second = inverse_factor(copies, total, cell_total)
    pick = table_of((LANES, total), lambda r, c: r - total == c)
    both = exact_dot(picked(second, pick), picked(table[...], pick))
    own = gathered(table_of((held * EIGHT, total), lambda r, c: orb * held + r // EIGHT == c), both)
    wide = picked(own, table_of((total, total * width), lambda r, c: c // width == r))
    for orbital in range(total):
        splats[orbital] = wide[:, orbital * width : (orbital + 1) * width].reshape(held, EIGHT, width)

    def write(sources, first_column):
        def body(row, carry):
            for strip in range(part // EIGHT):
                sums = None
                for orbital, load in sources:
                    values = load(row, strip)
                    terms = [splats[orbital, i] * values for i in range(held)]
                    sums = terms if sums is None else [a + b for a, b in zip(sums, terms)]
                column = pl.multiple_of(first_column + strip * EIGHT, EIGHT)
                for i in range(held):
                    out[i, row, pl.ds(column, EIGHT), :] = sums[i]
            return carry

        lax.fori_loop(0, rows, body, 0, unroll=2)

    def at(ref, index):
        def load(row, strip):
            return ref[index, pl.ds(pl.multiple_of(row * part + strip * EIGHT, EIGHT), EIGHT), :]

        return load

    write([(j, at(block, j)) for j in range(total)], orb * part)
    write([(j, at(block_near, j)) for j in range(total)], (orb ^ 1) * part)

    def leave(which, index):
        columns = pl.ds(pl.multiple_of(which * CORES * part, EIGHT), CORES * part)
        return pltpu.make_async_copy(out.at[:, :, columns], out_far.at[:, :, columns], sems_out.at[index])

    leave(chip, 0).start()
    for fetch in fetches:
        fetch.wait()

    def piece_at(ref, first, second):
        return lambda row, strip: ref[first, second, row, pl.ds(strip * EIGHT, EIGHT), :]

    kinds, kept = count // 2, held // 2
    core = orb % CORES
    for turn in range(CORES):
        share = core ^ turn
        sources = []
        for flip in range(2):
            for kind in range(kinds - 1):
                quad = (orb ^ CORES if kind // 2 else orb) ^ flip
                for stage in range(kept):
                    orbital = quad * held + (side ^ (kind % 2)) * kept + stage
                    sources.append((orbital, piece_at(spares[flip * kinds + kind], stage, share)))
            quad = orb ^ CORES ^ turn ^ flip
            for stage in range(kept):
                orbital = quad * held + (side ^ 1) * kept + stage
                sources.append((orbital, piece_at(spares[turn * kinds + kinds - 1], flip, stage)))
        write(sources, ((1 - chip) * CORES + share) * part)
    leave(1 - chip, 1).start()
    leave(chip, 0).wait()
    leave(1 - chip, 1).wait()


def small_call(kernel, out_shape, specs, *args):
    return pl.pallas_call(
        kernel,
        out_shape=out_shape,
        in_specs=specs,
        out_specs=jax.tree.map(lambda _: VMEM, out_shape),
        compiler_params=pltpu.CompilerParams(vmem_limit_bytes=24 * 1024 * 1024),
    )(*args)


def whole(orbitals, potential):
    pair_count, orb_count = lax.axis_size("pair"), lax.axis_size("orb")
    slabs = 2 * pair_count
    side, orb = lax.axis_index("side"), lax.axis_index("orb")
    held, rows, cols, width = orbitals.shape
    kept = held // 2
    part = cols // orb_count

    slant = [(i, (i + (1 if i % 2 else -1)) % slabs) for i in range(slabs)]
    ahead = [(i, (i + (2 if i % 2 else -2)) % slabs) for i in range(slabs)]
    swap = [(0, 1), (1, 0)]
    slab_axes = ("pair", "side")

    group = 2 * orb_count
    me = 2 * orb + side

    def flat_of(index):
        return (index % 2) * orb_count + index // 2

    place = jnp.stack([side, me, orb]).astype(jnp.int32)
    mine, edge, *sent = packed(place, orbitals, potential, orb_count)

    pieces = [lax.ppermute(mine, "side", swap)]
    pieces += [lax.ppermute(edge, slab_axes, slant), lax.ppermute(edge, slab_axes, ahead)]
    joined = pl.pallas_call(
        join_kernel,
        out_shape=jax.ShapeDtypeStruct((rows + 2 * WIDE, part, width), jnp.float32),
        in_specs=[VMEM] * 3,
        out_specs=VMEM,
        compiler_params=pltpu.CompilerParams(vmem_limit_bytes=16 * 1024 * 1024),
    )(*pieces)
    pot_far = [joined] + [
        lax.ppermute(joined, "orb", [(i, i ^ m) for i in range(orb_count)]) for m in range(1, orb_count)
    ]

    fetched = []
    for at in range(kept):
        swapped = lax.ppermute(sent[3 * at + 1], "side", swap)
        slanted = lax.ppermute(sent[3 * at], slab_axes, slant)
        straight = lax.ppermute(sent[3 * at + 2], slab_axes, ahead)
        fetched.append((slanted, swapped, straight))

    early = tuple(sorted((m for m in range(1, group) if m != CORES), key=lambda m: (m < 2 * CORES, -(m % 2), m)))
    late = (0, CORES)
    spares = 3 if orb_count == 2 * CORES and kept == 2 else 0

    def to_partner(piece, m):
        if m == 0:
            return piece
        return lax.ppermute(piece, ("side", "orb"), [(flat_of(i), flat_of(i ^ m)) for i in range(group)])

    parts, stages = [], []
    for at in range(kept):
        *outs, pieces = filtered_pieces(at, place, orbitals, fetched[at], potential, pot_far, group, early)
        parts += [to_partner(piece, m) for piece, m in zip(outs, early)]
        stages.append(pieces)
    piece = (rows, part, width)
    shapes = [(kept, *piece)] * len(late) + [(kept, CORES, *piece)] * spares
    outs = small_call(
        functools.partial(late_kernel, kept, late),
        [jax.ShapeDtypeStruct(shape, jnp.float32) for shape in shapes],
        [SMEM] + [VMEM] * kept,
        *(place, *stages),
    )
    parts += [to_partner(piece, m) for piece, m in zip(outs, late)]
    spare = outs[len(late) :]
    total, devices = held * orb_count, slabs * orb_count
    cell_total = rows * part * width * devices
    block_shape = jax.ShapeDtypeStruct((total, rows * part, width), jnp.float32)
    message_shape = jax.ShapeDtypeStruct((devices, 1, total * total), jnp.float32)

    def exchanged(message):
        return lax.all_to_all(message, ALL, 0, 0)

    block, message = small_call(
        functools.partial(first_kernel, early, late, kept),
        [block_shape, message_shape],
        [SMEM] + [VMEM] * len(parts),
        *(place, *parts),
    )
    if spares:
        across = [(i, i ^ CORES) for i in range(orb_count)]
        cores = [(i, i ^ 1) for i in range(orb_count)]
        given = [
            spare[0],
            lax.ppermute(spare[1], "side", swap),
            lax.ppermute(spare[2], "orb", across),
        ]
        forward = small_call(
            forward_kernel, jax.ShapeDtypeStruct((CORES, kept, rows, part, width), jnp.float32), [SMEM, VMEM], place, block
        )
        given.append(lax.ppermute(forward, "orb", across))
        block_near = lax.ppermute(block, "orb", cores)
        table_shape = jax.ShapeDtypeStruct((total, LANES), jnp.float32)
        near = [lax.ppermute(piece, "orb", cores) for piece in given[:-1]]
        given = given + near + [lax.ppermute(given[-1], "orb", cores)]
        copies = exchanged(message)
        table, message = pl.pallas_call(
            functools.partial(table_kernel, cell_total),
            out_shape=[table_shape, message_shape],
            in_specs=[VMEM] * 2,
            out_specs=[VMEM] * 2,
            input_output_aliases={0: 1},
            compiler_params=pltpu.CompilerParams(vmem_limit_bytes=24 * 1024 * 1024),
        )(copies, block)
        return pl.pallas_call(
            functools.partial(last_kernel, cell_total),
            out_shape=jax.ShapeDtypeStruct((held, rows, cols, width), jnp.float32),
            in_specs=[SMEM] + [VMEM] * 4 + [HBM] * len(given),
            out_specs=HBM,
            scratch_shapes=[
                pltpu.VMEM((total, held, EIGHT, width), jnp.float32),
                pltpu.VMEM((held, rows, cols, width), jnp.float32),
                *(pltpu.VMEM(piece.shape, jnp.float32) for piece in given),
                pltpu.SemaphoreType.DMA((len(given),)),
                pltpu.SemaphoreType.DMA((2,)),
            ],
            compiler_params=pltpu.CompilerParams(vmem_limit_bytes=24 * 1024 * 1024),
        )(place, exchanged(message), table, block, block_near, *given)
    basis, message = small_call(
        functools.partial(second_kernel, cell_total), [block_shape, message_shape], [VMEM] * 2, exchanged(message), block
    )
    basis = small_call(functools.partial(third_kernel, cell_total), block_shape, [VMEM] * 2, exchanged(message), basis)
    basis = basis.reshape(total, rows, part, width)
    return lax.all_to_all(basis, "orb", split_axis=0, concat_axis=2, tiled=True)


def solution(mesh):
    slabs, orb_count = mesh.shape["dom"], mesh.shape["orb"]
    fine = Mesh(mesh.devices.reshape(slabs // 2, 2, orb_count), ALL)
    spec = P("orb", ("pair", "side"), None, None)
    return jax.shard_map(
        whole,
        mesh=fine,
        in_specs=(spec, P(("pair", "side"), None, None)),
        out_specs=spec,
        check_vma=False,
    )
```

```python
import functools

import jax
import jax.numpy as jnp
from jax import lax
from jax.experimental import pallas as pl
from jax.experimental.pallas import tpu as pltpu
from jax.sharding import Mesh
from jax.sharding import PartitionSpec as P

coefficients = (-49.0 / 18.0, 1.5, -0.15, 1.0 / 90.0)
spacing = 0.5
filter_centre = 23.0
filter_half = 23.0

REACH = 3
STEPS = 3
DEEP = REACH * STEPS
WIDE = REACH * (STEPS - 1)
EIGHT = 8
CORES = 2
WIDTH = 4
BLOCKS = 3
ALL = ("pair", "side", "orb")

VMEM = pl.BlockSpec(memory_space=pltpu.VMEM)
SMEM = pl.BlockSpec(memory_space=pltpu.SMEM)
HBM = pl.BlockSpec(memory_space=pltpu.HBM)

kinetic = -0.5 / (spacing * spacing)
taps = tuple(kinetic * c / filter_half for c in coefficients)
denominator = 180.0
whole_taps = tuple(round(denominator * c) for c in coefficients)
lane_scale = kinetic / filter_half / denominator
shift = (kinetic * 2.0 * coefficients[0] - filter_centre) / filter_half


def pack_kernel(place, orbitals, potential, *rest):
    outs, sems = rest[:-1], rest[-1]
    side, orb = place[0], place[2]
    kept, rows = orbitals.shape[0] // 2, orbitals.shape[1]
    part = outs[0].shape[1]
    columns = pl.ds(pl.multiple_of(orb * part, part), part)
    edge, shallow = pl.ds(side * (rows - DEEP), DEEP), pl.ds(side * (rows - WIDE), WIDE)
    sources = [potential.at[:, columns], potential.at[shallow, columns]]
    for at in range(kept):
        given, stays = orbitals.at[(1 - side) * kept + at], orbitals.at[side * kept + at]
        sources += [given.at[edge], given, stays.at[edge]]
    copies = [pltpu.make_async_copy(a, b, sems.at[i]) for i, (a, b) in enumerate(zip(sources, outs))]
    for copy in copies:
        copy.start()
    for copy in copies:
        copy.wait()


def packed(place, orbitals, potential, orb_count):
    held, rows, cols, width = orbitals.shape
    part = cols // orb_count
    shapes = [(rows, part, width), (WIDE, part, width)]
    shapes += [(DEEP, cols, width), (rows, cols, width), (DEEP, cols, width)] * (held // 2)
    return pl.pallas_call(
        pack_kernel,
        out_shape=[jax.ShapeDtypeStruct(shape, jnp.float32) for shape in shapes],
        in_specs=[SMEM, HBM, HBM],
        out_specs=[VMEM] * len(shapes),
        scratch_shapes=[pltpu.SemaphoreType.DMA((len(shapes),))],
        compiler_params=pltpu.CompilerParams(vmem_limit_bytes=16 * 1024 * 1024),
    )(place, *(pltpu.with_memory_space_constraint(array, pltpu.HBM) for array in (orbitals, potential)))


def join_kernel(swapped, slanted, straight, out):
    rows = swapped.shape[0]
    out[pl.ds(0, rows)] = swapped[...]
    out[pl.ds(rows, WIDE)] = slanted[...]
    out[pl.ds(rows + WIDE, WIDE)] = straight[...]


def split_dot(values, table):
    high = values.astype(jnp.bfloat16)
    rest = values - high.astype(jnp.float32)
    middle = rest.astype(jnp.bfloat16)
    low = (rest - middle.astype(jnp.float32)).astype(jnp.bfloat16)
    wide = jnp.concatenate([high, middle], axis=1)
    twice = jnp.concatenate([table, table], axis=0)
    return jnp.dot(wide, twice, preferred_element_type=jnp.float32) + jnp.dot(
        low, table, preferred_element_type=jnp.float32
    )


def filter_kernel(at, shares, early, place, own, swapped, slanted, straight, own_pot, lane_table, *rest):
    pot_far, outs = rest[:shares], rest[shares:-4]
    field, first, second, weight = rest[-4:]
    outs, sorted_pieces = outs[:-1], outs[-1]
    side, me, orb = place[0], place[1], place[2]
    rows, cols, _ = swapped.shape
    both = 2 * rows
    strips = cols // EIGHT

    def keep(ref, row, strip, value):
        ref[row, pl.ds(EIGHT * (strip + 1), EIGHT), :] = value
        if strip == 0:
            ref[row, pl.ds(cols + EIGHT, EIGHT), :] = value
        if strip == strips - 1:
            ref[row, pl.ds(0, EIGHT), :] = value

    def gather(load, count, row_to):
        def body(row, carry):
            for strip in range(strips):
                keep(field, row_to + row, strip, load(row, pl.ds(EIGHT * strip, EIGHT)))
            return carry

        lax.fori_loop(0, count, body, 0, unroll=3)

    kept = own.shape[0] // 2
    gather(lambda row, span: own[side * kept + at, row, span, :], rows, DEEP + side * rows)
    gather(lambda row, span: swapped[row, span, :], rows, DEEP + (1 - side) * rows)
    gather(lambda row, span: slanted[row, span, :], DEEP, side * (both + DEEP))
    gather(lambda row, span: straight[row, span, :], DEEP, (1 - side) * (both + DEEP))

    def weigh(values):
        return values * (1.0 / filter_half) + shift

    weight[pl.ds(WIDE + side * rows, rows)] = weigh(own_pot[...])
    part = cols // shares
    for apart, far in enumerate(pot_far):
        columns = pl.ds(pl.multiple_of((orb ^ apart) * part, part), part)
        weight[pl.ds(WIDE + (1 - side) * rows, rows), columns] = weigh(far[pl.ds(0, rows)])
        weight[pl.ds(side * (both + WIDE), WIDE), columns] = weigh(far[pl.ds(rows, WIDE)])
        weight[pl.ds((1 - side) * (both + WIDE), WIDE), columns] = weigh(far[pl.ds(rows + WIDE, WIDE)])

    def step(source, before, before_at, weight_at, total, store):
        width = source.shape[2]
        count = total // BLOCKS

        def body(index, carry):
            base = index * count
            centres = source[pl.ds(base + REACH, count), pl.ds(EIGHT, cols), :]
            along = split_dot(centres.reshape(count * cols, width), lane_table[...])
            for strip in range(strips):
                start = EIGHT * (strip + 1)
                window = [source[base + i, pl.ds(start, EIGHT), :] for i in range(count + 2 * REACH)]
                for i in range(count):
                    row = base + i
                    value = window[i + REACH] * weight[weight_at + row, pl.ds(EIGHT * strip, EIGHT), :]
                    from_lanes = i * cols + EIGHT * strip
                    value = value + along[from_lanes : from_lanes + EIGHT] * lane_scale
                    for k in range(1, REACH + 1):
                        near = window[i + REACH - k] + window[i + REACH + k]
                        near = near + (
                            source[row + REACH, pl.ds(start - k, EIGHT), :]
                            + source[row + REACH, pl.ds(start + k, EIGHT), :]
                        )
                        value = value + taps[k] * near
                    if before is not None:
                        value = 2.0 * value - before[before_at + row, pl.ds(start, EIGHT), :]
                    store(row, strip, value)
            return carry

        lax.fori_loop(0, BLOCKS, body, 0)

    step(field, None, 0, 0, both + 2 * WIDE, functools.partial(keep, first))
    step(first, field, 2 * REACH, REACH, both + 2 * REACH, functools.partial(keep, second))
    piece = sorted_pieces.shape[2]

    def store_out(row, strip, value):
        to = (EIGHT * strip) // piece
        half = row // rows
        sorted_pieces[2 * to + half, row - half * rows, pl.ds(EIGHT * strip - to * piece, EIGHT), :] = value

    step(second, first, 2 * REACH, 2 * REACH, both, store_out)
    for apart, out in zip(early, outs):
        out[...] = sorted_pieces[me ^ apart]


def late_kernel(stages, late, place, *refs):
    given, outs = refs[:stages], refs[stages:]
    side, me, orb = place[0], place[1], place[2]
    for stage, pieces in enumerate(given):
        for apart, out in zip(late, outs):
            out[stage] = pieces[me ^ apart]
        for index, out in enumerate(outs[len(late) :]):
            chip = orb // CORES ^ (1 if index < 2 else 0)
            for core in range(CORES):
                out[stage, core] = pieces[2 * (CORES * chip + core) + (side ^ (index % 2))]


def filtered_pieces(at, place, own, fetched, own_pot, pot_far, group, early):
    slanted, swapped, straight = fetched
    rows, cols, width = own.shape[1:]
    both = 2 * rows
    apart = jnp.arange(width)[:, None] - jnp.arange(width)[None, :]
    lane_table = jnp.zeros((width, width), jnp.float32)
    for k, tap in enumerate(whole_taps):
        hit = (apart % width == k) | (-apart % width == k)
        lane_table = jnp.where(hit, float(tap), lane_table)

    def scratch(margin):
        return pltpu.VMEM((both + 2 * margin, cols + 2 * EIGHT, width), jnp.float32)

    piece = (rows, 2 * cols // group, width)
    shapes = [piece] * len(early) + [(group, *piece)]
    return pl.pallas_call(
        functools.partial(filter_kernel, at, len(pot_far), early),
        out_shape=[jax.ShapeDtypeStruct(shape, jnp.float32) for shape in shapes],
        in_specs=[SMEM] + [VMEM] * (6 + len(pot_far)),
        out_specs=[VMEM] * len(shapes),
        scratch_shapes=[
            scratch(DEEP),
            scratch(WIDE),
            scratch(REACH),
            pltpu.VMEM((both + 2 * WIDE, cols, width), jnp.float32),
        ],
        compiler_params=pltpu.CompilerParams(vmem_limit_bytes=24 * 1024 * 1024),
    )(place, own, swapped, slanted, straight, own_pot, lane_table.astype(jnp.bfloat16), *pot_far)


LANES = 128


def exact_dot(a, b, contract=((1,), (0,))):
    return lax.dot_general(
        a, b, (contract, ((), ())), precision=lax.Precision.HIGHEST, preferred_element_type=jnp.float32
    )


def table_of(shape, test):
    rows = lax.broadcasted_iota(jnp.int32, shape, 0)
    columns = lax.broadcasted_iota(jnp.int32, shape, 1)
    return jnp.where(test(rows, columns), 1.0, 0.0).astype(jnp.float32)


def split(values):
    high = values.astype(jnp.bfloat16)
    rest = values - high.astype(jnp.float32)
    middle = rest.astype(jnp.bfloat16)
    return high, middle, (rest - middle.astype(jnp.float32)).astype(jnp.bfloat16)


def product(a, b, contract=((1,), (0,))):
    return lax.dot_general(a, b, (contract, ((), ())), preferred_element_type=jnp.float32)


def picked(values, table):
    chosen = table.astype(jnp.bfloat16)
    return sum(product(part, chosen) for part in split(values))


def gathered(table, values):
    chosen = table.astype(jnp.bfloat16)
    return sum(product(chosen, part) for part in split(values))


def gram_message(wide, total):
    tall = total * EIGHT
    high, middle, low = split(wide)
    joined, doubled = jnp.concatenate([high, middle], axis=1), jnp.concatenate([high, high], axis=1)
    mixed = product(doubled, jnp.concatenate([middle, low], axis=1), ((1,), (1,)))
    sums = product(joined, joined, ((1,), (1,))) + (mixed + mixed.T)
    sums = sums * table_of((tall, tall), lambda r, c: r % EIGHT == c % EIGHT)
    partial = gathered(table_of((total, tall), lambda r, c: c // EIGHT == r), sums)
    spread = picked(partial, table_of((tall, LANES), lambda r, c: r // EIGHT == c % total))
    per = LANES // total
    spread = spread * table_of((total, LANES), lambda r, c: c // total == r % per)
    return jnp.concatenate(
        [jnp.sum(spread[i * per : (i + 1) * per], axis=0, keepdims=True) for i in range(total // per)], axis=1
    )


def inverse_factor(copies, total, cell_total):
    row = jnp.sum(copies[...], axis=0) * (1.0 / cell_total)
    per = LANES // total
    wide = jnp.concatenate(
        [jnp.broadcast_to(row[:, i * LANES : (i + 1) * LANES], (per, LANES)) for i in range(total // per)], axis=0
    )
    wide = wide * table_of((total, LANES), lambda r, c: c // total == r % per)
    table = picked(wide, table_of((LANES, LANES), lambda r, c: r % total == c))
    table = table + table_of((total, LANES), lambda r, c: c - total == r)
    index = lax.broadcasted_iota(jnp.int32, (total, LANES), 0)
    for start in range(0, total, WIDTH):
        block = range(start, min(start + WIDTH, total))
        columns = {j: jnp.broadcast_to(table[:, j : j + 1], (total, LANES)) for j in block}
        rows = {j: table[j : j + 1, :] for j in block}
        reduced = table
        for j in block:
            value = columns[j][j : j + 1, :]
            scale = lax.rsqrt(value)
            scale = scale * (1.5 - 0.5 * value * scale * scale)
            factor, rows[j] = columns[j] * scale, rows[j] * scale
            for later in block:
                if later > j:
                    share = factor[later : later + 1, :]
                    columns[later] = columns[later] - factor * share
                    rows[later] = rows[later] - share * rows[j]
            reduced = reduced - factor * rows[j]
        for j in block:
            table = jnp.where(index == j, rows[j], table)
        table = jnp.where(index > block[-1], reduced, table)
    return table


def by_tiles(table, total):
    tall = total * EIGHT
    wide = picked(table, table_of((LANES, tall), lambda r, c: r - total == c // EIGHT))
    both = gathered(table_of((tall, total), lambda r, c: r // EIGHT == c), wide)
    return both * table_of((tall, tall), lambda r, c: r % EIGHT == c % EIGHT)


def side_by_side(ref):
    total, length, width = ref.shape
    tiles = [ref[:, start : start + EIGHT, :].reshape(total * EIGHT, width) for start in range(0, length, EIGHT)]
    return jnp.concatenate(tiles, axis=1)


def forward_kernel(place, block, out):
    kept, held = out.shape[1], 2 * out.shape[1]
    for flip in range(CORES):
        for at in range(kept):
            out[flip, at] = block[(place[2] ^ flip) * held + (place[0] ^ 1) * kept + at].reshape(out.shape[2:])


def first_kernel(early, late, kept, place, *refs):
    given, (block, message) = refs[:-2], refs[-2:]
    me, shape = place[1], block.shape[1:]
    for at in range(kept):
        for index, apart in enumerate(early):
            block[(me ^ apart) * kept + at] = given[at * len(early) + index][...].reshape(shape)
        for index, apart in enumerate(late):
            block[(me ^ apart) * kept + at] = given[kept * len(early) + index][at].reshape(shape)
    message[...] = jnp.broadcast_to(gram_message(side_by_side(block), block.shape[0])[None], message.shape)


def applied(table, block):
    total = block.shape[0]
    tall = total * EIGHT
    high, middle, low = split(by_tiles(table, total))
    values_high, values_middle, values_low = split(side_by_side(block))
    left = jnp.concatenate(
        [jnp.concatenate([high, high], axis=1), jnp.concatenate([middle, middle], axis=1)], axis=0
    )
    main = product(left, jnp.concatenate([values_high, values_middle], axis=0))
    rest = product(jnp.concatenate([low, high], axis=1), jnp.concatenate([values_high, values_low], axis=0))
    return main[:tall] + (main[tall:] + rest)


def put(wide, basis):
    total, length, width = basis.shape
    for t in range(length // EIGHT):
        piece = wide[:, t * width : (t + 1) * width].reshape(total, EIGHT, width)
        basis[:, EIGHT * t : EIGHT * (t + 1), :] = piece


def second_kernel(cell_total, copies, block, basis, message):
    total = block.shape[0]
    wide = applied(inverse_factor(copies, total, cell_total), block)
    put(wide, basis)
    message[...] = jnp.broadcast_to(gram_message(wide, total)[None], message.shape)


def third_kernel(cell_total, copies, block, basis):
    put(applied(inverse_factor(copies, block.shape[0], cell_total), block), basis)


def table_kernel(cell_total, copies, block, table_out, message):
    total = block.shape[0]
    table = inverse_factor(copies, total, cell_total)
    table_out[...] = table
    message[...] = jnp.broadcast_to(gram_message(applied(table, block), total)[None], message.shape)


def last_kernel(cell_total, place, copies, table, block, block_near, *refs):
    count = (len(refs) - 5) // 2
    far, (out_far, splats, out), spares = refs[:count], refs[count : count + 3], refs[count + 3 : 2 * count + 3]
    sems, sems_out = refs[2 * count + 3 :]
    total, length, width = block.shape
    held, rows = out.shape[:2]
    part = length // rows
    side, orb = place[0], place[2]
    chip = orb // CORES
    fetches = [pltpu.make_async_copy(a, b, sems.at[i]) for i, (a, b) in enumerate(zip(far, spares))]
    for fetch in fetches:
        fetch.start()
    second = inverse_factor(copies, total, cell_total)
    pick = table_of((LANES, total), lambda r, c: r - total == c)
    both = exact_dot(picked(second, pick), picked(table[...], pick))
    own = gathered(table_of((held * EIGHT, total), lambda r, c: orb * held + r // EIGHT == c), both)
    wide = picked(own, table_of((total, total * width), lambda r, c: c // width == r))
    for orbital in range(total):
        splats[orbital] = wide[:, orbital * width : (orbital + 1) * width].reshape(held, EIGHT, width)

    def write(sources, first_column):
        def body(row, carry):
            for strip in range(part // EIGHT):
                sums = None
                for orbital, load in sources:
                    values = load(row, strip)
                    terms = [splats[orbital, i] * values for i in range(held)]
                    sums = terms if sums is None else [a + b for a, b in zip(sums, terms)]
                column = pl.multiple_of(first_column + strip * EIGHT, EIGHT)
                for i in range(held):
                    out[i, row, pl.ds(column, EIGHT), :] = sums[i]
            return carry

        lax.fori_loop(0, rows, body, 0, unroll=4)

    def at(ref, index):
        def load(row, strip):
            return ref[index, pl.ds(pl.multiple_of(row * part + strip * EIGHT, EIGHT), EIGHT), :]

        return load

    write([(j, at(block, j)) for j in range(total)], orb * part)
    write([(j, at(block_near, j)) for j in range(total)], (orb ^ 1) * part)

    def leave(which, index):
        columns = pl.ds(pl.multiple_of(which * CORES * part, EIGHT), CORES * part)
        return pltpu.make_async_copy(out.at[:, :, columns], out_far.at[:, :, columns], sems_out.at[index])

    leave(chip, 0).start()
    for fetch in fetches:
        fetch.wait()

    def piece_at(ref, first, second):
        return lambda row, strip: ref[first, second, row, pl.ds(strip * EIGHT, EIGHT), :]

    kinds, kept = count // 2, held // 2
    core = orb % CORES
    for turn in range(CORES):
        share = core ^ turn
        sources = []
        for flip in range(2):
            for kind in range(kinds - 1):
                quad = (orb ^ CORES if kind // 2 else orb) ^ flip
                for stage in range(kept):
                    orbital = quad * held + (side ^ (kind % 2)) * kept + stage
                    sources.append((orbital, piece_at(spares[flip * kinds + kind], stage, share)))
            quad = orb ^ CORES ^ turn ^ flip
            for stage in range(kept):
                orbital = quad * held + (side ^ 1) * kept + stage
                sources.append((orbital, piece_at(spares[turn * kinds + kinds - 1], flip, stage)))
        write(sources, ((1 - chip) * CORES + share) * part)
    leave(1 - chip, 1).start()
    leave(chip, 0).wait()
    leave(1 - chip, 1).wait()


def small_call(kernel, out_shape, specs, *args):
    return pl.pallas_call(
        kernel,
        out_shape=out_shape,
        in_specs=specs,
        out_specs=jax.tree.map(lambda _: VMEM, out_shape),
        compiler_params=pltpu.CompilerParams(vmem_limit_bytes=24 * 1024 * 1024),
    )(*args)


def whole(orbitals, potential):
    pair_count, orb_count = lax.axis_size("pair"), lax.axis_size("orb")
    slabs = 2 * pair_count
    side, orb = lax.axis_index("side"), lax.axis_index("orb")
    held, rows, cols, width = orbitals.shape
    kept = held // 2
    part = cols // orb_count

    slant = [(i, (i + (1 if i % 2 else -1)) % slabs) for i in range(slabs)]
    ahead = [(i, (i + (2 if i % 2 else -2)) % slabs) for i in range(slabs)]
    swap = [(0, 1), (1, 0)]
    slab_axes = ("pair", "side")

    group = 2 * orb_count
    me = 2 * orb + side

    def flat_of(index):
        return (index % 2) * orb_count + index // 2

    place = jnp.stack([side, me, orb]).astype(jnp.int32)
    mine, edge, *sent = packed(place, orbitals, potential, orb_count)

    pieces = [
        lax.ppermute(mine, "side", swap),
        lax.ppermute(edge, slab_axes, slant),
        lax.ppermute(edge, slab_axes, ahead),
    ]
    joined = pl.pallas_call(
        join_kernel,
        out_shape=jax.ShapeDtypeStruct((rows + 2 * WIDE, part, width), jnp.float32),
        in_specs=[VMEM] * 3,
        out_specs=VMEM,
        compiler_params=pltpu.CompilerParams(vmem_limit_bytes=16 * 1024 * 1024),
    )(*pieces)
    pot_far = [joined] + [
        lax.ppermute(joined, "orb", [(i, i ^ m) for i in range(orb_count)]) for m in range(1, orb_count)
    ]

    fetched = []
    for at in range(kept):
        swapped = lax.ppermute(sent[3 * at + 1], "side", swap)
        slanted = lax.ppermute(sent[3 * at], slab_axes, slant)
        straight = lax.ppermute(sent[3 * at + 2], slab_axes, ahead)
        fetched.append((slanted, swapped, straight))

    early = tuple(sorted((m for m in range(1, group) if m != CORES), key=lambda m: (m < 2 * CORES, -(m % 2), m)))
    late = (0, CORES)
    spares = 3 if orb_count == 2 * CORES and kept == 2 else 0

    def to_partner(piece, m):
        if m == 0:
            return piece
        return lax.ppermute(piece, ("side", "orb"), [(flat_of(i), flat_of(i ^ m)) for i in range(group)])

    parts, stages = [], []
    for at in range(kept):
        *outs, pieces = filtered_pieces(at, place, orbitals, fetched[at], potential, pot_far, group, early)
        parts += [to_partner(piece, m) for piece, m in zip(outs, early)]
        stages.append(pieces)
    piece = (rows, part, width)
    shapes = [(kept, *piece)] * len(late) + [(kept, CORES, *piece)] * spares
    outs = small_call(
        functools.partial(late_kernel, kept, late),
        [jax.ShapeDtypeStruct(shape, jnp.float32) for shape in shapes],
        [SMEM] + [VMEM] * kept,
        *(place, *stages),
    )
    parts += [to_partner(piece, m) for piece, m in zip(outs, late)]
    spare = outs[len(late) :]
    total, devices = held * orb_count, slabs * orb_count
    cell_total = rows * part * width * devices
    block_shape = jax.ShapeDtypeStruct((total, rows * part, width), jnp.float32)
    message_shape = jax.ShapeDtypeStruct((devices, 1, total * total), jnp.float32)

    def exchanged(message):
        return lax.all_to_all(message, ALL, 0, 0)

    block, message = small_call(
        functools.partial(first_kernel, early, late, kept),
        [block_shape, message_shape],
        [SMEM] + [VMEM] * len(parts),
        *(place, *parts),
    )
    if spares:
        across = [(i, i ^ CORES) for i in range(orb_count)]
        cores = [(i, i ^ 1) for i in range(orb_count)]
        given = [
            spare[0],
            lax.ppermute(spare[1], "side", swap),
            lax.ppermute(spare[2], "orb", across),
        ]
        forward = small_call(
            forward_kernel, jax.ShapeDtypeStruct((CORES, kept, rows, part, width), jnp.float32), [SMEM, VMEM], place, block
        )
        given.append(lax.ppermute(forward, "orb", across))
        block_near = lax.ppermute(block, "orb", cores)
        table_shape = jax.ShapeDtypeStruct((total, LANES), jnp.float32)
        near = [lax.ppermute(piece, "orb", cores) for piece in given[:-1]]
        given = given + near + [lax.ppermute(given[-1], "orb", cores)]
        copies = exchanged(message)
        table, message = pl.pallas_call(
            functools.partial(table_kernel, cell_total),
            out_shape=[table_shape, message_shape],
            in_specs=[VMEM] * 2,
            out_specs=[VMEM] * 2,
            input_output_aliases={0: 1},
            compiler_params=pltpu.CompilerParams(vmem_limit_bytes=24 * 1024 * 1024),
        )(copies, block)
        return pl.pallas_call(
            functools.partial(last_kernel, cell_total),
            out_shape=jax.ShapeDtypeStruct((held, rows, cols, width), jnp.float32),
            in_specs=[SMEM] + [VMEM] * 4 + [HBM] * len(given),
            out_specs=HBM,
            scratch_shapes=[
                pltpu.VMEM((total, held, EIGHT, width), jnp.float32),
                pltpu.VMEM((held, rows, cols, width), jnp.float32),
                *(pltpu.VMEM(piece.shape, jnp.float32) for piece in given),
                pltpu.SemaphoreType.DMA((len(given),)),
                pltpu.SemaphoreType.DMA((2,)),
            ],
            compiler_params=pltpu.CompilerParams(vmem_limit_bytes=24 * 1024 * 1024),
        )(place, exchanged(message), table, block, block_near, *given)
    basis, message = small_call(
        functools.partial(second_kernel, cell_total), [block_shape, message_shape], [VMEM] * 2, exchanged(message), block
    )
    basis = small_call(functools.partial(third_kernel, cell_total), block_shape, [VMEM] * 2, exchanged(message), basis)
    basis = basis.reshape(total, rows, part, width)
    return lax.all_to_all(basis, "orb", split_axis=0, concat_axis=2, tiled=True)


def solution(mesh):
    slabs, orb_count = mesh.shape["dom"], mesh.shape["orb"]
    fine = Mesh(mesh.devices.reshape(slabs // 2, 2, orb_count), ALL)
    spec = P("orb", ("pair", "side"), None, None)
    return jax.shard_map(
        whole,
        mesh=fine,
        in_specs=(spec, P(("pair", "side"), None, None)),
        out_specs=spec,
        check_vma=False,
    )
```
